32 devices in a mesh: seq: 16 (over z, y, x), chan: 2 (over core).
Axes of the slice: x: 2, y: 2, z: 4, core: 2. Of those that a mesh axis runs over, the one named last changes fastest.
Arguments:
- streams: bfloat16 [3, 4096, 8192], P(None, 'seq', 'chan'), may hold values from -6 to 6
- grad_out: bfloat16 [4096, 8192], P('seq', 'chan'), may hold values from -9 to 9
- long_filter: float32 [8192, 8192], P('seq', 'chan'), may hold values from -0.0625 to 0.0625
- short_filter: float32 [3, 7, 8192], P(None, None, 'chan'), may hold values from -3 to 3
- skip_gain: float32 [8192], P('chan'), may hold values from -4 to 4
Outputs:
- output: bfloat16 [4096, 8192], P('seq', 'chan')
- grad_streams: bfloat16 [3, 4096, 8192], P(None, 'seq', 'chan')
- filter_grad: float32 [8192, 8192], P('seq', 'chan')
- short_grad: float32 [3, 7, 8192], P(None, None, 'chan')
- bias_grad: float32 [8192], P('chan')
The draws below stay inside these ranges and needn't reach their ends.
All inputs are finite; a program needn't handle non-finite values.
Results may differ from the reference program's by a relative error of at most 0.0075.
Values may be sent and summed in bfloat16 or wider, within the bound.
No kernel may reach another device: no remote copies, remote signals or barrier semaphores. Data moves between devices by JAX's collectives and lax.ppermute only.
A program may use at most 320 MiB of HBM per device.

```python
import math
import jax
import jax.numpy as jnp
from jax import lax

D = 8192
LF = 8192
TAPS = 7
SEQ = 4096


def draw_grad_out(key, part):
    ramp = 3.0 ** (jnp.arange(D, dtype=jnp.float32) / D)
    base = jnp.clip(jax.random.normal(key, (SEQ, D), jnp.float32), -5.0, 5.0)
    return (base * ramp[None, :] * 0.6).astype(jnp.bfloat16)


def shard_levels(own_key, extent, shards, least, high):
    def one(axis_at, parts):
        steps = jax.random.uniform(jax.random.fold_in(jax.random.fold_in(own_key, 6), axis_at), (parts,), jnp.float32, least / len(shards), high / len(shards))
        return jnp.repeat(jnp.exp(steps), extent[axis_at] // parts).reshape((-1,) + (1,) * (len(extent) - axis_at - 1))

    level = one(*shards[0])
    for cut in shards[1:]:
        level = level * one(*cut)
    return level


def scatter_about(stream_key, dims, scale, most, shards=(), kind=jnp.bfloat16):
    values = scale * jax.random.normal(stream_key, dims, jnp.float32)
    if shards:
        values = values * shard_levels(stream_key, dims, shards, -0.22, 0.18)
    return jnp.clip(values, -most, most).astype(kind)


def setup_inputs(seed: int = 0) -> dict:
    keys = jax.random.split(jax.random.key(seed), 6)
    streams = scatter_about(keys[0], (3, SEQ, D), 1.0, 6.0, ((1, 16), (2, 2)))
    grad_out = draw_grad_out(jax.random.fold_in(keys[5], 71), 0)
    long_filter = scatter_about(keys[2], (LF, D), LF ** -0.5, 0.0625, ((0, 16), (1, 2)), jnp.float32)
    short_filter = scatter_about(keys[3], (3, TAPS, D), 0.5, 3.0, ((2, 2),), jnp.float32)
    skip_gain = scatter_about(keys[4], (D,), 1.0, 4.0, ((0, 2),), jnp.float32)
    return dict(streams=streams, grad_out=grad_out, long_filter=long_filter, short_filter=short_filter, skip_gain=skip_gain)


def short_conv(signal, taps_w):
    length = signal.shape[1]
    result = taps_w[:, 0, None, :] * signal
    for offset in range(1, TAPS):
        moved = jnp.pad(signal, ((0, 0), (offset, 0), (0, 0)))[:, :length, :]
        result = result + taps_w[:, offset, None, :] * moved
    return result

def short_conv_back(signal, taps_w):
    result = taps_w[:, 0, None, :] * signal
    for offset in range(1, TAPS):
        moved = jnp.pad(signal, ((0, 0), (0, offset), (0, 0)))[:, offset:, :]
        result = result + taps_w[:, offset, None, :] * moved
    return result

def block_work(pieces):
    streams, grad_out, long_filter, short_filter, skip_gain = pieces
    inputs = streams.astype(jnp.float32)
    filtered = short_conv(inputs, short_filter)
    gated = (filtered[0] * filtered[2]).astype(jnp.bfloat16)
    gout = grad_out.astype(jnp.float32)
    grad_mix = (gout * filtered[1]).astype(jnp.bfloat16)
    gated_f = gated.astype(jnp.float32)
    mix_f = grad_mix.astype(jnp.float32)
    point_count = 2 * SEQ
    live_taps = min(LF, SEQ)
    spec_gated = jnp.fft.rfft(gated_f, point_count, axis=0)
    spec_filter = jnp.fft.rfft(long_filter[:live_taps], point_count, axis=0)
    spec_mix = jnp.fft.rfft(mix_f, point_count, axis=0)
    long_out = jnp.fft.irfft(spec_gated * spec_filter, point_count, axis=0)[:SEQ]
    mixed = (long_out + skip_gain[None, :] * gated_f).astype(jnp.bfloat16)
    mixed_f = mixed.astype(jnp.float32)
    output = (filtered[1] * mixed_f).astype(jnp.bfloat16)
    back = jnp.fft.irfft(jnp.conj(spec_filter) * spec_mix, point_count, axis=0)[:SEQ]
    grad_gated = (back + skip_gain[None, :] * mix_f).astype(jnp.bfloat16)
    raw_filter = jnp.fft.irfft(jnp.conj(spec_gated) * spec_mix, point_count, axis=0)[:live_taps]
    raw_filter = jnp.pad(raw_filter, ((0, LF - live_taps), (0, 0)))
    raw_bias = lax.optimization_barrier(jnp.sum(mix_f * gated_f, axis=0))
    gg_f = grad_gated.astype(jnp.float32)
    grad_pre = jnp.stack([gg_f * filtered[2], gout * mixed_f, gg_f * filtered[0]])
    grad_streams = short_conv_back(grad_pre, short_filter).astype(jnp.bfloat16)
    short_terms = []
    for offset in range(TAPS):
        moved = jnp.pad(inputs, ((0, 0), (offset, 0), (0, 0)))[:, :SEQ, :]
        short_terms.append(lax.optimization_barrier(jnp.sum(grad_pre * moved, axis=1)))
    raw_short = jnp.stack(short_terms, axis=1)
    return (output, grad_streams, raw_filter, raw_short, raw_bias)

def reference(streams, grad_out, long_filter, short_filter, skip_gain):
    width = math.gcd(D, 512)
    nblocks = D // width
    pieces = (streams.reshape(3, SEQ, nblocks, width).transpose(2, 0, 1, 3), grad_out.reshape(SEQ, nblocks, width).transpose(1, 0, 2), long_filter.reshape(LF, nblocks, width).transpose(1, 0, 2), short_filter.reshape(3, TAPS, nblocks, width).transpose(2, 0, 1, 3), skip_gain.reshape(nblocks, width))
    output, grad_streams, raw_filter, raw_short, raw_bias = lax.map(block_work, pieces)
    output = output.transpose(1, 0, 2).reshape(SEQ, D)
    grad_streams = grad_streams.transpose(1, 2, 0, 3).reshape(3, SEQ, D)
    raw_filter = raw_filter.transpose(1, 0, 2).reshape(LF, D)
    raw_short = raw_short.transpose(1, 2, 0, 3).reshape(3, TAPS, D)
    raw_bias = raw_bias.reshape(D)
    sq_total = jnp.sum(raw_filter * raw_filter) + jnp.sum(raw_short * raw_short) + jnp.sum(raw_bias * raw_bias)
    param_count = LF * D + (3 * TAPS + 1) * D
    clip_factor = 1.0 / jnp.sqrt(sq_total / param_count + 1e-06)
    return (output, grad_streams, raw_filter * clip_factor, raw_short * clip_factor, raw_bias * clip_factor)
```

```python
import math

import jax
import jax.numpy as jnp
from jax import lax
from jax.experimental import pallas as pl
from jax.experimental.pallas import tpu as pltpu
from jax.sharding import PartitionSpec as P

D = 8192
LF = 8192
TAPS = 7
HALO = 8
LANES = 128
F32 = jnp.float32
BF16 = jnp.bfloat16


def add(a, b):
    if a is None:
        return b
    if b is None:
        return a
    return a + b


def neg(a):
    return None if a is None else -a


def sub(a, b):
    if b is None:
        return a
    if a is None:
        return -b
    return a - b


def scaled(a, c):
    if a is None or abs(c) < 1e-12:
        return None
    if abs(c - 1.0) < 1e-12:
        return a
    if abs(c + 1.0) < 1e-12:
        return -a
    return a * c


def cadd(a, b):
    return (add(a[0], b[0]), add(a[1], b[1]))


def csub(a, b):
    return (sub(a[0], b[0]), sub(a[1], b[1]))


def times_i(a, sign):
    return (neg(a[1]), a[0]) if sign > 0 else (a[1], neg(a[0]))


def cmul(a, angle, gain=1.0):
    c = math.cos(angle)
    s = math.sin(angle)
    re, im = a
    if abs(abs(c) - abs(s)) < 1e-12 and re is not None and im is not None:
        root = abs(c) * gain
        sc = 1.0 if c > 0 else -1.0
        ss = 1.0 if s > 0 else -1.0
        if sc * ss > 0:
            return ((re - im) * (root * sc), (re + im) * (root * sc))
        return ((re + im) * (root * sc), (im - re) * (root * sc))
    c = c * gain
    s = s * gain
    return (sub(scaled(re, c), scaled(im, s)), add(scaled(im, c), scaled(re, s)))


def complex_dft(xs, sign):
    n = len(xs)
    if n == 1:
        return list(xs)
    half = n // 2
    sums = [cadd(xs[i], xs[i + half]) for i in range(half)]
    difs = [csub(xs[i], xs[i + half]) for i in range(half)]
    if n == 2:
        return [sums[0], difs[0]]
    quarter = n // 4
    out = [None] * n
    out[0::2] = complex_dft(sums, sign)
    turn = sign * 2.0 * math.pi / n
    first = []
    third = []
    for i in range(quarter):
        rot = times_i(difs[i + quarter], sign)
        first.append(cmul(cadd(difs[i], rot), turn * i))
        third.append(cmul(csub(difs[i], rot), turn * 3 * i))
    out[1::4] = complex_dft(first, sign)
    out[3::4] = complex_dft(third, sign)
    return out


def real_dft(xs):
    n = len(xs)
    if n == 1:
        return [(xs[0], None)]
    half = n // 2
    sums = [add(xs[i], xs[i + half]) for i in range(half)]
    difs = [sub(xs[i], xs[i + half]) for i in range(half)]
    if n == 2:
        return [(sums[0], None), (difs[0], None)]
    quarter = n // 4
    out = [None] * (half + 1)
    out[0::2] = real_dft(sums)
    turn = -2.0 * math.pi / n
    odd = [cmul((difs[i], neg(difs[i + quarter])), turn * i) for i in range(quarter)]
    for j, value in enumerate(complex_dft(odd, -1)):
        k = 4 * j + 1
        if k <= half:
            out[k] = value
        else:
            out[n - k] = (value[0], neg(value[1]))
    return out


def real_idft(spec, keep):
    n = 2 * (len(spec) - 1)
    if n == 2:
        both = [add(spec[0][0], spec[1][0]), sub(spec[0][0], spec[1][0])]
        return both[:keep]
    half = n // 2
    quarter = n // 4
    even = real_idft(spec[0::2], half)
    odd = []
    for j in range(quarter):
        k = 4 * j + 1
        odd.append(spec[k] if k <= half else (spec[n - k][0], neg(spec[n - k][1])))
    turn = 2.0 * math.pi / n
    rest = [cmul(v, turn * i, 2.0) for i, v in enumerate(complex_dft(odd, 1))]
    wave = [rest[i][0] for i in range(quarter)] + [neg(rest[i][1]) for i in range(quarter)]
    out = [add(even[i], wave[i]) for i in range(half)]
    if keep > half:
        out = out + [sub(even[i], wave[i]) for i in range(half)]
    return out[:keep]


def turn_tables(shards, rows):
    radix = 2 * shards
    count = radix * rows
    k1 = jnp.arange(shards + 1, dtype=jnp.int32)[:, None]
    r = jnp.arange(rows, dtype=jnp.int32)
    fine = 2.0 * math.pi / count * (k1 * r[None, :] % count).astype(F32)
    coarse = 2.0 * math.pi / rows * (r[:, None] * r[None, :] % rows).astype(F32)
    fine_c = jnp.cos(fine)
    fine_s = jnp.sin(fine)
    coarse_c = jnp.cos(coarse)[None]
    coarse_s = jnp.sin(coarse)[None]

    def pair(fc, fs, gain):
        cos = fc * coarse_c - fs * coarse_s
        sin = fs * coarse_c + fc * coarse_s
        return (jnp.concatenate([cos, sin], axis=1) * gain).astype(BF16)

    fwd = pair(fine_c[:, None, :], fine_s[:, None, :], 1.0)
    inv = pair(fine_c[:, :, None], fine_s[:, :, None], 1.0 / count)
    return fwd, inv


def lane_step(chans):
    return 128 if chans % 128 == 0 else chans


def over_tiles(rows, chans, work):
    lanes = lane_step(chans)
    sub_rows = 16
    across = chans // lanes

    def step(i, carry):
        r = pl.multiple_of((i // across) * sub_rows, sub_rows)
        if across == 1:
            c = 0
        else:
            c = pl.multiple_of((i % across) * lanes, lanes)
        work(pl.ds(r, sub_rows), pl.ds(c, lanes))
        return carry

    lax.fori_loop(0, (rows // sub_rows) * across, step, 0)


def split_in(src, dst, at, shards, rows, chans):
    blocks = src.shape[0]

    def work(rs, cs):
        xs = [src[s, rs, cs].astype(F32) for s in range(blocks)]
        xs = xs + [None] * (2 * shards - blocks)
        for k, (re, im) in enumerate(real_dft(xs)):
            dst[k, at, rs, cs] = re.astype(BF16)
            if im is None:
                dst[k, at + 1, rs, cs] = jnp.zeros(re.shape, BF16)
            else:
                dst[k, at + 1, rs, cs] = im.astype(BF16)

    over_tiles(rows, chans, work)


def load_spec(src, at, shards, rs, cs):
    spec = []
    for k in range(shards + 1):
        edge = k == 0 or k == shards
        spec.append((src[k, at, rs, cs], None if edge else src[k, at + 1, rs, cs]))
    return spec


def dot(a, b):
    return jnp.dot(a, b, preferred_element_type=F32)


def forward(table, a_re, a_im, rows):
    p = dot(table, a_re)
    q = dot(table, a_im)
    return p[:rows] + q[rows:], q[:rows] - p[rows:]


def backward(table, z_re, z_im, rows):
    p = dot(table, z_re.astype(BF16))
    q = dot(table, z_im.astype(BF16))
    return p[:rows] - q[rows:], p[rows:] + q[:rows]


def whole(shape):
    zeros = (0,) * len(shape)
    return pl.BlockSpec(shape, lambda *_: zeros, pipeline_mode=pl.Buffered(1))


def per_step(shape):
    zeros = (0,) * (len(shape) - 1)
    return pl.BlockSpec(shape, lambda i: (i,) + zeros)


def value_path(gated, taps, skip, fwd, inv):
    shards, rows, chans = gated.shape
    live = min(taps.shape[0], shards)
    steps = shards + 1

    def kernel(g_ref, h_ref, skip_ref, fwd_ref, inv_ref, mixed_ref, gs_ref, hs_ref, a_ref, y_ref):
        k = pl.program_id(0)

        @pl.when(k == 0)
        def _():
            split_in(g_ref, a_ref, 0, shards, rows, chans)
            split_in(h_ref, a_ref, 2, shards, rows, chans)

        g_re, g_im = forward(fwd_ref[0], a_ref[k, 0], a_ref[k, 1], rows)
        h_re, h_im = forward(fwd_ref[0], a_ref[k, 2], a_ref[k, 3], rows)
        gs_ref[0, 0] = g_re
        gs_ref[0, 1] = g_im
        hs_ref[0, 0] = h_re
        hs_ref[0, 1] = h_im
        y_re, y_im = backward(inv_ref[0], g_re * h_re - g_im * h_im, g_re * h_im + g_im * h_re, rows)
        y_ref[k, 0] = y_re
        y_ref[k, 1] = y_im

        @pl.when(k == steps - 1)
        def _():
            def work(rs, cs):
                out = real_idft(load_spec(y_ref, 0, shards, rs, cs), shards)
                gain = skip_ref[:, cs]
                for s in range(shards):
                    mixed = out[s] + gain * g_ref[s, rs, cs].astype(F32)
                    mixed_ref[s, rs, cs] = mixed.astype(BF16)

            over_tiles(rows, chans, work)

    spec_shape = jax.ShapeDtypeStruct((steps, 2, rows, chans), F32)
    return pl.pallas_call(
        kernel,
        grid=(steps,),
        in_specs=[
            whole((shards, rows, chans)),
            whole((live, rows, chans)),
            whole((1, chans)),
            per_step((1, 2 * rows, rows)),
            per_step((1, 2 * rows, rows)),
        ],
        out_specs=[
            whole((shards, rows, chans)),
            per_step((1, 2, rows, chans)),
            per_step((1, 2, rows, chans)),
        ],
        out_shape=[jax.ShapeDtypeStruct((shards, rows, chans), BF16), spec_shape, spec_shape],
        scratch_shapes=[
            pltpu.VMEM((steps, 4, rows, chans), BF16),
            pltpu.VMEM((steps, 2, rows, chans), F32),
        ],
        cost_estimate=pl.CostEstimate(flops=30 * 10**9, transcendentals=0, bytes_accessed=40 * 10**6),
        name="value_path",
    )(gated, taps, skip, fwd, inv)


def grad_path(mix, spec_g, spec_h, skip, fwd, inv, filter_blocks):
    shards, rows, chans = mix.shape
    live = min(filter_blocks, shards)
    steps = shards + 1

    def kernel(m_ref, gs_ref, hs_ref, skip_ref, fwd_ref, inv_ref, gg_ref, raw_ref, sq_ref, a_ref, y_ref):
        k = pl.program_id(0)

        @pl.when(k == 0)
        def _():
            split_in(m_ref, a_ref, 0, shards, rows, chans)

        m_re, m_im = forward(fwd_ref[0], a_ref[k, 0], a_ref[k, 1], rows)
        for at, ref in ((0, hs_ref), (2, gs_ref)):
            c_re = ref[0, 0]
            c_im = ref[0, 1]
            y_re, y_im = backward(inv_ref[0], c_re * m_re + c_im * m_im, c_re * m_im - c_im * m_re, rows)
            y_ref[k, at] = y_re
            y_ref[k, at + 1] = y_im

        @pl.when(k == steps - 1)
        def _():
            sq_ref[...] = jnp.zeros(sq_ref.shape, F32)

            def back_work(rs, cs):
                out = real_idft(load_spec(y_ref, 0, shards, rs, cs), shards)
                gain = skip_ref[:, cs]
                for s in range(shards):
                    total = out[s] + gain * m_ref[s, rs, cs].astype(F32)
                    gg_ref[s, rs, cs] = total.astype(BF16)

            over_tiles(rows, chans, back_work)

            def raw_work(rs, cs):
                out = real_idft(load_spec(y_ref, 2, shards, rs, cs), shards)
                square = None
                for s in range(live):
                    raw_ref[s, rs, cs] = out[s].astype(BF16)
                    square = add(square, out[s] * out[s])
                for s in range(live, filter_blocks):
                    raw_ref[s, rs, cs] = jnp.zeros(out[0].shape, BF16)
                sq_ref[:, cs] += square[:8] + square[8:]

            over_tiles(rows, chans, raw_work)

    return pl.pallas_call(
        kernel,
        grid=(steps,),
        in_specs=[
            whole((shards, rows, chans)),
            per_step((1, 2, rows, chans)),
            per_step((1, 2, rows, chans)),
            whole((1, chans)),
            per_step((1, 2 * rows, rows)),
            per_step((1, 2 * rows, rows)),
        ],
        out_specs=[
            whole((shards, rows, chans)),
            whole((filter_blocks, rows, chans)),
            whole((8, chans)),
        ],
        out_shape=[
            jax.ShapeDtypeStruct((shards, rows, chans), BF16),
            jax.ShapeDtypeStruct((filter_blocks, rows, chans), BF16),
            jax.ShapeDtypeStruct((8, chans), F32),
        ],
        scratch_shapes=[
            pltpu.VMEM((steps, 2, rows, chans), BF16),
            pltpu.VMEM((steps, 4, rows, chans), F32),
        ],
        cost_estimate=pl.CostEstimate(flops=30 * 10**9, transcendentals=0, bytes_accessed=40 * 10**6),
        name="grad_path",
    )(mix, spec_g, spec_h, skip, fwd, inv)


def groups_of(chans):
    return 1 if chans % LANES == 0 else LANES // chans


def put(ref, rs, c, value):
    groups, _, chans = ref.shape
    if groups == 1:
        ref[0, rs, pl.ds(c, value.shape[1])] = value
        return
    for i in range(groups):
        ref[i, rs, :] = value[:, i * chans : (i + 1) * chans]


def take(ref, rs, c, lanes):
    groups = ref.shape[0]
    if groups == 1:
        return ref[0, rs, pl.ds(c, lanes)].astype(F32)
    return jnp.concatenate([ref[i, rs, :].astype(F32) for i in range(groups)], axis=1)


def pack_taps(long_filter, shards):
    rows, width = long_filter.shape
    chans = width // shards
    groups = groups_of(chans)

    def kernel(x_ref, o_ref):
        for c in range(0, chans * groups, LANES):
            put(o_ref, pl.ds(0, rows), c, x_ref[:, pl.ds(c, LANES)].astype(BF16))

    return pl.pallas_call(
        kernel,
        grid=(shards // groups,),
        in_specs=[pl.BlockSpec((rows, chans * groups), lambda i: (0, i))],
        out_specs=pl.BlockSpec((groups, rows, chans), lambda i: (i, 0, 0)),
        out_shape=jax.ShapeDtypeStruct((shards, rows, chans), BF16),
        name="pack_taps",
    )(long_filter)


def scale_taps(raw, clip):
    shards, rows, chans = raw.shape
    groups = groups_of(chans)

    def kernel(c_ref, x_ref, o_ref):
        for c in range(0, chans * groups, LANES):
            o_ref[:, pl.ds(c, LANES)] = take(x_ref, pl.ds(0, rows), c, LANES) * c_ref[0, 0]

    return pl.pallas_call(
        kernel,
        grid=(shards // groups,),
        in_specs=[
            pl.BlockSpec(memory_space=pltpu.SMEM),
            pl.BlockSpec((groups, rows, chans), lambda i: (i, 0, 0)),
        ],
        out_specs=pl.BlockSpec((rows, chans * groups), lambda i: (0, i)),
        out_shape=jax.ShapeDtypeStruct((rows, shards * chans), F32),
        name="scale_taps",
    )(clip, raw)


def short_rows(ext_ref, w_ref, i, cs, r, rows):
    total = w_ref[i, 0:1, cs] * ext_ref[i, pl.ds(HALO + r, rows), :]
    for j in range(1, TAPS):
        total = total + w_ref[i, j : j + 1, cs] * ext_ref[i, pl.ds(HALO + r - j, rows), :]
    return total


def gates(streams, before, grad_out, short_filter, shards):
    _, rows, width = streams.shape
    chans = width // shards
    groups = groups_of(chans)
    block = chans * groups
    chunk = math.gcd(rows, 64)

    def kernel(x_ref, b_ref, go_ref, w_ref, g_ref, m_ref, bias_ref, ext_ref):
        for c in range(0, block, LANES):
            cs = pl.ds(c, LANES)
            for i in range(3):
                ext_ref[i, pl.ds(0, HALO), :] = b_ref[i, :, cs].astype(F32)
                ext_ref[i, pl.ds(HALO, rows), :] = x_ref[i, :, cs].astype(F32)
            total = jnp.zeros((1, LANES), F32)
            for r in range(0, rows, chunk):
                rs = pl.ds(r, chunk)
                gated = short_rows(ext_ref, w_ref, 0, cs, r, chunk) * short_rows(ext_ref, w_ref, 2, cs, r, chunk)
                gated = gated.astype(BF16)
                mix = go_ref[rs, cs].astype(F32) * short_rows(ext_ref, w_ref, 1, cs, r, chunk)
                mix = mix.astype(BF16)
                put(g_ref, rs, c, gated)
                put(m_ref, rs, c, mix)
                total = total + jnp.sum(gated.astype(F32) * mix.astype(F32), axis=0, keepdims=True)
            bias_ref[:, cs] = total

    blocks = jax.ShapeDtypeStruct((shards, rows, chans), BF16)
    return pl.pallas_call(
        kernel,
        grid=(shards // groups,),
        in_specs=[
            pl.BlockSpec((3, rows, block), lambda i: (0, 0, i)),
            pl.BlockSpec((3, HALO, block), lambda i: (0, 0, i)),
            pl.BlockSpec((rows, block), lambda i: (0, i)),
            pl.BlockSpec((3, TAPS, block), lambda i: (0, 0, i)),
        ],
        out_specs=[
            pl.BlockSpec((groups, rows, chans), lambda i: (i, 0, 0)),
            pl.BlockSpec((groups, rows, chans), lambda i: (i, 0, 0)),
            pl.BlockSpec((1, block), lambda i: (0, i)),
        ],
        out_shape=[blocks, blocks, jax.ShapeDtypeStruct((1, width), F32)],
        scratch_shapes=[pltpu.VMEM((3, rows + HALO, LANES), F32)],
        cost_estimate=pl.CostEstimate(flops=60 * 10**6, transcendentals=0, bytes_accessed=14 * 10**6),
        name="gates",
    )(streams, before, grad_out, short_filter)


def finish(streams, before, grad_out, short_filter, mixed, gg, after, shards):
    _, rows, width = streams.shape
    chans = width // shards
    groups = groups_of(chans)
    block = chans * groups
    chunk = math.gcd(rows, 64)

    def kernel(x_ref, b_ref, go_ref, w_ref, mi_ref, gg_ref, n_ref, o_ref, gs_ref, st_ref, ext_ref, pre_ref):
        for c in range(0, block, LANES):
            cs = pl.ds(c, LANES)
            for i in range(3):
                ext_ref[i, pl.ds(0, HALO), :] = b_ref[i, :, cs].astype(F32)
                ext_ref[i, pl.ds(HALO, rows), :] = x_ref[i, :, cs].astype(F32)
                pre_ref[i, pl.ds(rows, HALO), :] = n_ref[i, :, cs]
            for r in range(0, rows, chunk):
                rs = pl.ds(r, chunk)
                mixed_rows = take(mi_ref, rs, c, LANES)
                back = take(gg_ref, rs, c, LANES)
                pre_ref[0, rs, :] = back * short_rows(ext_ref, w_ref, 2, cs, r, chunk)
                pre_ref[2, rs, :] = back * short_rows(ext_ref, w_ref, 0, cs, r, chunk)
                pre_ref[1, rs, :] = go_ref[rs, cs].astype(F32) * mixed_rows
                o_ref[rs, cs] = (short_rows(ext_ref, w_ref, 1, cs, r, chunk) * mixed_rows).astype(BF16)
            for i in range(3):
                sums = [jnp.zeros((8, LANES), F32) for _ in range(TAPS)]
                for r in range(0, rows, chunk):
                    rs = pl.ds(r, chunk)
                    own = pre_ref[i, rs, :]
                    total = w_ref[i, 0:1, cs] * own
                    for j in range(TAPS):
                        if j:
                            total = total + w_ref[i, j : j + 1, cs] * pre_ref[i, pl.ds(r + j, chunk), :]
                        term = own * ext_ref[i, pl.ds(HALO + r - j, chunk), :]
                        sums[j] = sums[j] + jnp.sum(term.reshape(chunk // 8, 8, LANES), axis=0)
                    gs_ref[i, rs, cs] = total.astype(BF16)
                for j in range(TAPS):
                    st_ref[i, j : j + 1, cs] = jnp.sum(sums[j], axis=0, keepdims=True)

    return pl.pallas_call(
        kernel,
        grid=(shards // groups,),
        in_specs=[
            pl.BlockSpec((3, rows, block), lambda i: (0, 0, i)),
            pl.BlockSpec((3, HALO, block), lambda i: (0, 0, i)),
            pl.BlockSpec((rows, block), lambda i: (0, i)),
            pl.BlockSpec((3, TAPS, block), lambda i: (0, 0, i)),
            pl.BlockSpec((groups, rows, chans), lambda i: (i, 0, 0)),
            pl.BlockSpec((groups, rows, chans), lambda i: (i, 0, 0)),
            pl.BlockSpec((3, HALO, block), lambda i: (0, 0, i)),
        ],
        out_specs=[
            pl.BlockSpec((rows, block), lambda i: (0, i)),
            pl.BlockSpec((3, rows, block), lambda i: (0, 0, i)),
            pl.BlockSpec((3, TAPS, block), lambda i: (0, 0, i)),
        ],
        out_shape=[
            jax.ShapeDtypeStruct((rows, width), BF16),
            jax.ShapeDtypeStruct((3, rows, width), BF16),
            jax.ShapeDtypeStruct((3, TAPS, width), F32),
        ],
        scratch_shapes=[
            pltpu.VMEM((3, rows + HALO, LANES), F32),
            pltpu.VMEM((3, rows + HALO, LANES), F32),
        ],
        cost_estimate=pl.CostEstimate(flops=150 * 10**6, transcendentals=0, bytes_accessed=24 * 10**6),
        name="finish",
    )(streams, before, grad_out, short_filter, mixed, gg, after)


def from_behind(block, axis, distance):
    devices = range(lax.axis_size(axis))
    route = [(i - distance, i) for i in devices if i - distance in devices]
    return lax.ppermute(block, axis, route)


def exchange(blocks):
    return lax.all_to_all(blocks, "seq", split_axis=0, concat_axis=0, tiled=True)


def first_rows_of(streams, before, grad_out, short_filter, mixed, gg, shards):
    width = streams.shape[2]
    top = jnp.concatenate([before, streams[:, :HALO]], axis=1).astype(F32)

    def short(i):
        total = short_filter[i, 0] * top[i, HALO:]
        for j in range(1, TAPS):
            total = total + short_filter[i, j] * top[i, HALO - j : 2 * HALO - j]
        return total

    def rows_of(blocks):
        return blocks[:, :HALO].transpose(1, 0, 2).reshape(HALO, width).astype(F32)

    mixed_top = rows_of(mixed)
    gg_top = rows_of(gg)
    gout_top = grad_out[:HALO].astype(F32)
    return jnp.stack([gg_top * short(2), gout_top * mixed_top, gg_top * short(0)])


def body(streams, grad_out, long_filter, short_filter, skip_gain):
    shards = lax.axis_size("seq")
    rows = streams.shape[1]
    chans = streams.shape[2] // shards
    filter_len = long_filter.shape[0] * shards
    filter_blocks = filter_len // rows
    fwd, inv = turn_tables(shards, rows)
    taps = exchange(pack_taps(long_filter, shards)).reshape(filter_blocks, rows, chans)
    before = from_behind(streams[:, rows - HALO :], "seq", 1)
    gated, mix, bias_part = gates(streams, before, grad_out, short_filter, shards)
    skip = lax.dynamic_slice_in_dim(skip_gain, lax.axis_index("seq") * chans, chans)[None]
    gated_all = exchange(gated)
    mix_all = exchange(mix)
    mixed_all, spec_g, spec_h = value_path(gated_all, taps, skip, fwd, inv)
    mixed = exchange(mixed_all)
    gg_all, raw_all, sq_part = grad_path(mix_all, spec_g, spec_h, skip, fwd, inv, filter_blocks)
    gg = exchange(gg_all)
    raw = exchange(raw_all.reshape(shards, filter_len // shards, chans))
    after = from_behind(first_rows_of(streams, before, grad_out, short_filter, mixed, gg, shards), "seq", -1)
    output, grad_streams, short_part = finish(
        streams, before, grad_out, short_filter, mixed, gg, after, shards
    )
    short_bias = jnp.concatenate([short_part.reshape(3 * TAPS, -1), bias_part], axis=0)
    short_bias = lax.psum(short_bias, "seq")
    local_sq = jnp.sum(sq_part) + jnp.sum(short_bias * short_bias) / shards
    sq_total = lax.psum(local_sq, ("seq", "chan"))
    param_count = LF * D + (3 * TAPS + 1) * D
    clip = 1.0 / jnp.sqrt(sq_total / param_count + 1e-06)
    filter_grad = scale_taps(raw, clip.reshape(1, 1))
    small = short_bias * clip
    return (
        output,
        grad_streams,
        filter_grad,
        small[: 3 * TAPS].reshape(3, TAPS, -1),
        small[3 * TAPS],
    )


def solution(mesh):
    placed = (
        P(None, "seq", "chan"),
        P("seq", "chan"),
        P("seq", "chan"),
        P(None, None, "chan"),
        P("chan"),
    )
    return jax.shard_map(
        body,
        mesh=mesh,
        in_specs=placed,
        out_specs=(
            P("seq", "chan"),
            P(None, "seq", "chan"),
            P("seq", "chan"),
            P(None, None, "chan"),
            P("chan"),
        ),
        check_vma=False,
    )
```

```python
import math

import jax
import jax.numpy as jnp
from jax import lax
from jax.experimental import pallas as pl
from jax.experimental.pallas import tpu as pltpu
from jax.sharding import PartitionSpec as P

D = 8192
LF = 8192
TAPS = 7
HALO = 8
EDGE = 16
LANES = 128
SUMS = 24
F32 = jnp.float32
BF16 = jnp.bfloat16


def add(a, b):
    if a is None:
        return b
    if b is None:
        return a
    return a + b


def neg(a):
    return None if a is None else -a


def sub(a, b):
    if b is None:
        return a
    if a is None:
        return -b
    return a - b


def scaled(a, c):
    if a is None or abs(c) < 1e-12:
        return None
    if abs(c - 1.0) < 1e-12:
        return a
    if abs(c + 1.0) < 1e-12:
        return -a
    return a * c


def cadd(a, b):
    return (add(a[0], b[0]), add(a[1], b[1]))


def csub(a, b):
    return (sub(a[0], b[0]), sub(a[1], b[1]))


def times_i(a, sign):
    return (neg(a[1]), a[0]) if sign > 0 else (a[1], neg(a[0]))


def cmul(a, angle, gain=1.0):
    c = math.cos(angle)
    s = math.sin(angle)
    re, im = a
    if abs(abs(c) - abs(s)) < 1e-12 and re is not None and im is not None:
        root = abs(c) * gain
        sc = 1.0 if c > 0 else -1.0
        ss = 1.0 if s > 0 else -1.0
        if sc * ss > 0:
            return ((re - im) * (root * sc), (re + im) * (root * sc))
        return ((re + im) * (root * sc), (im - re) * (root * sc))
    c = c * gain
    s = s * gain
    return (sub(scaled(re, c), scaled(im, s)), add(scaled(im, c), scaled(re, s)))


def complex_dft(xs, sign):
    n = len(xs)
    if n == 1:
        return list(xs)
    half = n // 2
    sums = [cadd(xs[i], xs[i + half]) for i in range(half)]
    difs = [csub(xs[i], xs[i + half]) for i in range(half)]
    if n == 2:
        return [sums[0], difs[0]]
    quarter = n // 4
    out = [None] * n
    out[0::2] = complex_dft(sums, sign)
    turn = sign * 2.0 * math.pi / n
    first = []
    third = []
    for i in range(quarter):
        rot = times_i(difs[i + quarter], sign)
        first.append(cmul(cadd(difs[i], rot), turn * i))
        third.append(cmul(csub(difs[i], rot), turn * 3 * i))
    out[1::4] = complex_dft(first, sign)
    out[3::4] = complex_dft(third, sign)
    return out


def real_dft(xs):
    n = len(xs)
    if n == 1:
        return [(xs[0], None)]
    half = n // 2
    sums = [add(xs[i], xs[i + half]) for i in range(half)]
    difs = [sub(xs[i], xs[i + half]) for i in range(half)]
    if n == 2:
        return [(sums[0], None), (difs[0], None)]
    quarter = n // 4
    out = [None] * (half + 1)
    out[0::2] = real_dft(sums)
    turn = -2.0 * math.pi / n
    odd = [cmul((difs[i], neg(difs[i + quarter])), turn * i) for i in range(quarter)]
    for j, value in enumerate(complex_dft(odd, -1)):
        k = 4 * j + 1
        if k <= half:
            out[k] = value
        else:
            out[n - k] = (value[0], neg(value[1]))
    return out


def real_idft(spec, keep):
    n = 2 * (len(spec) - 1)
    if n == 2:
        both = [add(spec[0][0], spec[1][0]), sub(spec[0][0], spec[1][0])]
        return both[:keep]
    half = n // 2
    quarter = n // 4
    even = real_idft(spec[0::2], half)
    odd = []
    for j in range(quarter):
        k = 4 * j + 1
        odd.append(spec[k] if k <= half else (spec[n - k][0], neg(spec[n - k][1])))
    turn = 2.0 * math.pi / n
    rest = [cmul(v, turn * i, 2.0) for i, v in enumerate(complex_dft(odd, 1))]
    wave = [rest[i][0] for i in range(quarter)] + [neg(rest[i][1]) for i in range(quarter)]
    out = [add(even[i], wave[i]) for i in range(half)]
    if keep > half:
        out = out + [sub(even[i], wave[i]) for i in range(half)]
    return out[:keep]


def turn_tables(shards, rows):
    radix = 2 * shards
    count = radix * rows
    k1 = jnp.arange(shards + 1, dtype=jnp.int32)[:, None]
    r = jnp.arange(rows, dtype=jnp.int32)
    fine = 2.0 * math.pi / count * (k1 * r[None, :] % count).astype(F32)
    coarse = 2.0 * math.pi / rows * (r[:, None] * r[None, :] % rows).astype(F32)
    fine_c = jnp.cos(fine)
    fine_s = jnp.sin(fine)
    coarse_c = jnp.cos(coarse)[None]
    coarse_s = jnp.sin(coarse)[None]

    def pair(fc, fs, gain):
        cos = fc * coarse_c - fs * coarse_s
        sin = fs * coarse_c + fc * coarse_s
        return (jnp.concatenate([cos, sin], axis=1) * gain).astype(BF16)

    fwd = pair(fine_c[:, None, :], fine_s[:, None, :], 1.0)
    inv = pair(fine_c[:, :, None], fine_s[:, :, None], 1.0 / count)
    return fwd, inv


def over_tiles(rows, work):
    def step(i, carry):
        work(pl.multiple_of(i * 16, 16))
        return carry

    lax.fori_loop(0, rows // 16, step, 0)


def split_in(load, blocks, shards, rows, store):
    def work(r):
        rs = pl.ds(r, 16)
        xs = [load(s, rs).astype(F32) for s in range(blocks)]
        xs = xs + [None] * (2 * shards - blocks)
        for k, (re, im) in enumerate(real_dft(xs)):
            if im is None:
                im = jnp.zeros(re.shape, F32)
            store(k, rs, re.astype(BF16), im.astype(BF16))

    over_tiles(rows, work)


def load_spec(load, shards):
    spec = []
    for k in range(shards + 1):
        re, im = load(k)
        spec.append((re, None if k == 0 or k == shards else im))
    return spec


def dot(a, b):
    return jnp.dot(a, b, preferred_element_type=F32)


def backward(table, z_re, z_im, rows, step):
    chans = z_re.shape[1]
    z_re = z_re.astype(BF16)
    z_im = z_im.astype(BF16)
    if step == chans:
        p = dot(table, jnp.concatenate([z_re, z_im], axis=1))
        return p[:rows, :step] - p[rows:, step:], p[rows:, :step] + p[:rows, step:]
    p = dot(table, z_re)
    q = dot(table, z_im)
    return p[:rows] - q[rows:], p[rows:] + q[:rows]


def whole(shape):
    zeros = (0,) * len(shape)
    return pl.BlockSpec(shape, lambda *_: zeros, pipeline_mode=pl.Buffered(1))


def per_step(shape):
    zeros = (0,) * (len(shape) - 1)
    return pl.BlockSpec(shape, lambda i: (i,) + zeros)


def in_smem():
    return pl.BlockSpec(memory_space=pltpu.SMEM)


def untouched():
    return pl.BlockSpec(memory_space=pl.ANY)


def raw_path(both, fwd, inv, is_low, packed, low_before, part, parts, tap_rows, live, fold):
    shards, _, rows, chans = both.shape
    steps = shards + 1
    step = max(chans, LANES)
    per_shard = tap_rows // rows
    blocks = live * per_shard

    def kernel(*refs):
        refs = list(refs)
        x_ref, fwd_ref, inv_ref = refs[:3]
        del refs[:3]
        if fold:
            flag_ref, h_ref = refs[:2]
            del refs[:2]
        if part:
            del refs[:1]
        spec_ref, low_ref, sq_ref = refs[:3]
        del refs[:3]
        if fold:
            send_ref = refs.pop(0)
        a_ref, y_ref = refs
        k = pl.program_id(0)

        @pl.when(k == 0)
        def _():
            for i in range(2):

                def store(at, rs, re, im, i=i):
                    a_ref[at, 0, rs, pl.ds(i * step, chans)] = re
                    a_ref[at, 1, rs, pl.ds(i * step, chans)] = im

                split_in(lambda s, rs, i=i: x_ref[s, i, rs, :], shards, shards, rows, store)

        p = dot(fwd_ref[0], a_ref[k, 0])
        q = dot(fwd_ref[0], a_ref[k, 1])
        re = p[:rows] + q[rows:]
        im = q[:rows] - p[rows:]
        spec_ref[0, 0] = re
        spec_ref[0, 1] = im
        g_re = re[:, :chans]
        g_im = im[:, :chans]
        m_re = re[:, step : step + chans]
        m_im = im[:, step : step + chans]
        y_re, y_im = backward(inv_ref[0], g_re * m_re + g_im * m_im, g_re * m_im - g_im * m_re, rows, step)
        y_ref[k, 0] = y_re
        y_ref[k, 1] = y_im

        @pl.when(k == steps - 1)
        def _():
            sq_ref[...] = jnp.zeros(sq_ref.shape, F32)

            def work(r):
                rs = pl.ds(r, 16)
                out = real_idft(load_spec(lambda at: (y_ref[at, 0, rs, :], y_ref[at, 1, rs, :]), shards), shards)
                square = None
                for s in range(blocks):
                    low_ref[s // per_shard, 0, pl.ds((s % per_shard) * rows + r, 16), :] = out[s].astype(BF16)
                    square = add(square, out[s] * out[s])
                sq_ref[...] += square[:8] + square[8:]

            over_tiles(rows, work)
            if fold:

                @pl.when(flag_ref[0, 0] == 1)
                def _():
                    for s in range(shards):
                        send_ref[s] = h_ref[s]

                @pl.when(flag_ref[0, 0] == 0)
                def _():
                    for s in range(shards):
                        if s < live:
                            send_ref[s] = low_ref[s, 0]
                        else:
                            send_ref[s] = jnp.zeros((tap_rows, chans), BF16)

    ins = [both, fwd, inv]
    in_specs = [
        whole(both.shape),
        per_step((1, 2 * rows, rows)),
        per_step((1, 2 * rows, rows)),
    ]
    if fold:
        ins += [is_low, packed]
        in_specs += [in_smem(), whole(packed.shape)]
    aliases = {}
    if part:
        aliases = {len(ins): 1}
        ins.append(low_before)
        in_specs.append(untouched())
    out_specs = [
        per_step((1, 2, rows, 2 * step)),
        pl.BlockSpec((live, 1, tap_rows, chans), lambda i: (0, part, 0, 0), pipeline_mode=pl.Buffered(1)),
        whole((8, chans)),
    ]
    out_shape = [
        jax.ShapeDtypeStruct((steps, 2, rows, 2 * step), F32),
        jax.ShapeDtypeStruct((live, parts, tap_rows, chans), BF16),
        jax.ShapeDtypeStruct((8, chans), F32),
    ]
    if fold:
        out_specs.append(whole(packed.shape))
        out_shape.append(jax.ShapeDtypeStruct(packed.shape, BF16))
    return pl.pallas_call(
        kernel,
        grid=(steps,),
        in_specs=in_specs,
        out_specs=out_specs,
        out_shape=out_shape,
        scratch_shapes=[
            pltpu.VMEM((steps, 2, rows, 2 * step), BF16),
            pltpu.VMEM((steps, 2, rows, chans), F32),
        ],
        input_output_aliases=aliases,
        cost_estimate=pl.CostEstimate(flops=20 * 10**9, transcendentals=0, bytes_accessed=25 * 10**6),
        name="raw_path",
    )(*ins)


def conv_path(both, taps, spec, skip, fwd, inv):
    shards, _, rows, chans = both.shape
    steps = shards + 1
    step = max(chans, LANES)
    blocks = min(taps.shape[0], shards)

    def kernel(x_ref, h_ref, spec_ref, skip_ref, fwd_ref, inv_ref, out_ref, a_ref, y_ref):
        k = pl.program_id(0)

        @pl.when(k == 0)
        def _():
            def store(at, rs, re, im):
                a_ref[at, rs, pl.ds(0, chans)] = re
                a_ref[at, rs, pl.ds(step, chans)] = im

            split_in(lambda s, rs: h_ref[s, rs, :], blocks, shards, rows, store)

        p = dot(fwd_ref[0], a_ref[k])
        h_re = p[:rows, :chans] + p[rows:, step : step + chans]
        h_im = p[:rows, step : step + chans] - p[rows:, :chans]
        g_re = spec_ref[0, 0, :, pl.ds(0, chans)]
        g_im = spec_ref[0, 1, :, pl.ds(0, chans)]
        m_re = spec_ref[0, 0, :, pl.ds(step, chans)]
        m_im = spec_ref[0, 1, :, pl.ds(step, chans)]
        y_re, y_im = backward(inv_ref[0], g_re * h_re - g_im * h_im, g_re * h_im + g_im * h_re, rows, step)
        y_ref[k, 0] = y_re
        y_ref[k, 1] = y_im
        y_re, y_im = backward(inv_ref[0], h_re * m_re + h_im * m_im, h_re * m_im - h_im * m_re, rows, step)
        y_ref[k, 2] = y_re
        y_ref[k, 3] = y_im

        @pl.when(k == steps - 1)
        def _():
            gain = skip_ref[...]
            for i in range(2):

                def work(r, i=i):
                    rs = pl.ds(r, 16)
                    spectrum = load_spec(lambda at: (y_ref[at, 2 * i, rs, :], y_ref[at, 2 * i + 1, rs, :]), shards)
                    out = real_idft(spectrum, shards)
                    out = [(out[s] + gain * x_ref[s, i, rs, :].astype(F32)).astype(BF16) for s in range(shards)]
                    for s in range(shards):
                        out_ref[s, i, rs, :] = out[s]

                    @pl.when(r == 0)
                    def _():
                        for s in range(shards - 1):
                            out_ref[s, i, pl.ds(rows, EDGE), :] = out[s + 1]
                        out_ref[shards - 1, i, pl.ds(rows, EDGE), :] = jnp.zeros((EDGE, chans), BF16)

                over_tiles(rows, work)

    out_block = (shards, 2, rows + EDGE, chans)
    return pl.pallas_call(
        kernel,
        grid=(steps,),
        in_specs=[
            whole(both.shape),
            whole((blocks, rows, chans)),
            per_step((1, 2, rows, 2 * step)),
            whole((1, chans)),
            per_step((1, 2 * rows, rows)),
            per_step((1, 2 * rows, rows)),
        ],
        out_specs=whole(out_block),
        out_shape=jax.ShapeDtypeStruct(out_block, BF16),
        scratch_shapes=[
            pltpu.VMEM((steps, rows, 2 * step), BF16),
            pltpu.VMEM((steps, 4, rows, chans), F32),
        ],
        cost_estimate=pl.CostEstimate(flops=20 * 10**9, transcendentals=0, bytes_accessed=25 * 10**6),
        name="conv_path",
    )(both, taps, spec, skip, fwd, inv)


def plan_lanes(width, chans):
    block = max(chans, LANES)
    while block < 512 and width % (2 * block) == 0:
        block *= 2
    return block


def put(ref, lead, rs, c, value):
    chans = ref.shape[-1]
    width = value.shape[1]
    if chans >= width:
        ref[(c // chans,) + lead + (rs, pl.ds(c % chans, width))] = value
        return
    for i in range(width // chans):
        ref[(c // chans + i,) + lead + (rs, slice(None))] = value[:, i * chans : (i + 1) * chans]


def take(ref, lead, rs, c, width):
    chans = ref.shape[-1]
    if chans >= width:
        return ref[(c // chans,) + lead + (rs, pl.ds(c % chans, width))].astype(F32)
    first = c // chans
    return jnp.concatenate(
        [ref[(first + i,) + lead + (rs, slice(None))].astype(F32) for i in range(width // chans)], axis=1
    )


def pack_taps(long_filter, shards, part, parts):
    rows, width = long_filter.shape
    width = width // parts
    chans = width // shards
    block = plan_lanes(width, chans)
    count = width // block
    groups = block // chans

    def kernel(x_ref, o_ref):
        for c in range(0, block, LANES):
            put(o_ref, (), pl.ds(0, rows), c, x_ref[:, pl.ds(c, LANES)].astype(BF16))

    return pl.pallas_call(
        kernel,
        grid=(count,),
        in_specs=[pl.BlockSpec((rows, block), lambda i: (0, part * count + i))],
        out_specs=pl.BlockSpec((groups, rows, chans), lambda i: (i, 0, 0)),
        out_shape=jax.ShapeDtypeStruct((shards, rows, chans), BF16),
        cost_estimate=pl.CostEstimate(flops=10**6, transcendentals=0, bytes_accessed=6 * 10**6),
        name="pack_taps",
    )(long_filter)


def scale_taps(clip, low, shared, shards):
    live, parts, rows, chans = low.shape
    width = shards * chans
    block = plan_lanes(width, chans)
    while (live * chans) % block:
        block //= 2
    count = width // block
    groups = block // chans
    split = live // groups

    def kernel(*refs):
        c_ref, low_ref = refs[:2]
        o_ref = refs[-1]
        q = pl.program_id(0)
        i = pl.program_id(1)
        gain = c_ref[0, 0]

        @pl.when(i < split)
        def _():
            for c in range(0, block, LANES):
                o_ref[:, pl.ds(c, LANES)] = take(low_ref, (0,), pl.ds(0, rows), c, LANES) * gain

        for part, x_ref in enumerate(refs[2:-1]):

            @pl.when(jnp.logical_and(i >= split, q == part))
            def _():
                for c in range(0, block, LANES):
                    o_ref[:, pl.ds(c, LANES)] = take(x_ref, (), pl.ds(0, rows), c, LANES) * gain

    def shared_map(part):
        def index(q, i):
            upper = jnp.maximum(i, split)
            held = split if part else count - 1
            return (jnp.where(q == part, upper, held), 0, 0)

        return index

    return pl.pallas_call(
        kernel,
        grid=(parts, count),
        in_specs=[
            in_smem(),
            pl.BlockSpec((groups, 1, rows, chans), lambda q, i: (jnp.minimum(i, split - 1), q, 0, 0)),
        ]
        + [pl.BlockSpec((groups, rows, chans), shared_map(p)) for p in range(len(shared))],
        out_specs=pl.BlockSpec((rows, block), lambda q, i: (0, q * count + i)),
        out_shape=jax.ShapeDtypeStruct((rows, parts * width), F32),
        name="scale_taps",
    )(clip, low, *shared)


def short_rows(ext_ref, w_ref, i, cs, r, rows):
    total = w_ref[i, 0:1, cs] * ext_ref[i, pl.ds(HALO + r, rows), :]
    for j in range(1, TAPS):
        total = total + w_ref[i, j : j + 1, cs] * ext_ref[i, pl.ds(HALO + r - j, rows), :]
    return total


def gates(streams, before, grad_out, short_filter, shards, part, parts):
    _, rows, width = streams.shape
    width = width // parts
    chans = width // shards
    block = plan_lanes(width, chans)
    count = width // block
    groups = block // chans
    chunk = math.gcd(rows, 64)

    def kernel(x_ref, b_ref, go_ref, w_ref, o_ref, ext_ref):
        for c in range(0, block, LANES):
            cs = pl.ds(c, LANES)
            for i in range(3):
                ext_ref[i, pl.ds(0, HALO), :] = b_ref[i, :, cs].astype(F32)
                ext_ref[i, pl.ds(HALO, rows), :] = x_ref[i, :, cs].astype(F32)
            for r in range(0, rows, chunk):
                rs = pl.ds(r, chunk)
                gated = short_rows(ext_ref, w_ref, 0, cs, r, chunk) * short_rows(ext_ref, w_ref, 2, cs, r, chunk)
                mix = go_ref[rs, cs].astype(F32) * short_rows(ext_ref, w_ref, 1, cs, r, chunk)
                put(o_ref, (0,), rs, c, gated.astype(BF16))
                put(o_ref, (1,), rs, c, mix.astype(BF16))

    return pl.pallas_call(
        kernel,
        grid=(count,),
        in_specs=[
            pl.BlockSpec((3, rows, block), lambda i: (0, 0, part * count + i)),
            pl.BlockSpec((3, HALO, block), lambda i: (0, 0, part * count + i)),
            pl.BlockSpec((rows, block), lambda i: (0, part * count + i)),
            pl.BlockSpec((3, TAPS, block), lambda i: (0, 0, part * count + i)),
        ],
        out_specs=pl.BlockSpec((groups, 2, rows, chans), lambda i: (i, 0, 0, 0)),
        out_shape=jax.ShapeDtypeStruct((shards, 2, rows, chans), BF16),
        scratch_shapes=[pltpu.VMEM((3, rows + HALO, LANES), F32)],
        cost_estimate=pl.CostEstimate(flops=60 * 10**6, transcendentals=0, bytes_accessed=7 * 10**6),
        name="gates",
    )(streams, before, grad_out, short_filter)


def finish(streams, before, after, grad_out, short_filter, back, earlier, shards, part, parts):
    _, rows, full = streams.shape
    width = full // parts
    chans = width // shards
    block = plan_lanes(width, chans)
    count = width // block
    groups = block // chans
    chunk = math.gcd(rows, 64)

    def kernel(x_ref, b_ref, n_ref, go_ref, w_ref, y_ref, *refs):
        o_ref, gs_ref, st_ref, ext_ref, pre_ref = refs[-5:]
        for c in range(0, block, LANES):
            cs = pl.ds(c, LANES)
            for i in range(3):
                ext_ref[i, pl.ds(0, HALO), :] = b_ref[i, :, cs].astype(F32)
                ext_ref[i, pl.ds(HALO, rows), :] = x_ref[i, :, cs].astype(F32)
                ext_ref[i, pl.ds(HALO + rows, HALO), :] = n_ref[i, :, cs].astype(F32)
            bias = jnp.zeros((8, LANES), F32)
            for r in range(0, rows, chunk):
                rs = pl.ds(r, chunk)
                gout = go_ref[rs, cs].astype(F32)
                mixed = take(y_ref, (0,), rs, c, LANES)
                upper = take(y_ref, (1,), rs, c, LANES)
                x1s = short_rows(ext_ref, w_ref, 0, cs, r, chunk)
                vs = short_rows(ext_ref, w_ref, 2, cs, r, chunk)
                pre_ref[0, rs, :] = upper * vs
                pre_ref[2, rs, :] = upper * x1s
                pre_ref[1, rs, :] = gout * mixed
                gated = (x1s * vs).astype(BF16).astype(F32)
                x2s = short_rows(ext_ref, w_ref, 1, cs, r, chunk)
                o_ref[rs, cs] = (x2s * mixed).astype(BF16)
                term = gated * (gout * x2s).astype(BF16).astype(F32)
                bias = bias + jnp.sum(term.reshape(chunk // 8, 8, LANES), axis=0)
            mixed = take(y_ref, (0,), pl.ds(rows, EDGE), c, LANES)[:HALO]
            upper = take(y_ref, (1,), pl.ds(rows, EDGE), c, LANES)[:HALO]
            pre_ref[0, pl.ds(rows, HALO), :] = upper * short_rows(ext_ref, w_ref, 2, cs, rows, HALO)
            pre_ref[2, pl.ds(rows, HALO), :] = upper * short_rows(ext_ref, w_ref, 0, cs, rows, HALO)
            pre_ref[1, pl.ds(rows, HALO), :] = n_ref[3, :, cs].astype(F32) * mixed
            lines = []
            for i in range(3):
                sums = [jnp.zeros((8, LANES), F32) for _ in range(TAPS)]
                for r in range(0, rows, chunk):
                    rs = pl.ds(r, chunk)
                    own = pre_ref[i, rs, :]
                    total = w_ref[i, 0:1, cs] * own
                    for j in range(TAPS):
                        if j:
                            total = total + w_ref[i, j : j + 1, cs] * pre_ref[i, pl.ds(r + j, chunk), :]
                        term = own * ext_ref[i, pl.ds(HALO + r - j, chunk), :]
                        sums[j] = sums[j] + jnp.sum(term.reshape(chunk // 8, 8, LANES), axis=0)
                    gs_ref[i, rs, cs] = total.astype(BF16)
                lines += [jnp.sum(v, axis=0, keepdims=True) for v in sums]
            lines.append(jnp.sum(bias, axis=0, keepdims=True))
            lines.append(jnp.zeros((SUMS - len(lines), LANES), F32))
            put(st_ref, (0,), pl.ds(0, SUMS), c, jnp.concatenate(lines, axis=0))

    at = lambda i: part * count + i
    ins = [streams, before, after, grad_out, short_filter, back]
    return pl.pallas_call(
        kernel,
        grid=(count,),
        in_specs=[
            pl.BlockSpec((3, rows, block), lambda i: (0, 0, at(i))),
            pl.BlockSpec((3, HALO, block), lambda i: (0, 0, at(i))),
            pl.BlockSpec((4, HALO, block), lambda i: (0, 0, at(i))),
            pl.BlockSpec((rows, block), lambda i: (0, at(i))),
            pl.BlockSpec((3, TAPS, block), lambda i: (0, 0, at(i))),
            pl.BlockSpec((groups, 2, rows + EDGE, chans), lambda i: (i, 0, 0, 0)),
        ]
        + [untouched() for _ in earlier],
        out_specs=[
            pl.BlockSpec((rows, block), lambda i: (0, at(i))),
            pl.BlockSpec((3, rows, block), lambda i: (0, 0, at(i))),
            pl.BlockSpec((groups, 1, SUMS, chans), lambda i: (i, part, 0, 0)),
        ],
        out_shape=[
            jax.ShapeDtypeStruct((rows, full), BF16),
            jax.ShapeDtypeStruct((3, rows, full), BF16),
            jax.ShapeDtypeStruct((shards, parts, SUMS, chans), F32),
        ],
        scratch_shapes=[
            pltpu.VMEM((3, rows + 2 * HALO, LANES), F32),
            pltpu.VMEM((3, rows + HALO, LANES), F32),
        ],
        input_output_aliases={len(ins) + i: i for i in range(len(earlier))},
        cost_estimate=pl.CostEstimate(flops=150 * 10**6, transcendentals=0, bytes_accessed=12 * 10**6),
        name="finish",
    )(*ins, *earlier)


def shift(block, axis, distance):
    devices = range(lax.axis_size(axis))
    route = [(i - distance, i) for i in devices if i - distance in devices]
    return lax.ppermute(block, axis, route)


def exchange(blocks, groups=None):
    return lax.all_to_all(blocks, "seq", split_axis=0, concat_axis=0, axis_index_groups=groups, tiled=True)


def following(value, earlier):
    return lax.optimization_barrier((value, earlier))[0]


def operator(streams, grad_out, long_filter, short_filter, skip_gain):
    shards = lax.axis_size("seq")
    rows = streams.shape[1]
    width = streams.shape[2]
    parts = 2 if width % (2 * shards * LANES) == 0 else 1
    span = width // parts
    chans = span // shards
    tap_rows = long_filter.shape[0]
    live = min(shards, shards * rows // tap_rows)
    fold = 2 * live <= shards
    mine = lax.axis_index("seq")
    is_low = (mine < live).astype(jnp.int32).reshape(1, 1)
    fwd, inv = turn_tables(shards, rows)
    before = shift(streams[:, rows - HALO :], "seq", 1)
    after = shift(jnp.concatenate([streams[:, :HALO], grad_out[None, :HALO]], axis=0), "seq", -1)
    skips = [lax.dynamic_slice_in_dim(skip_gain, p * span + mine * chans, chans)[None] for p in range(parts)]

    both = []
    packed = []
    for p in range(parts):
        sent = gates(streams, before, grad_out, short_filter, shards, p, parts)
        both.append(exchange(sent))
    for p in range(parts):
        packed.append(pack_taps(long_filter, shards, p, parts))
    spec = []
    shared = []
    squares = 0.0
    low = None
    for p in range(parts):
        out = raw_path(both[p], fwd, inv, is_low, packed[p], low, p, parts, tap_rows, live, fold)
        spec.append(out[0])
        low = out[1]
        squares = squares + jnp.sum(out[2])
        shared.append(exchange(out[3] if fold else packed[p]))
    back = []
    for p in range(parts):
        taps = shared[p].reshape(shards * tap_rows // rows, rows, chans)
        sent = conv_path(both[p], taps, spec[p], skips[p], fwd, inv)
        back.append(exchange(sent))
    groups = None
    if fold:
        groups = [list(range(i, i + live)) for i in range(0, shards, live)]
    raw = exchange(following(low, back[-1]), groups)
    done = []
    for p in range(parts):
        done = finish(streams, before, after, grad_out, short_filter, back[p], done, shards, p, parts)
    output, grad_streams, sums = done
    mine_sums = jnp.sum(exchange(following(sums, raw)), axis=0)
    local_sq = squares + jnp.sum(mine_sums * mine_sums)
    line = lax.broadcasted_iota(jnp.int32, mine_sums.shape, 1)
    mine_sums = jnp.where(line == SUMS - 1, local_sq, mine_sums)
    small = exchange(jnp.broadcast_to(mine_sums[None], (shards,) + mine_sums.shape))
    sq_total = lax.psum(jnp.sum(small[:, 0, SUMS - 1, 0]), "chan")
    param_count = LF * D + (3 * TAPS + 1) * D
    clip = 1.0 / jnp.sqrt(sq_total / param_count + 1e-06)
    kept = jnp.where(is_low == 1, clip, 0.0)
    filter_grad = scale_taps(kept, raw, shared if fold else [], shards)
    small = small.transpose(2, 1, 0, 3).reshape(SUMS, width) * clip
    return (
        output,
        grad_streams,
        filter_grad,
        small[: 3 * TAPS].reshape(3, TAPS, width),
        small[3 * TAPS],
    )


def solution(mesh):
    placed = (
        P(None, "seq", "chan"),
        P("seq", "chan"),
        P("seq", "chan"),
        P(None, None, "chan"),
        P("chan"),
    )
    return jax.shard_map(
        operator,
        mesh=mesh,
        in_specs=placed,
        out_specs=(
            P("seq", "chan"),
            P(None, "seq", "chan"),
            P("seq", "chan"),
            P(None, None, "chan"),
            P("chan"),
        ),
        check_vma=False,
    )
```

```python
import math

import jax
import jax.numpy as jnp
from jax import lax
from jax.experimental import pallas as pl
from jax.experimental.pallas import tpu as pltpu
from jax.sharding import PartitionSpec as P


D = 8192
LF = 8192
TAPS = 7
HALO = 8
EDGE = 8
LANES = 128
SUMS = 24
F32 = jnp.float32
BF16 = jnp.bfloat16


def add(a, b):
    if a is None:
        return b
    if b is None:
        return a
    return a + b


def neg(a):
    return None if a is None else -a


def sub(a, b):
    if b is None:
        return a
    if a is None:
        return -b
    return a - b


def scaled(a, c):
    if a is None or abs(c) < 1e-12:
        return None
    if abs(c - 1.0) < 1e-12:
        return a
    if abs(c + 1.0) < 1e-12:
        return -a
    return a * c


def cadd(a, b):
    return (add(a[0], b[0]), add(a[1], b[1]))


def csub(a, b):
    return (sub(a[0], b[0]), sub(a[1], b[1]))


def times_i(a, sign):
    return (neg(a[1]), a[0]) if sign > 0 else (a[1], neg(a[0]))


def cmul(a, angle, gain=1.0):
    c = math.cos(angle)
    s = math.sin(angle)
    re, im = a
    if abs(abs(c) - abs(s)) < 1e-12 and re is not None and im is not None:
        root = abs(c) * gain
        sc = 1.0 if c > 0 else -1.0
        ss = 1.0 if s > 0 else -1.0
        if sc * ss > 0:
            return ((re - im) * (root * sc), (re + im) * (root * sc))
        return ((re + im) * (root * sc), (im - re) * (root * sc))
    c = c * gain
    s = s * gain
    return (sub(scaled(re, c), scaled(im, s)), add(scaled(im, c), scaled(re, s)))


def complex_dft(xs, sign):
    n = len(xs)
    if n == 1:
        return list(xs)
    half = n // 2
    sums = [cadd(xs[i], xs[i + half]) for i in range(half)]
    difs = [csub(xs[i], xs[i + half]) for i in range(half)]
    if n == 2:
        return [sums[0], difs[0]]
    quarter = n // 4
    out = [None] * n
    out[0::2] = complex_dft(sums, sign)
    turn = sign * 2.0 * math.pi / n
    first = []
    third = []
    for i in range(quarter):
        rot = times_i(difs[i + quarter], sign)
        first.append(cmul(cadd(difs[i], rot), turn * i))
        third.append(cmul(csub(difs[i], rot), turn * 3 * i))
    out[1::4] = complex_dft(first, sign)
    out[3::4] = complex_dft(third, sign)
    return out


def real_dft(xs):
    n = len(xs)
    if n == 1:
        return [(xs[0], None)]
    half = n // 2
    sums = [add(xs[i], xs[i + half]) for i in range(half)]
    difs = [sub(xs[i], xs[i + half]) for i in range(half)]
    if n == 2:
        return [(sums[0], None), (difs[0], None)]
    quarter = n // 4
    out = [None] * (half + 1)
    out[0::2] = real_dft(sums)
    turn = -2.0 * math.pi / n
    odd = [cmul((difs[i], neg(difs[i + quarter])), turn * i) for i in range(quarter)]
    for j, value in enumerate(complex_dft(odd, -1)):
        k = 4 * j + 1
        if k <= half:
            out[k] = value
        else:
            out[n - k] = (value[0], neg(value[1]))
    return out


def real_idft(spec, keep):
    n = 2 * (len(spec) - 1)
    if n == 2:
        both = [add(spec[0][0], spec[1][0]), sub(spec[0][0], spec[1][0])]
        return both[:keep]
    half = n // 2
    quarter = n // 4
    even = real_idft(spec[0::2], half)
    odd = []
    for j in range(quarter):
        k = 4 * j + 1
        odd.append(spec[k] if k <= half else (spec[n - k][0], neg(spec[n - k][1])))
    turn = 2.0 * math.pi / n
    rest = [cmul(v, turn * i, 2.0) for i, v in enumerate(complex_dft(odd, 1))]
    wave = [rest[i][0] for i in range(quarter)] + [neg(rest[i][1]) for i in range(quarter)]
    out = [add(even[i], wave[i]) for i in range(half)]
    if keep > half:
        out = out + [sub(even[i], wave[i]) for i in range(half)]
    return out[:keep]


def turn_tables(shards, rows):
    radix = 2 * shards
    count = radix * rows
    k1 = jnp.arange(shards + 1, dtype=jnp.int32)[:, None]
    r = jnp.arange(rows, dtype=jnp.int32)
    fine = 2.0 * math.pi / count * (k1 * r[None, :] % count).astype(F32)
    coarse = 2.0 * math.pi / rows * (r[:, None] * r[None, :] % rows).astype(F32)
    fine_c = jnp.cos(fine)
    fine_s = jnp.sin(fine)
    coarse_c = jnp.cos(coarse)[None]
    coarse_s = jnp.sin(coarse)[None]

    def pair(fc, fs, gain):
        cos = fc * coarse_c - fs * coarse_s
        sin = fs * coarse_c + fc * coarse_s
        return (jnp.concatenate([cos, sin], axis=1) * gain).astype(BF16)

    fwd = pair(fine_c[:, None, :], fine_s[:, None, :], 1.0)
    inv = pair(fine_c[:, :, None], fine_s[:, :, None], 1.0 / count)
    return fwd, inv


def over_tiles(rows, work):
    def step(i, carry):
        work(pl.multiple_of(i * 16, 16))
        return carry

    lax.fori_loop(0, rows // 16, step, 0)


def split_in(load, blocks, shards, rows, store):
    def work(r):
        rs = pl.ds(r, 16)
        xs = [load(s, rs).astype(F32) for s in range(blocks)]
        xs = xs + [None] * (2 * shards - blocks)
        for k, (re, im) in enumerate(real_dft(xs)):
            if im is None:
                im = jnp.zeros(re.shape, F32)
            store(k, rs, re.astype(BF16), im.astype(BF16))

    over_tiles(rows, work)


def load_spec(load, shards):
    spec = []
    for k in range(shards + 1):
        re, im = load(k)
        spec.append((re, None if k == 0 or k == shards else im))
    return spec


def dot(a, b):
    return jnp.dot(a, b, preferred_element_type=F32)


def backward(table, z_re, z_im, rows, step):
    chans = z_re.shape[1]
    z_re = z_re.astype(BF16)
    z_im = z_im.astype(BF16)
    if step == chans:
        p = dot(table, jnp.concatenate([z_re, z_im], axis=1))
        return p[:rows, :step] - p[rows:, step:], p[rows:, :step] + p[:rows, step:]
    p = dot(table, z_re)
    q = dot(table, z_im)
    return p[:rows] - q[rows:], p[rows:] + q[:rows]


def whole(shape):
    zeros = (0,) * len(shape)
    return pl.BlockSpec(shape, lambda *_: zeros, pipeline_mode=pl.Buffered(1))


def per_step(shape):
    zeros = (0,) * (len(shape) - 1)
    return pl.BlockSpec(shape, lambda i: (i,) + zeros)


def in_smem():
    return pl.BlockSpec(memory_space=pltpu.SMEM)


def resident():
    return pl.BlockSpec(memory_space=pltpu.VMEM)


def untouched():
    return pl.BlockSpec(memory_space=pl.ANY)


def raw_path(both, fwd, inv, where, packed, low_before, part, parts, tap_rows, live, fold):
    shards, _, rows, chans = both.shape
    steps = shards + 1
    step = max(chans, LANES)
    per_shard = tap_rows // rows
    blocks = live * per_shard

    def kernel(*refs):
        refs = list(refs)
        x_ref, fwd_ref, inv_ref = refs[:3]
        del refs[:3]
        if fold:
            flag_ref, h_ref = refs[:2]
            del refs[:2]
        if part:
            del refs[:1]
        spec_ref, low_ref, sq_ref = refs[:3]
        del refs[:3]
        if fold:
            send_ref = refs.pop(0)
        a_ref, y_ref = refs
        k = pl.program_id(0)
        mine = flag_ref[0, 1] if fold else 0

        @pl.when(k == 0)
        def _():
            for i in range(2):

                def store(at, rs, re, im, i=i):
                    a_ref[at, 0, rs, pl.ds(i * step, chans)] = re
                    a_ref[at, 1, rs, pl.ds(i * step, chans)] = im

                split_in(lambda s, rs, i=i: x_ref[s, i, rs, :], shards, shards, rows, store)

        p = dot(fwd_ref[0], a_ref[k, 0])
        q = dot(fwd_ref[0], a_ref[k, 1])
        re = p[:rows] + q[rows:]
        im = q[:rows] - p[rows:]
        spec_ref[0, 0] = re
        spec_ref[0, 1] = im
        g_re = re[:, :chans]
        g_im = im[:, :chans]
        m_re = re[:, step : step + chans]
        m_im = im[:, step : step + chans]
        y_re, y_im = backward(inv_ref[0], g_re * m_re + g_im * m_im, g_re * m_im - g_im * m_re, rows, step)
        y_ref[k, 0] = y_re
        y_ref[k, 1] = y_im

        @pl.when(k == steps - 1)
        def _():
            sq_ref[...] = jnp.zeros(sq_ref.shape, F32)

            def work(r):
                rs = pl.ds(r, 16)
                out = real_idft(load_spec(lambda at: (y_ref[at, 0, rs, :], y_ref[at, 1, rs, :]), shards), shards)
                square = None
                for s in range(blocks):
                    at = (s // per_shard) ^ mine
                    low_ref[at, 0, pl.ds((s % per_shard) * rows + r, 16), :] = out[s].astype(BF16)
                    square = add(square, out[s] * out[s])
                sq_ref[...] += square[:8] + square[8:]

            over_tiles(rows, work)
            if fold:

                @pl.when(flag_ref[0, 0] == 1)
                def _():
                    for s in range(shards):
                        send_ref[s] = h_ref[s]

                @pl.when(flag_ref[0, 0] == 0)
                def _():
                    for s in range(shards):
                        if s < live:
                            send_ref[s] = low_ref[s ^ mine, 0]
                        else:
                            send_ref[s] = jnp.zeros((tap_rows, chans), BF16)

    ins = [both, fwd, inv]
    in_specs = [
        resident(),
        per_step((1, 2 * rows, rows)),
        per_step((1, 2 * rows, rows)),
    ]
    if fold:
        ins += [where, packed]
        in_specs += [in_smem(), whole(packed.shape)]
    aliases = {}
    if part:
        aliases = {len(ins): 1}
        ins.append(low_before)
        in_specs.append(untouched())
    out_specs = [
        per_step((1, 2, rows, 2 * step)),
        pl.BlockSpec((live, 1, tap_rows, chans), lambda i: (0, part, 0, 0), pipeline_mode=pl.Buffered(1)),
        whole((8, chans)),
    ]
    out_shape = [
        jax.ShapeDtypeStruct((steps, 2, rows, 2 * step), F32),
        jax.ShapeDtypeStruct((live, parts, tap_rows, chans), BF16),
        jax.ShapeDtypeStruct((8, chans), F32),
    ]
    if fold:
        out_specs.append(whole(packed.shape))
        out_shape.append(jax.ShapeDtypeStruct(packed.shape, BF16))
    return pl.pallas_call(
        kernel,
        grid=(steps,),
        in_specs=in_specs,
        out_specs=out_specs,
        out_shape=out_shape,
        scratch_shapes=[
            pltpu.VMEM((steps, 2, rows, 2 * step), BF16),
            pltpu.VMEM((steps, 2, rows, chans), F32),
        ],
        input_output_aliases=aliases,
        cost_estimate=pl.CostEstimate(flops=20 * 10**9, transcendentals=0, bytes_accessed=25 * 10**6),
        name="raw_path",
    )(*ins)


def conv_path(both, taps, spec, skip, fwd, inv):
    shards, _, rows, chans = both.shape
    steps = shards + 1
    step = max(chans, LANES)
    blocks = min(taps.shape[0], shards)

    def kernel(x_ref, h_ref, spec_ref, skip_ref, fwd_ref, inv_ref, out_ref, a_ref, y_ref):
        k = pl.program_id(0)

        @pl.when(k == 0)
        def _():
            def store(at, rs, re, im):
                a_ref[at, rs, pl.ds(0, chans)] = re
                a_ref[at, rs, pl.ds(step, chans)] = im

            split_in(lambda s, rs: h_ref[s, rs, :], blocks, shards, rows, store)

        p = dot(fwd_ref[0], a_ref[k])
        h_re = p[:rows, :chans] + p[rows:, step : step + chans]
        h_im = p[:rows, step : step + chans] - p[rows:, :chans]
        g_re = spec_ref[0, 0, :, pl.ds(0, chans)]
        g_im = spec_ref[0, 1, :, pl.ds(0, chans)]
        m_re = spec_ref[0, 0, :, pl.ds(step, chans)]
        m_im = spec_ref[0, 1, :, pl.ds(step, chans)]
        y_re, y_im = backward(inv_ref[0], g_re * h_re - g_im * h_im, g_re * h_im + g_im * h_re, rows, step)
        y_ref[k, 0] = y_re
        y_ref[k, 1] = y_im
        y_re, y_im = backward(inv_ref[0], h_re * m_re + h_im * m_im, h_re * m_im - h_im * m_re, rows, step)
        y_ref[k, 2] = y_re
        y_ref[k, 3] = y_im

        @pl.when(k == steps - 1)
        def _():
            gain = skip_ref[...]
            for i in range(2):

                def work(r, i=i):
                    rs = pl.ds(r, 16)
                    spectrum = load_spec(lambda at: (y_ref[at, 2 * i, rs, :], y_ref[at, 2 * i + 1, rs, :]), shards)
                    out = real_idft(spectrum, shards)
                    out = [(out[s] + gain * x_ref[s, i, rs, :].astype(F32)).astype(BF16) for s in range(shards)]
                    for s in range(shards):
                        out_ref[s, i, rs, :] = out[s]

                    @pl.when(r == 0)
                    def _():
                        for s in range(shards - 1):
                            out_ref[s, i, pl.ds(rows, EDGE), :] = out[s + 1][:EDGE]
                        out_ref[shards - 1, i, pl.ds(rows, EDGE), :] = jnp.zeros((EDGE, chans), BF16)

                over_tiles(rows, work)

    out_block = (shards, 2, rows + EDGE, chans)
    return pl.pallas_call(
        kernel,
        grid=(steps,),
        in_specs=[
            resident(),
            resident(),
            per_step((1, 2, rows, 2 * step)),
            whole((1, chans)),
            per_step((1, 2 * rows, rows)),
            per_step((1, 2 * rows, rows)),
        ],
        out_specs=whole(out_block),
        out_shape=jax.ShapeDtypeStruct(out_block, BF16),
        scratch_shapes=[
            pltpu.VMEM((steps, rows, 2 * step), BF16),
            pltpu.VMEM((steps, 4, rows, chans), F32),
        ],
        cost_estimate=pl.CostEstimate(flops=20 * 10**9, transcendentals=0, bytes_accessed=25 * 10**6),
        name="conv_path",
    )(both, taps, spec, skip, fwd, inv)


def plan_lanes(width, chans):
    block = max(chans, LANES)
    while block < 512 and width % (2 * block) == 0:
        block *= 2
    return block


def put(ref, lead, rs, c, value):
    chans = ref.shape[-1]
    width = value.shape[1]
    if chans >= width:
        ref[(c // chans,) + lead + (rs, pl.ds(c % chans, width))] = value
        return
    for i in range(width // chans):
        ref[(c // chans + i,) + lead + (rs, slice(None))] = value[:, i * chans : (i + 1) * chans]


def take(ref, lead, rs, c, width):
    chans = ref.shape[-1]
    if chans >= width:
        return ref[(c // chans,) + lead + (rs, pl.ds(c % chans, width))].astype(F32)
    first = c // chans
    return jnp.concatenate(
        [ref[(first + i,) + lead + (rs, slice(None))].astype(F32) for i in range(width // chans)], axis=1
    )


def pack_taps(long_filter, shards, part, parts):
    rows, width = long_filter.shape
    width = width // parts
    chans = width // shards
    block = plan_lanes(width, chans)
    count = width // block
    groups = block // chans

    def kernel(x_ref, o_ref):
        for c in range(0, block, LANES):
            put(o_ref, (), pl.ds(0, rows), c, x_ref[:, pl.ds(c, LANES)].astype(BF16))

    return pl.pallas_call(
        kernel,
        grid=(count,),
        in_specs=[pl.BlockSpec((rows, block), lambda i: (0, part * count + i))],
        out_specs=pl.BlockSpec((groups, rows, chans), lambda i: (i, 0, 0)),
        out_shape=jax.ShapeDtypeStruct((shards, rows, chans), BF16),
        cost_estimate=pl.CostEstimate(flops=10**6, transcendentals=0, bytes_accessed=6 * 10**6),
        name="pack_taps",
    )(long_filter)


def scale_taps(clip, where, lows, shared, shards, live):
    parts, rows, chans = lows[0].shape[-3:]
    width = shards * chans
    block = plan_lanes(width, chans)
    while (live * chans) % block:
        block //= 2
    count = width // block
    groups = block // chans
    split = live // groups
    listed = len(lows) > 1

    def kernel(*refs):
        c_ref, at_ref = refs[:2]
        low_refs = refs[2 : 2 + len(lows)]
        o_ref = refs[-1]
        q = pl.program_id(0)
        i = pl.program_id(1)
        gain = c_ref[0, 0]

        @pl.when(i < split)
        def _():
            if not listed:
                for c in range(0, block, LANES):
                    o_ref[:, pl.ds(c, LANES)] = take(low_refs[0], (0,), pl.ds(0, rows), c, LANES) * gain
                return
            for j in range(groups):
                source = (i * groups + j) ^ at_ref[0, 1]
                for d, x_ref in enumerate(low_refs):

                    @pl.when(source == d)
                    def _(j=j, x_ref=x_ref):
                        o_ref[:, pl.ds(j * chans, chans)] = x_ref[q].astype(F32) * gain

        for part, x_ref in enumerate(refs[2 + len(lows) : -1]):

            @pl.when(jnp.logical_and(i >= split, q == part))
            def _(x_ref=x_ref):
                for c in range(0, block, LANES):
                    o_ref[:, pl.ds(c, LANES)] = take(x_ref, (), pl.ds(0, rows), c, LANES) * gain

    def shared_map(part):
        def index(q, i):
            upper = jnp.maximum(i, split)
            held = split if part else count - 1
            return (jnp.where(q == part, upper, held), 0, 0)

        return index

    if listed:
        low_specs = [whole((parts, rows, chans)) for _ in lows]
    else:
        low_specs = [pl.BlockSpec((groups, 1, rows, chans), lambda q, i: (jnp.minimum(i, split - 1), q, 0, 0))]
    return pl.pallas_call(
        kernel,
        grid=(parts, count),
        in_specs=[in_smem(), in_smem()]
        + low_specs
        + [pl.BlockSpec((groups, rows, chans), shared_map(p)) for p in range(len(shared))],
        out_specs=pl.BlockSpec((rows, block), lambda q, i: (0, q * count + i)),
        out_shape=jax.ShapeDtypeStruct((rows, parts * width), F32),
        name="scale_taps",
    )(clip, where, *lows, *shared)


def short_rows(ext_ref, w_ref, i, cs, r, rows):
    total = w_ref[i, 0:1, cs] * ext_ref[i, pl.ds(HALO + r, rows), :]
    for j in range(1, TAPS):
        total = total + w_ref[i, j : j + 1, cs] * ext_ref[i, pl.ds(HALO + r - j, rows), :]
    return total


def gates(streams, before, grad_out, short_filter, shards, part, parts):
    _, rows, width = streams.shape
    width = width // parts
    chans = width // shards
    block = plan_lanes(width, chans)
    count = width // block
    groups = block // chans
    chunk = math.gcd(rows, 64)

    def kernel(x_ref, b_ref, go_ref, w_ref, o_ref, ext_ref):
        for c in range(0, block, LANES):
            cs = pl.ds(c, LANES)
            for i in range(3):
                ext_ref[i, pl.ds(0, HALO), :] = b_ref[i, :, cs].astype(F32)
                ext_ref[i, pl.ds(HALO, rows), :] = x_ref[i, :, cs].astype(F32)
            for r in range(0, rows, chunk):
                rs = pl.ds(r, chunk)
                gated = short_rows(ext_ref, w_ref, 0, cs, r, chunk) * short_rows(ext_ref, w_ref, 2, cs, r, chunk)
                mix = go_ref[rs, cs].astype(F32) * short_rows(ext_ref, w_ref, 1, cs, r, chunk)
                put(o_ref, (0,), rs, c, gated.astype(BF16))
                put(o_ref, (1,), rs, c, mix.astype(BF16))

    return pl.pallas_call(
        kernel,
        grid=(count,),
        in_specs=[
            pl.BlockSpec((3, rows, block), lambda i: (0, 0, part * count + i)),
            pl.BlockSpec((3, HALO, block), lambda i: (0, 0, part * count + i)),
            pl.BlockSpec((rows, block), lambda i: (0, part * count + i)),
            pl.BlockSpec((3, TAPS, block), lambda i: (0, 0, part * count + i)),
        ],
        out_specs=pl.BlockSpec((groups, 2, rows, chans), lambda i: (i, 0, 0, 0)),
        out_shape=jax.ShapeDtypeStruct((shards, 2, rows, chans), BF16),
        scratch_shapes=[pltpu.VMEM((3, rows + HALO, LANES), F32)],
        cost_estimate=pl.CostEstimate(flops=60 * 10**6, transcendentals=0, bytes_accessed=7 * 10**6),
        name="gates",
    )(streams, before, grad_out, short_filter)


def finish(streams, before, after, grad_out, short_filter, back, earlier, shards, part, parts):
    _, rows, full = streams.shape
    width = full // parts
    chans = width // shards
    block = plan_lanes(width, chans)
    count = width // block
    groups = block // chans
    chunk = math.gcd(rows, 64)

    def kernel(x_ref, b_ref, n_ref, go_ref, w_ref, y_ref, *refs):
        o_ref, gs_ref, st_ref, ext_ref, pre_ref = refs[-5:]
        for c in range(0, block, LANES):
            cs = pl.ds(c, LANES)
            for i in range(3):
                ext_ref[i, pl.ds(0, HALO), :] = b_ref[i, :, cs].astype(F32)
                ext_ref[i, pl.ds(HALO, rows), :] = x_ref[i, :, cs].astype(F32)
                ext_ref[i, pl.ds(HALO + rows, HALO), :] = n_ref[i, :, cs].astype(F32)
            bias = jnp.zeros((8, LANES), F32)
            for r in range(0, rows, chunk):
                rs = pl.ds(r, chunk)
                gout = go_ref[rs, cs].astype(F32)
                mixed = take(y_ref, (0,), rs, c, LANES)
                upper = take(y_ref, (1,), rs, c, LANES)
                x1s = short_rows(ext_ref, w_ref, 0, cs, r, chunk)
                vs = short_rows(ext_ref, w_ref, 2, cs, r, chunk)
                pre_ref[0, rs, :] = upper * vs
                pre_ref[2, rs, :] = upper * x1s
                pre_ref[1, rs, :] = gout * mixed
                gated = (x1s * vs).astype(BF16).astype(F32)
                x2s = short_rows(ext_ref, w_ref, 1, cs, r, chunk)
                o_ref[rs, cs] = (x2s * mixed).astype(BF16)
                term = gated * (gout * x2s).astype(BF16).astype(F32)
                bias = bias + jnp.sum(term.reshape(chunk // 8, 8, LANES), axis=0)
            mixed = take(y_ref, (0,), pl.ds(rows, EDGE), c, LANES)[:HALO]
            upper = take(y_ref, (1,), pl.ds(rows, EDGE), c, LANES)[:HALO]
            pre_ref[0, pl.ds(rows, HALO), :] = upper * short_rows(ext_ref, w_ref, 2, cs, rows, HALO)
            pre_ref[2, pl.ds(rows, HALO), :] = upper * short_rows(ext_ref, w_ref, 0, cs, rows, HALO)
            pre_ref[1, pl.ds(rows, HALO), :] = n_ref[3, :, cs].astype(F32) * mixed
            lines = []
            for i in range(3):
                sums = [jnp.zeros((8, LANES), F32) for _ in range(TAPS)]
                for r in range(0, rows, chunk):
                    rs = pl.ds(r, chunk)
                    own = pre_ref[i, rs, :]
                    total = w_ref[i, 0:1, cs] * own
                    for j in range(TAPS):
                        if j:
                            total = total + w_ref[i, j : j + 1, cs] * pre_ref[i, pl.ds(r + j, chunk), :]
                        term = own * ext_ref[i, pl.ds(HALO + r - j, chunk), :]
                        sums[j] = sums[j] + jnp.sum(term.reshape(chunk // 8, 8, LANES), axis=0)
                    gs_ref[i, rs, cs] = total.astype(BF16)
                lines += [jnp.sum(v, axis=0, keepdims=True) for v in sums]
            lines.append(jnp.sum(bias, axis=0, keepdims=True))
            lines.append(jnp.zeros((SUMS - len(lines), LANES), F32))
            put(st_ref, (0,), pl.ds(0, SUMS), c, jnp.concatenate(lines, axis=0))

    at = lambda i: part * count + i
    ins = [streams, before, after, grad_out, short_filter, back]
    return pl.pallas_call(
        kernel,
        grid=(count,),
        in_specs=[
            pl.BlockSpec((3, rows, block), lambda i: (0, 0, at(i))),
            pl.BlockSpec((3, HALO, block), lambda i: (0, 0, at(i))),
            pl.BlockSpec((4, HALO, block), lambda i: (0, 0, at(i))),
            pl.BlockSpec((rows, block), lambda i: (0, at(i))),
            pl.BlockSpec((3, TAPS, block), lambda i: (0, 0, at(i))),
            pl.BlockSpec((groups, 2, rows + EDGE, chans), lambda i: (i, 0, 0, 0)),
        ]
        + [untouched() for _ in earlier],
        out_specs=[
            pl.BlockSpec((rows, block), lambda i: (0, at(i))),
            pl.BlockSpec((3, rows, block), lambda i: (0, 0, at(i))),
            pl.BlockSpec((groups, 1, SUMS, chans), lambda i: (i, part, 0, 0)),
        ],
        out_shape=[
            jax.ShapeDtypeStruct((rows, full), BF16),
            jax.ShapeDtypeStruct((3, rows, full), BF16),
            jax.ShapeDtypeStruct((shards, parts, SUMS, chans), F32),
        ],
        scratch_shapes=[
            pltpu.VMEM((3, rows + 2 * HALO, LANES), F32),
            pltpu.VMEM((3, rows + HALO, LANES), F32),
        ],
        input_output_aliases={len(ins) + i: i for i in range(len(earlier))},
        cost_estimate=pl.CostEstimate(flops=150 * 10**6, transcendentals=0, bytes_accessed=12 * 10**6),
        name="finish",
    )(*ins, *earlier)


def shift(block, axis, distance):
    devices = range(lax.axis_size(axis))
    route = [(i - distance, i) for i in devices if i - distance in devices]
    return lax.ppermute(block, axis, route)


def exchange(blocks, groups=None):
    return lax.all_to_all(blocks, "seq", split_axis=0, concat_axis=0, axis_index_groups=groups, tiled=True)


def following(value, earlier):
    return lax.optimization_barrier((value, earlier))[0]


def operator(streams, grad_out, long_filter, short_filter, skip_gain):
    shards = lax.axis_size("seq")
    rows = streams.shape[1]
    width = streams.shape[2]
    parts = 2 if width % (2 * shards * LANES) == 0 else 1
    span = width // parts
    chans = span // shards
    tap_rows = long_filter.shape[0]
    live = min(shards, shards * rows // tap_rows)
    fold = 2 * live <= shards
    mine = lax.axis_index("seq")
    is_low = mine < live
    where = jnp.stack([is_low.astype(jnp.int32), mine % live]).reshape(1, 2)
    fwd, inv = turn_tables(shards, rows)
    before = shift(streams[:, rows - HALO :], "seq", 1)
    after = shift(jnp.concatenate([streams[:, :HALO], grad_out[None, :HALO]], axis=0), "seq", -1)
    skips = [lax.dynamic_slice_in_dim(skip_gain, p * span + mine * chans, chans)[None] for p in range(parts)]

    both = []
    packed = []
    for p in range(parts):
        sent = gates(streams, before, grad_out, short_filter, shards, p, parts)
        both.append(exchange(sent))
    for p in range(parts):
        packed.append(pack_taps(long_filter, shards, p, parts))
    spec = []
    shared = []
    squares = 0.0
    low = None
    for p in range(parts):
        out = raw_path(both[p], fwd, inv, where, packed[p], low, p, parts, tap_rows, live, fold)
        spec.append(out[0])
        low = out[1]
        squares = squares + jnp.sum(out[2])
        shared.append(exchange(out[3] if fold else packed[p]))
    back = []
    for p in range(parts):
        taps = shared[p].reshape(shards * tap_rows // rows, rows, chans)
        sent = conv_path(both[p], taps, spec[p], skips[p], fwd, inv)
        back.append(exchange(sent))
    done = []
    lows = []
    for p in range(parts):
        done = finish(streams, before, after, grad_out, short_filter, back[p], done, shards, p, parts)
        if p == 0 and fold:
            ready = following(low, done[2])
            lows.append(ready[0])
            for d in range(1, live):
                lows.append(lax.ppermute(ready[d], "seq", [(i, i ^ d) for i in range(live)]))
    output, grad_streams, sums = done
    if not fold:
        lows.append(exchange(following(low, back[-1])))
        sums = following(sums, lows[0])
    mine_sums = jnp.sum(exchange(sums), axis=0)
    local_sq = squares + jnp.sum(mine_sums * mine_sums)
    upper_sq = lax.reduce_precision(local_sq, 8, 7)
    line = lax.broadcasted_iota(jnp.int32, mine_sums.shape, 1)
    mine_sums = jnp.where(line == SUMS - 2, upper_sq, mine_sums)
    mine_sums = jnp.where(line == SUMS - 1, local_sq - upper_sq, mine_sums).astype(BF16)
    small = exchange(jnp.broadcast_to(mine_sums[None], (shards,) + mine_sums.shape)).astype(F32)
    sq_total = lax.psum(jnp.sum(small[:, 0, SUMS - 2 :, 0]), "chan")
    param_count = LF * D + (3 * TAPS + 1) * D
    clip = 1.0 / jnp.sqrt(sq_total / param_count + 1e-06)
    kept = jnp.where(is_low, clip, 0.0).reshape(1, 1)
    filter_grad = scale_taps(kept, where, lows, shared if fold else [], shards, live)
    small = small.transpose(2, 1, 0, 3).reshape(SUMS, width) * clip
    return (
        output,
        grad_streams,
        filter_grad,
        small[: 3 * TAPS].reshape(3, TAPS, width),
        small[3 * TAPS],
    )


def solution(mesh):
    placed = (
        P(None, "seq", "chan"),
        P("seq", "chan"),
        P("seq", "chan"),
        P(None, None, "chan"),
        P("chan"),
    )
    return jax.shard_map(
        operator,
        mesh=mesh,
        in_specs=placed,
        out_specs=(
            P("seq", "chan"),
            P(None, "seq", "chan"),
            P("seq", "chan"),
            P(None, None, "chan"),
            P("chan"),
        ),
        check_vma=False,
    )
```

```python
import math

import jax
import jax.numpy as jnp
from jax import lax
from jax.experimental import pallas as pl
from jax.experimental.pallas import tpu as pltpu
from jax.sharding import PartitionSpec as P


D = 8192
LF = 8192
TAPS = 7
HALO = 8
EDGE = 8
LANES = 128
SUMS = 24
ON_CHIP_BYTES = 9 * 2**18
F32 = jnp.float32
BF16 = jnp.bfloat16


def add(a, b):
    if a is None:
        return b
    if b is None:
        return a
    return a + b


def neg(a):
    return None if a is None else -a


def sub(a, b):
    if b is None:
        return a
    if a is None:
        return -b
    return a - b


def scaled(a, c):
    if a is None or abs(c) < 1e-12:
        return None
    if abs(c - 1.0) < 1e-12:
        return a
    if abs(c + 1.0) < 1e-12:
        return -a
    return a * c


def cadd(a, b):
    return (add(a[0], b[0]), add(a[1], b[1]))


def csub(a, b):
    return (sub(a[0], b[0]), sub(a[1], b[1]))


def times_i(a, sign):
    return (neg(a[1]), a[0]) if sign > 0 else (a[1], neg(a[0]))


def cmul(a, angle, gain=1.0):
    c = math.cos(angle)
    s = math.sin(angle)
    re, im = a
    if abs(abs(c) - abs(s)) < 1e-12 and re is not None and im is not None:
        root = abs(c) * gain
        sc = 1.0 if c > 0 else -1.0
        ss = 1.0 if s > 0 else -1.0
        if sc * ss > 0:
            return ((re - im) * (root * sc), (re + im) * (root * sc))
        return ((re + im) * (root * sc), (im - re) * (root * sc))
    c = c * gain
    s = s * gain
    return (sub(scaled(re, c), scaled(im, s)), add(scaled(im, c), scaled(re, s)))


def complex_dft(xs, sign):
    n = len(xs)
    if n == 1:
        return list(xs)
    half = n // 2
    sums = [cadd(xs[i], xs[i + half]) for i in range(half)]
    difs = [csub(xs[i], xs[i + half]) for i in range(half)]
    if n == 2:
        return [sums[0], difs[0]]
    quarter = n // 4
    out = [None] * n
    out[0::2] = complex_dft(sums, sign)
    turn = sign * 2.0 * math.pi / n
    first = []
    third = []
    for i in range(quarter):
        rot = times_i(difs[i + quarter], sign)
        first.append(cmul(cadd(difs[i], rot), turn * i))
        third.append(cmul(csub(difs[i], rot), turn * 3 * i))
    out[1::4] = complex_dft(first, sign)
    out[3::4] = complex_dft(third, sign)
    return out


def real_dft(xs):
    n = len(xs)
    if n == 1:
        return [(xs[0], None)]
    half = n // 2
    sums = [add(xs[i], xs[i + half]) for i in range(half)]
    difs = [sub(xs[i], xs[i + half]) for i in range(half)]
    if n == 2:
        return [(sums[0], None), (difs[0], None)]
    quarter = n // 4
    out = [None] * (half + 1)
    out[0::2] = real_dft(sums)
    turn = -2.0 * math.pi / n
    odd = [cmul((difs[i], neg(difs[i + quarter])), turn * i) for i in range(quarter)]
    for j, value in enumerate(complex_dft(odd, -1)):
        k = 4 * j + 1
        if k <= half:
            out[k] = value
        else:
            out[n - k] = (value[0], neg(value[1]))
    return out


def real_idft(spec, keep):
    n = 2 * (len(spec) - 1)
    if n == 2:
        both = [add(spec[0][0], spec[1][0]), sub(spec[0][0], spec[1][0])]
        return both[:keep]
    half = n // 2
    quarter = n // 4
    even = real_idft(spec[0::2], half)
    odd = []
    for j in range(quarter):
        k = 4 * j + 1
        odd.append(spec[k] if k <= half else (spec[n - k][0], neg(spec[n - k][1])))
    turn = 2.0 * math.pi / n
    rest = [cmul(v, turn * i, 2.0) for i, v in enumerate(complex_dft(odd, 1))]
    wave = [rest[i][0] for i in range(quarter)] + [neg(rest[i][1]) for i in range(quarter)]
    out = [add(even[i], wave[i]) for i in range(half)]
    if keep > half:
        out = out + [sub(even[i], wave[i]) for i in range(half)]
    return out[:keep]


def turn_tables(shards, rows):
    radix = 2 * shards
    count = radix * rows
    k1 = jnp.arange(shards + 1, dtype=jnp.int32)[:, None]
    r = jnp.arange(rows, dtype=jnp.int32)
    fine = 2.0 * math.pi / count * (k1 * r[None, :] % count).astype(F32)
    coarse = 2.0 * math.pi / rows * (r[:, None] * r[None, :] % rows).astype(F32)
    fine_c = jnp.cos(fine)
    fine_s = jnp.sin(fine)
    coarse_c = jnp.cos(coarse)[None]
    coarse_s = jnp.sin(coarse)[None]

    def pair(fc, fs, gain):
        cos = fc * coarse_c - fs * coarse_s
        sin = fs * coarse_c + fc * coarse_s
        return (jnp.concatenate([cos, sin], axis=1) * gain).astype(BF16)

    fwd = pair(fine_c[:, None, :], fine_s[:, None, :], 1.0)
    inv = pair(fine_c[:, :, None], fine_s[:, :, None], 1.0 / count)
    return fwd, inv


def over_tiles(rows, work):
    def step(i, carry):
        work(pl.multiple_of(i * 16, 16))
        return carry

    lax.fori_loop(0, rows // 16, step, 0)


def split_in(load, blocks, shards, rows, store):
    def work(r):
        rs = pl.ds(r, 16)
        xs = [load(s, rs).astype(F32) for s in range(blocks)]
        xs = xs + [None] * (2 * shards - blocks)
        for k, (re, im) in enumerate(real_dft(xs)):
            if im is None:
                im = jnp.zeros(re.shape, F32)
            store(k, rs, re.astype(BF16), im.astype(BF16))

    over_tiles(rows, work)


def load_spec(load, shards):
    spec = []
    for k in range(shards + 1):
        re, im = load(k)
        spec.append((re, None if k == 0 or k == shards else im))
    return spec


def dot(a, b):
    return jnp.dot(a, b, preferred_element_type=F32)


def backward(table, z_re, z_im, rows, step):
    chans = z_re.shape[1]
    z_re = z_re.astype(BF16)
    z_im = z_im.astype(BF16)
    if step == chans:
        p = dot(table, jnp.concatenate([z_re, z_im], axis=1))
        return p[:rows, :step] - p[rows:, step:], p[rows:, :step] + p[:rows, step:]
    p = dot(table, z_re)
    q = dot(table, z_im)
    return p[:rows] - q[rows:], p[rows:] + q[:rows]


def whole(shape):
    zeros = (0,) * len(shape)
    return pl.BlockSpec(shape, lambda *_: zeros, pipeline_mode=pl.Buffered(1))


def per_step(shape):
    zeros = (0,) * (len(shape) - 1)
    return pl.BlockSpec(shape, lambda i: (i,) + zeros)


def in_smem():
    return pl.BlockSpec(memory_space=pltpu.SMEM)


def resident():
    return pl.BlockSpec(memory_space=pltpu.VMEM)


def untouched():
    return pl.BlockSpec(memory_space=pl.ANY)


def raw_path(both, fwd, inv, where, packed, low_before, part, parts, tap_rows, live, fold):
    shards, _, rows, chans = both.shape
    steps = shards + 1
    step = max(chans, LANES)
    per_shard = tap_rows // rows
    blocks = live * per_shard

    def kernel(*refs):
        refs = list(refs)
        x_ref, fwd_ref, inv_ref = refs[:3]
        del refs[:3]
        if fold:
            flag_ref, h_ref = refs[:2]
            del refs[:2]
        if part:
            del refs[:1]
        spec_ref, low_ref, sq_ref = refs[:3]
        del refs[:3]
        if fold:
            send_ref = refs.pop(0)
        a_ref, y_ref = refs
        k = pl.program_id(0)
        mine = flag_ref[0, 1] if fold else 0

        @pl.when(k == 0)
        def _():
            for i in range(2):

                def store(at, rs, re, im, i=i):
                    a_ref[at, 0, rs, pl.ds(i * step, chans)] = re
                    a_ref[at, 1, rs, pl.ds(i * step, chans)] = im

                split_in(lambda s, rs, i=i: x_ref[s, i, rs, :], shards, shards, rows, store)

        p = dot(fwd_ref[0], a_ref[k, 0])
        q = dot(fwd_ref[0], a_ref[k, 1])
        re = p[:rows] + q[rows:]
        im = q[:rows] - p[rows:]
        spec_ref[0, 0] = re
        spec_ref[0, 1] = im
        g_re = re[:, :chans]
        g_im = im[:, :chans]
        m_re = re[:, step : step + chans]
        m_im = im[:, step : step + chans]
        y_re, y_im = backward(inv_ref[0], g_re * m_re + g_im * m_im, g_re * m_im - g_im * m_re, rows, step)
        y_ref[k, 0] = y_re
        y_ref[k, 1] = y_im

        @pl.when(k == steps - 1)
        def _():
            sq_ref[...] = jnp.zeros(sq_ref.shape, F32)

            def work(r):
                rs = pl.ds(r, 16)
                out = real_idft(load_spec(lambda at: (y_ref[at, 0, rs, :], y_ref[at, 1, rs, :]), shards), shards)
                square = None
                for s in range(blocks):
                    at = (s // per_shard) ^ mine
                    low_ref[at, 0, pl.ds((s % per_shard) * rows + r, 16), :] = out[s].astype(BF16)
                    square = add(square, out[s] * out[s])
                sq_ref[...] += square[:8] + square[8:]

            over_tiles(rows, work)
            if fold:

                @pl.when(flag_ref[0, 0] == 1)
                def _():
                    for s in range(shards):
                        send_ref[s] = h_ref[s]

                @pl.when(flag_ref[0, 0] == 0)
                def _():
                    for s in range(shards):
                        if s < live:
                            send_ref[s] = low_ref[s ^ mine, 0]
                        else:
                            send_ref[s] = jnp.zeros((tap_rows, chans), BF16)

    ins = [both, fwd, inv]
    in_specs = [
        resident(),
        per_step((1, 2 * rows, rows)),
        per_step((1, 2 * rows, rows)),
    ]
    if fold:
        ins += [where, packed]
        in_specs += [in_smem(), whole(packed.shape)]
    aliases = {}
    if part:
        aliases = {len(ins): 1}
        ins.append(low_before)
        in_specs.append(untouched())
    out_specs = [
        per_step((1, 2, rows, 2 * step)),
        pl.BlockSpec((live, 1, tap_rows, chans), lambda i: (0, part, 0, 0), pipeline_mode=pl.Buffered(1)),
        whole((8, chans)),
    ]
    out_shape = [
        jax.ShapeDtypeStruct((steps, 2, rows, 2 * step), F32),
        jax.ShapeDtypeStruct((live, parts, tap_rows, chans), BF16),
        jax.ShapeDtypeStruct((8, chans), F32),
    ]
    if fold:
        out_specs.append(whole(packed.shape))
        out_shape.append(jax.ShapeDtypeStruct(packed.shape, BF16))
    return pl.pallas_call(
        kernel,
        grid=(steps,),
        in_specs=in_specs,
        out_specs=out_specs,
        out_shape=out_shape,
        scratch_shapes=[
            pltpu.VMEM((steps, 2, rows, 2 * step), BF16),
            pltpu.VMEM((steps, 2, rows, chans), F32),
        ],
        input_output_aliases=aliases,
        cost_estimate=pl.CostEstimate(flops=20 * 10**9, transcendentals=0, bytes_accessed=25 * 10**6),
        name="raw_path",
    )(*ins)


def conv_path(both, taps, spec, skip, fwd, inv):
    shards, _, rows, chans = both.shape
    steps = shards + 1
    step = max(chans, LANES)
    blocks = min(taps.shape[0], shards)

    def kernel(x_ref, h_ref, spec_ref, skip_ref, fwd_ref, inv_ref, out_ref, a_ref, y_ref):
        k = pl.program_id(0)

        @pl.when(k == 0)
        def _():
            def store(at, rs, re, im):
                a_ref[at, rs, pl.ds(0, chans)] = re
                a_ref[at, rs, pl.ds(step, chans)] = im

            split_in(lambda s, rs: h_ref[s, rs, :], blocks, shards, rows, store)

        p = dot(fwd_ref[0], a_ref[k])
        h_re = p[:rows, :chans] + p[rows:, step : step + chans]
        h_im = p[:rows, step : step + chans] - p[rows:, :chans]
        g_re = spec_ref[0, 0, :, pl.ds(0, chans)]
        g_im = spec_ref[0, 1, :, pl.ds(0, chans)]
        m_re = spec_ref[0, 0, :, pl.ds(step, chans)]
        m_im = spec_ref[0, 1, :, pl.ds(step, chans)]
        y_re, y_im = backward(inv_ref[0], g_re * h_re - g_im * h_im, g_re * h_im + g_im * h_re, rows, step)
        y_ref[k, 0] = y_re
        y_ref[k, 1] = y_im
        y_re, y_im = backward(inv_ref[0], h_re * m_re + h_im * m_im, h_re * m_im - h_im * m_re, rows, step)
        y_ref[k, 2] = y_re
        y_ref[k, 3] = y_im

        @pl.when(k == steps - 1)
        def _():
            gain = skip_ref[...]
            for i in range(2):

                def work(r, i=i):
                    rs = pl.ds(r, 16)
                    spectrum = load_spec(lambda at: (y_ref[at, 2 * i, rs, :], y_ref[at, 2 * i + 1, rs, :]), shards)
                    out = real_idft(spectrum, shards)
                    out = [(out[s] + gain * x_ref[s, i, rs, :].astype(F32)).astype(BF16) for s in range(shards)]
                    for s in range(shards):
                        out_ref[s, i, rs, :] = out[s]

                    @pl.when(r == 0)
                    def _():
                        for s in range(shards - 1):
                            out_ref[s, i, pl.ds(rows, EDGE), :] = out[s + 1][:EDGE]
                        out_ref[shards - 1, i, pl.ds(rows, EDGE), :] = jnp.zeros((EDGE, chans), BF16)

                over_tiles(rows, work)

    out_block = (shards, 2, rows + EDGE, chans)
    return pl.pallas_call(
        kernel,
        grid=(steps,),
        in_specs=[
            resident(),
            resident(),
            per_step((1, 2, rows, 2 * step)),
            whole((1, chans)),
            per_step((1, 2 * rows, rows)),
            per_step((1, 2 * rows, rows)),
        ],
        out_specs=whole(out_block),
        out_shape=jax.ShapeDtypeStruct(out_block, BF16),
        scratch_shapes=[
            pltpu.VMEM((steps, rows, 2 * step), BF16),
            pltpu.VMEM((steps, 4, rows, chans), F32),
        ],
        cost_estimate=pl.CostEstimate(flops=20 * 10**9, transcendentals=0, bytes_accessed=25 * 10**6),
        name="conv_path",
    )(both, taps, spec, skip, fwd, inv)


def plan_lanes(width, chans):
    block = max(chans, LANES)
    while block < 512 and width % (2 * block) == 0:
        block *= 2
    return block


def put(ref, lead, rs, c, value):
    chans = ref.shape[-1]
    width = value.shape[1]
    if chans >= width:
        ref[(c // chans,) + lead + (rs, pl.ds(c % chans, width))] = value
        return
    for i in range(width // chans):
        ref[(c // chans + i,) + lead + (rs, slice(None))] = value[:, i * chans : (i + 1) * chans]


def take(ref, lead, rs, c, width, base=0):
    chans = ref.shape[-1]
    if chans >= width:
        return ref[(base + c // chans,) + lead + (rs, pl.ds(c % chans, width))].astype(F32)
    first = base + c // chans
    return jnp.concatenate(
        [ref[(first + i,) + lead + (rs, slice(None))].astype(F32) for i in range(width // chans)], axis=1
    )


def pack_taps(long_filter, shards, part, parts):
    rows, width = long_filter.shape
    width = width // parts
    chans = width // shards
    block = plan_lanes(width, chans)
    count = width // block
    groups = block // chans

    def kernel(x_ref, o_ref):
        for c in range(0, block, LANES):
            put(o_ref, (), pl.ds(0, rows), c, x_ref[:, pl.ds(c, LANES)].astype(BF16))

    return pl.pallas_call(
        kernel,
        grid=(count,),
        in_specs=[pl.BlockSpec((rows, block), lambda i: (0, part * count + i))],
        out_specs=pl.BlockSpec((groups, rows, chans), lambda i: (i, 0, 0)),
        out_shape=jax.ShapeDtypeStruct((shards, rows, chans), BF16),
        cost_estimate=pl.CostEstimate(flops=10**6, transcendentals=0, bytes_accessed=6 * 10**6),
        name="pack_taps",
    )(long_filter)


def scale_taps(clip, where, lows, shared, shards, live):
    parts, rows, chans = lows[0].shape[-3:]
    width = shards * chans
    block = plan_lanes(width, chans)
    while (live * chans) % block:
        block //= 2
    count = width // block
    groups = block // chans
    split = live // groups
    listed = len(lows) > 1

    def kernel(*refs):
        c_ref, at_ref = refs[:2]
        low_refs = refs[2 : 2 + len(lows)]
        o_ref = refs[-1]
        q = pl.program_id(0)
        i = pl.program_id(1)
        gain = c_ref[0, 0]

        @pl.when(i < split)
        def _():
            if not listed:
                for c in range(0, block, LANES):
                    o_ref[:, pl.ds(c, LANES)] = take(low_refs[0], (0,), pl.ds(0, rows), c, LANES) * gain
                return
            for j in range(groups):
                source = (i * groups + j) ^ at_ref[0, 1]
                for d, x_ref in enumerate(low_refs):

                    @pl.when(source == d)
                    def _(j=j, x_ref=x_ref):
                        o_ref[:, pl.ds(j * chans, chans)] = x_ref[q].astype(F32) * gain

        for part, x_ref in enumerate(refs[2 + len(lows) : -1]):

            @pl.when(jnp.logical_and(i >= split, q == part))
            def _(x_ref=x_ref):
                for c in range(0, block, LANES):
                    o_ref[:, pl.ds(c, LANES)] = take(x_ref, (), pl.ds(0, rows), c, LANES) * gain

    def shared_map(part):
        def index(q, i):
            upper = jnp.maximum(i, split)
            held = split if part else count - 1
            return (jnp.where(q == part, upper, held), 0, 0)

        return index

    if listed:
        lows = [on_chip(x) for x in lows]
        low_specs = [resident() for _ in lows]
    else:
        low_specs = [pl.BlockSpec((groups, 1, rows, chans), lambda q, i: (jnp.minimum(i, split - 1), q, 0, 0))]
    return pl.pallas_call(
        kernel,
        grid=(parts, count),
        in_specs=[in_smem(), in_smem()]
        + low_specs
        + [pl.BlockSpec((groups, rows, chans), shared_map(p)) for p in range(len(shared))],
        out_specs=pl.BlockSpec((rows, block), lambda q, i: (0, q * count + i)),
        out_shape=jax.ShapeDtypeStruct((rows, parts * width), F32),
        name="scale_taps",
    )(clip, where, *lows, *shared)


def short_rows(ext_ref, w_ref, i, cs, r, rows):
    total = w_ref[i, 0:1, cs] * ext_ref[i, pl.ds(HALO + r, rows), :]
    for j in range(1, TAPS):
        total = total + w_ref[i, j : j + 1, cs] * ext_ref[i, pl.ds(HALO + r - j, rows), :]
    return total


def gates(streams, before, grad_out, short_filter, shards, part, parts):
    _, rows, width = streams.shape
    width = width // parts
    chans = width // shards
    block = plan_lanes(width, chans)
    count = width // block
    groups = block // chans
    chunk = math.gcd(rows, 64)

    def kernel(x_ref, b_ref, go_ref, w_ref, o_ref, ext_ref):
        for c in range(0, block, LANES):
            cs = pl.ds(c, LANES)
            for i in range(3):
                ext_ref[i, pl.ds(0, HALO), :] = b_ref[i, :, cs].astype(F32)
                ext_ref[i, pl.ds(HALO, rows), :] = x_ref[i, :, cs].astype(F32)
            for r in range(0, rows, chunk):
                rs = pl.ds(r, chunk)
                gated = short_rows(ext_ref, w_ref, 0, cs, r, chunk) * short_rows(ext_ref, w_ref, 2, cs, r, chunk)
                mix = go_ref[rs, cs].astype(F32) * short_rows(ext_ref, w_ref, 1, cs, r, chunk)
                put(o_ref, (0,), rs, c, gated.astype(BF16))
                put(o_ref, (1,), rs, c, mix.astype(BF16))

    return pl.pallas_call(
        kernel,
        grid=(count,),
        in_specs=[
            pl.BlockSpec((3, rows, block), lambda i: (0, 0, part * count + i)),
            pl.BlockSpec((3, HALO, block), lambda i: (0, 0, part * count + i)),
            pl.BlockSpec((rows, block), lambda i: (0, part * count + i)),
            pl.BlockSpec((3, TAPS, block), lambda i: (0, 0, part * count + i)),
        ],
        out_specs=pl.BlockSpec((groups, 2, rows, chans), lambda i: (i, 0, 0, 0)),
        out_shape=jax.ShapeDtypeStruct((shards, 2, rows, chans), BF16),
        scratch_shapes=[pltpu.VMEM((3, rows + HALO, LANES), F32)],
        cost_estimate=pl.CostEstimate(flops=60 * 10**6, transcendentals=0, bytes_accessed=7 * 10**6),
        name="gates",
    )(streams, before, grad_out, short_filter)


def fill_ext(ext_ref, x_ref, b_ref, n_ref, cs, rows):
    for i in range(3):
        ext_ref[i, pl.ds(0, HALO), :] = b_ref[i, :, cs].astype(F32)
        ext_ref[i, pl.ds(HALO, rows), :] = x_ref[i, :, cs].astype(F32)
        if n_ref is not None:
            ext_ref[i, pl.ds(HALO + rows, HALO), :] = n_ref[i, :, cs].astype(F32)


def short_sums(streams, before, grad_out, short_filter, back, earlier, shards, part, parts):
    _, rows, full = streams.shape
    width = full // parts
    chans = width // shards
    block = plan_lanes(width, chans)
    count = width // block
    groups = block // chans
    chunk = math.gcd(rows, 64)

    def kernel(x_ref, b_ref, go_ref, w_ref, y_ref, *refs):
        st_ref, ext_ref, pre_ref = refs[-3:]
        base = pl.program_id(0) * groups
        for c in range(0, block, LANES):
            cs = pl.ds(c, LANES)
            fill_ext(ext_ref, x_ref, b_ref, None, cs, rows)
            bias = jnp.zeros((8, LANES), F32)
            for r in range(0, rows, chunk):
                rs = pl.ds(r, chunk)
                gout = go_ref[rs, cs].astype(F32)
                upper = take(y_ref, (1,), rs, c, LANES, base)
                x1s = short_rows(ext_ref, w_ref, 0, cs, r, chunk)
                vs = short_rows(ext_ref, w_ref, 2, cs, r, chunk)
                pre_ref[0, rs, :] = upper * vs
                pre_ref[2, rs, :] = upper * x1s
                pre_ref[1, rs, :] = gout * take(y_ref, (0,), rs, c, LANES, base)
                gated = (x1s * vs).astype(BF16).astype(F32)
                x2s = short_rows(ext_ref, w_ref, 1, cs, r, chunk)
                term = gated * (gout * x2s).astype(BF16).astype(F32)
                bias = bias + jnp.sum(term.reshape(chunk // 8, 8, LANES), axis=0)
            lines = []
            for i in range(3):
                sums = [jnp.zeros((8, LANES), F32) for _ in range(TAPS)]
                for r in range(0, rows, chunk):
                    own = pre_ref[i, pl.ds(r, chunk), :]
                    for j in range(TAPS):
                        term = own * ext_ref[i, pl.ds(HALO + r - j, chunk), :]
                        sums[j] = sums[j] + jnp.sum(term.reshape(chunk // 8, 8, LANES), axis=0)
                lines += [jnp.sum(v, axis=0, keepdims=True) for v in sums]
            lines.append(jnp.sum(bias, axis=0, keepdims=True))
            lines.append(jnp.zeros((SUMS - len(lines), LANES), F32))
            put(st_ref, (0,), pl.ds(0, SUMS), c, jnp.concatenate(lines, axis=0))

    at = lambda i: part * count + i
    ins = [streams, before, grad_out, short_filter, back]
    return pl.pallas_call(
        kernel,
        grid=(count,),
        in_specs=[
            pl.BlockSpec((3, rows, block), lambda i: (0, 0, at(i))),
            pl.BlockSpec((3, HALO, block), lambda i: (0, 0, at(i))),
            pl.BlockSpec((rows, block), lambda i: (0, at(i))),
            pl.BlockSpec((3, TAPS, block), lambda i: (0, 0, at(i))),
            resident(),
        ]
        + [untouched() for _ in earlier],
        out_specs=pl.BlockSpec((groups, 1, SUMS, chans), lambda i: (i, part, 0, 0)),
        out_shape=jax.ShapeDtypeStruct((shards, parts, SUMS, chans), F32),
        scratch_shapes=[
            pltpu.VMEM((3, rows + HALO, LANES), F32),
            pltpu.VMEM((3, rows, LANES), F32),
        ],
        input_output_aliases={len(ins): 0} if earlier else {},
        cost_estimate=pl.CostEstimate(flops=150 * 10**6, transcendentals=0, bytes_accessed=8 * 10**6),
        name="short_sums",
    )(*ins, *earlier)


def finish(streams, before, after, grad_out, short_filter, back, earlier, shards, part, parts):
    _, rows, full = streams.shape
    width = full // parts
    chans = width // shards
    block = plan_lanes(width, chans)
    count = width // block
    groups = block // chans
    chunk = math.gcd(rows, 64)

    def kernel(x_ref, b_ref, n_ref, go_ref, w_ref, y_ref, *refs):
        o_ref, gs_ref, ext_ref, pre_ref = refs[-4:]
        base = pl.program_id(0) * groups
        for c in range(0, block, LANES):
            cs = pl.ds(c, LANES)
            fill_ext(ext_ref, x_ref, b_ref, n_ref, cs, rows)
            for r in range(0, rows, chunk):
                rs = pl.ds(r, chunk)
                mixed = take(y_ref, (0,), rs, c, LANES, base)
                upper = take(y_ref, (1,), rs, c, LANES, base)
                pre_ref[0, rs, :] = upper * short_rows(ext_ref, w_ref, 2, cs, r, chunk)
                pre_ref[2, rs, :] = upper * short_rows(ext_ref, w_ref, 0, cs, r, chunk)
                pre_ref[1, rs, :] = go_ref[rs, cs].astype(F32) * mixed
                o_ref[rs, cs] = (short_rows(ext_ref, w_ref, 1, cs, r, chunk) * mixed).astype(BF16)
            mixed = take(y_ref, (0,), pl.ds(rows, EDGE), c, LANES, base)[:HALO]
            upper = take(y_ref, (1,), pl.ds(rows, EDGE), c, LANES, base)[:HALO]
            pre_ref[0, pl.ds(rows, HALO), :] = upper * short_rows(ext_ref, w_ref, 2, cs, rows, HALO)
            pre_ref[2, pl.ds(rows, HALO), :] = upper * short_rows(ext_ref, w_ref, 0, cs, rows, HALO)
            pre_ref[1, pl.ds(rows, HALO), :] = n_ref[3, :, cs].astype(F32) * mixed
            for i in range(3):
                for r in range(0, rows, chunk):
                    total = w_ref[i, 0:1, cs] * pre_ref[i, pl.ds(r, chunk), :]
                    for j in range(1, TAPS):
                        total = total + w_ref[i, j : j + 1, cs] * pre_ref[i, pl.ds(r + j, chunk), :]
                    gs_ref[i, pl.ds(r, chunk), cs] = total.astype(BF16)

    at = lambda i: part * count + i
    ins = [streams, before, after, grad_out, short_filter, back]
    return pl.pallas_call(
        kernel,
        grid=(count,),
        in_specs=[
            pl.BlockSpec((3, rows, block), lambda i: (0, 0, at(i))),
            pl.BlockSpec((3, HALO, block), lambda i: (0, 0, at(i))),
            pl.BlockSpec((4, HALO, block), lambda i: (0, 0, at(i))),
            pl.BlockSpec((rows, block), lambda i: (0, at(i))),
            pl.BlockSpec((3, TAPS, block), lambda i: (0, 0, at(i))),
            resident(),
        ]
        + [untouched() for _ in earlier],
        out_specs=[
            pl.BlockSpec((rows, block), lambda i: (0, at(i))),
            pl.BlockSpec((3, rows, block), lambda i: (0, 0, at(i))),
        ],
        out_shape=[
            jax.ShapeDtypeStruct((rows, full), BF16),
            jax.ShapeDtypeStruct((3, rows, full), BF16),
        ],
        scratch_shapes=[
            pltpu.VMEM((3, rows + 2 * HALO, LANES), F32),
            pltpu.VMEM((3, rows + HALO, LANES), F32),
        ],
        input_output_aliases={len(ins) + i: i for i in range(len(earlier))},
        cost_estimate=pl.CostEstimate(flops=150 * 10**6, transcendentals=0, bytes_accessed=12 * 10**6),
        name="finish",
    )(*ins, *earlier)


def shift(block, axis, distance):
    devices = range(lax.axis_size(axis))
    route = [(i - distance, i) for i in devices if i - distance in devices]
    return lax.ppermute(block, axis, route)


def exchange(blocks, groups=None):
    return lax.all_to_all(blocks, "seq", split_axis=0, concat_axis=0, axis_index_groups=groups, tiled=True)


def on_chip(value):
    lanes = -(-value.shape[-1] // LANES) * LANES
    if math.prod(value.shape[:-1]) * lanes * value.dtype.itemsize > ON_CHIP_BYTES:
        return value
    return pltpu.with_memory_space_constraint(value, pltpu.VMEM)


def following(value, earlier):
    return lax.optimization_barrier((value, earlier))[0]


def operator(streams, grad_out, long_filter, short_filter, skip_gain):
    shards = lax.axis_size("seq")
    rows = streams.shape[1]
    width = streams.shape[2]
    parts = 2 if width % (2 * shards * LANES) == 0 else 1
    span = width // parts
    chans = span // shards
    tap_rows = long_filter.shape[0]
    live = min(shards, shards * rows // tap_rows)
    fold = 2 * live <= shards
    mine = lax.axis_index("seq")
    is_low = mine < live
    where = jnp.stack([is_low.astype(jnp.int32), mine % live]).reshape(1, 2)
    fwd, inv = turn_tables(shards, rows)
    before = shift(streams[:, rows - HALO :], "seq", 1)
    after = shift(jnp.concatenate([streams[:, :HALO], grad_out[None, :HALO]], axis=0), "seq", -1)
    skips = [lax.dynamic_slice_in_dim(skip_gain, p * span + mine * chans, chans)[None] for p in range(parts)]

    both = []
    packed = []
    for p in range(parts):
        sent = gates(streams, before, grad_out, short_filter, shards, p, parts)
        both.append(on_chip(exchange(sent)))
    for p in range(parts):
        packed.append(pack_taps(long_filter, shards, p, parts))
    spec = []
    shared = []
    squares = 0.0
    low = None
    for p in range(parts):
        out = raw_path(both[p], fwd, inv, where, packed[p], low, p, parts, tap_rows, live, fold)
        spec.append(out[0])
        low = out[1]
        squares = squares + jnp.sum(out[2])
        shared.append(exchange(out[3] if fold else packed[p]))
    back = []
    for p in range(parts):
        taps = shared[p].reshape(shards * tap_rows // rows, rows, chans)
        sent = conv_path(both[p], taps, spec[p], skips[p], fwd, inv)
        back.append(on_chip(exchange(sent)))
        sent_last = sent
    done = []
    sums = []
    lows = []

    def send_low(first, last, cue):
        ready = following(low, cue)
        if first == 0:
            lows.append(ready[0])
        for d in range(max(first, 1), last):
            lows.append(lax.ppermute(ready[d], "seq", [(i, i ^ d) for i in range(live)]))

    if fold:
        send_low(0, live // 2 + 1, sent_last)
    for p in range(parts):
        sums = [short_sums(streams, before, grad_out, short_filter, back[p], sums, shards, p, parts)]
        if p == 0 and fold:
            send_low(live // 2 + 1, live, back[0])
        done = finish(streams, before, after, grad_out, short_filter, back[p], done, shards, p, parts)
    output, grad_streams = done
    sums = sums[0]
    if not fold:
        lows.append(exchange(following(low, back[-1])))
        sums = following(sums, lows[0])
    mine_sums = jnp.sum(exchange(sums), axis=0)
    local_sq = squares + jnp.sum(mine_sums * mine_sums)
    upper_sq = lax.reduce_precision(local_sq, 8, 7)
    line = lax.broadcasted_iota(jnp.int32, mine_sums.shape, 1)
    mine_sums = jnp.where(line == SUMS - 2, upper_sq, mine_sums)
    mine_sums = jnp.where(line == SUMS - 1, local_sq - upper_sq, mine_sums).astype(BF16)
    small = exchange(jnp.broadcast_to(mine_sums[None], (shards,) + mine_sums.shape)).astype(F32)
    sq_total = lax.psum(jnp.sum(small[:, 0, SUMS - 2 :, 0]), "chan")
    param_count = LF * D + (3 * TAPS + 1) * D
    clip = 1.0 / jnp.sqrt(sq_total / param_count + 1e-06)
    kept = jnp.where(is_low, clip, 0.0).reshape(1, 1)
    filter_grad = scale_taps(kept, where, lows, shared if fold else [], shards, live)
    small = small.transpose(2, 1, 0, 3).reshape(SUMS, width) * clip
    return (
        output,
        grad_streams,
        filter_grad,
        small[: 3 * TAPS].reshape(3, TAPS, width),
        small[3 * TAPS],
    )


def solution(mesh):
    placed = (
        P(None, "seq", "chan"),
        P("seq", "chan"),
        P("seq", "chan"),
        P(None, None, "chan"),
        P("chan"),
    )
    return jax.shard_map(
        operator,
        mesh=mesh,
        in_specs=placed,
        out_specs=(
            P("seq", "chan"),
            P(None, "seq", "chan"),
            P("seq", "chan"),
            P(None, None, "chan"),
            P("chan"),
        ),
        check_vma=False,
    )
```

```python
import math

import jax
import jax.numpy as jnp
from jax import lax
from jax.experimental import pallas as pl
from jax.experimental.pallas import tpu as pltpu
from jax.sharding import PartitionSpec as P


D = 8192
LF = 8192
TAPS = 7
HALO = 8
EDGE = 8
LANES = 128
SUMS = 24
ON_CHIP_BYTES = 9 * 2**18
F32 = jnp.float32
BF16 = jnp.bfloat16


def add(a, b):
    if a is None:
        return b
    if b is None:
        return a
    return a + b


def neg(a):
    return None if a is None else -a


def sub(a, b):
    if b is None:
        return a
    if a is None:
        return -b
    return a - b


def scaled(a, c):
    if a is None or abs(c) < 1e-12:
        return None
    if abs(c - 1.0) < 1e-12:
        return a
    if abs(c + 1.0) < 1e-12:
        return -a
    return a * c


def cadd(a, b):
    return (add(a[0], b[0]), add(a[1], b[1]))


def csub(a, b):
    return (sub(a[0], b[0]), sub(a[1], b[1]))


def times_i(a, sign):
    return (neg(a[1]), a[0]) if sign > 0 else (a[1], neg(a[0]))


def cmul(a, angle, gain=1.0):
    c = math.cos(angle)
    s = math.sin(angle)
    re, im = a
    if abs(abs(c) - abs(s)) < 1e-12 and re is not None and im is not None:
        root = abs(c) * gain
        sc = 1.0 if c > 0 else -1.0
        ss = 1.0 if s > 0 else -1.0
        if sc * ss > 0:
            return ((re - im) * (root * sc), (re + im) * (root * sc))
        return ((re + im) * (root * sc), (im - re) * (root * sc))
    c = c * gain
    s = s * gain
    return (sub(scaled(re, c), scaled(im, s)), add(scaled(im, c), scaled(re, s)))


def complex_dft(xs, sign):
    n = len(xs)
    if n == 1:
        return list(xs)
    half = n // 2
    sums = [cadd(xs[i], xs[i + half]) for i in range(half)]
    difs = [csub(xs[i], xs[i + half]) for i in range(half)]
    if n == 2:
        return [sums[0], difs[0]]
    quarter = n // 4
    out = [None] * n
    out[0::2] = complex_dft(sums, sign)
    turn = sign * 2.0 * math.pi / n
    first = []
    third = []
    for i in range(quarter):
        rot = times_i(difs[i + quarter], sign)
        first.append(cmul(cadd(difs[i], rot), turn * i))
        third.append(cmul(csub(difs[i], rot), turn * 3 * i))
    out[1::4] = complex_dft(first, sign)
    out[3::4] = complex_dft(third, sign)
    return out


def real_dft(xs):
    n = len(xs)
    if n == 1:
        return [(xs[0], None)]
    half = n // 2
    sums = [add(xs[i], xs[i + half]) for i in range(half)]
    difs = [sub(xs[i], xs[i + half]) for i in range(half)]
    if n == 2:
        return [(sums[0], None), (difs[0], None)]
    quarter = n // 4
    out = [None] * (half + 1)
    out[0::2] = real_dft(sums)
    turn = -2.0 * math.pi / n
    odd = [cmul((difs[i], neg(difs[i + quarter])), turn * i) for i in range(quarter)]
    for j, value in enumerate(complex_dft(odd, -1)):
        k = 4 * j + 1
        if k <= half:
            out[k] = value
        else:
            out[n - k] = (value[0], neg(value[1]))
    return out


def real_idft(spec, keep):
    n = 2 * (len(spec) - 1)
    if n == 2:
        both = [add(spec[0][0], spec[1][0]), sub(spec[0][0], spec[1][0])]
        return both[:keep]
    half = n // 2
    quarter = n // 4
    even = real_idft(spec[0::2], half)
    odd = []
    for j in range(quarter):
        k = 4 * j + 1
        odd.append(spec[k] if k <= half else (spec[n - k][0], neg(spec[n - k][1])))
    turn = 2.0 * math.pi / n
    rest = [cmul(v, turn * i, 2.0) for i, v in enumerate(complex_dft(odd, 1))]
    wave = [rest[i][0] for i in range(quarter)] + [neg(rest[i][1]) for i in range(quarter)]
    out = [add(even[i], wave[i]) for i in range(half)]
    if keep > half:
        out = out + [sub(even[i], wave[i]) for i in range(half)]
    return out[:keep]


def turn_tables(shards, rows):
    radix = 2 * shards
    count = radix * rows
    k1 = jnp.arange(shards + 1, dtype=jnp.int32)[:, None]
    r = jnp.arange(rows, dtype=jnp.int32)
    fine = 2.0 * math.pi / count * (k1 * r[None, :] % count).astype(F32)
    coarse = 2.0 * math.pi / rows * (r[:, None] * r[None, :] % rows).astype(F32)
    fine_c = jnp.cos(fine)
    fine_s = jnp.sin(fine)
    coarse_c = jnp.cos(coarse)[None]
    coarse_s = jnp.sin(coarse)[None]

    def pair(fc, fs, gain):
        cos = fc * coarse_c - fs * coarse_s
        sin = fs * coarse_c + fc * coarse_s
        return (jnp.concatenate([cos, sin], axis=1) * gain).astype(BF16)

    fwd = pair(fine_c[:, None, :], fine_s[:, None, :], 1.0)
    inv = pair(fine_c[:, :, None], fine_s[:, :, None], 1.0 / count)
    return fwd, inv


def over_tiles(rows, work):
    def step(i, carry):
        work(pl.multiple_of(i * 16, 16))
        return carry

    lax.fori_loop(0, rows // 16, step, 0)


def split_in(load, blocks, shards, rows, store):
    def work(r):
        rs = pl.ds(r, 16)
        xs = [load(s, rs).astype(F32) for s in range(blocks)]
        xs = xs + [None] * (2 * shards - blocks)
        for k, (re, im) in enumerate(real_dft(xs)):
            if im is None:
                im = jnp.zeros(re.shape, F32)
            store(k, rs, re.astype(BF16), im.astype(BF16))

    over_tiles(rows, work)


def load_spec(load, shards):
    spec = []
    for k in range(shards + 1):
        re, im = load(k)
        spec.append((re, None if k == 0 or k == shards else im))
    return spec


def dot(a, b):
    return jnp.dot(a, b, preferred_element_type=F32)


def backward(table, z_re, z_im, rows, step):
    chans = z_re.shape[1]
    z_re = z_re.astype(BF16)
    z_im = z_im.astype(BF16)
    if step == chans:
        p = dot(table, jnp.concatenate([z_re, z_im], axis=1))
        return p[:rows, :step] - p[rows:, step:], p[rows:, :step] + p[:rows, step:]
    p = dot(table, z_re)
    q = dot(table, z_im)
    return p[:rows] - q[rows:], p[rows:] + q[:rows]


def whole(shape):
    zeros = (0,) * len(shape)
    return pl.BlockSpec(shape, lambda *_: zeros, pipeline_mode=pl.Buffered(1))


def per_step(shape):
    zeros = (0,) * (len(shape) - 1)
    return pl.BlockSpec(shape, lambda i: (i,) + zeros)


def in_smem():
    return pl.BlockSpec(memory_space=pltpu.SMEM)


def resident():
    return pl.BlockSpec(memory_space=pltpu.VMEM)


def untouched():
    return pl.BlockSpec(memory_space=pl.ANY)


def raw_path(both, fwd, inv, where, packed, low_before, part, parts, tap_rows, live, fold):
    shards, _, rows, chans = both.shape
    steps = shards + 1
    step = max(chans, LANES)
    per_shard = tap_rows // rows
    blocks = live * per_shard

    def kernel(*refs):
        refs = list(refs)
        x_ref, fwd_ref, inv_ref = refs[:3]
        del refs[:3]
        if fold:
            flag_ref, h_ref = refs[:2]
            del refs[:2]
        if part:
            del refs[:1]
        spec_ref, low_ref, sq_ref = refs[:3]
        del refs[:3]
        if fold:
            send_ref = refs.pop(0)
        a_ref, y_ref = refs
        k = pl.program_id(0)
        mine = flag_ref[0, 1] if fold else 0

        @pl.when(k == 0)
        def _():
            for i in range(2):

                def store(at, rs, re, im, i=i):
                    a_ref[at, 0, rs, pl.ds(i * step, chans)] = re
                    a_ref[at, 1, rs, pl.ds(i * step, chans)] = im

                split_in(lambda s, rs, i=i: x_ref[s, i, rs, :], shards, shards, rows, store)

        p = dot(fwd_ref[0], a_ref[k, 0])
        q = dot(fwd_ref[0], a_ref[k, 1])
        re = p[:rows] + q[rows:]
        im = q[:rows] - p[rows:]
        spec_ref[0, 0] = re
        spec_ref[0, 1] = im
        g_re = re[:, :chans]
        g_im = im[:, :chans]
        m_re = re[:, step : step + chans]
        m_im = im[:, step : step + chans]
        y_re, y_im = backward(inv_ref[0], g_re * m_re + g_im * m_im, g_re * m_im - g_im * m_re, rows, step)
        y_ref[k, 0] = y_re
        y_ref[k, 1] = y_im

        @pl.when(k == steps - 1)
        def _():
            sq_ref[...] = jnp.zeros(sq_ref.shape, F32)

            def work(r):
                rs = pl.ds(r, 16)
                out = real_idft(load_spec(lambda at: (y_ref[at, 0, rs, :], y_ref[at, 1, rs, :]), shards), shards)
                square = None
                for s in range(blocks):
                    at = (s // per_shard) ^ mine
                    low_ref[at, 0, pl.ds((s % per_shard) * rows + r, 16), :] = out[s].astype(BF16)
                    square = add(square, out[s] * out[s])
                sq_ref[...] += square[:8] + square[8:]

            over_tiles(rows, work)
            if fold:

                @pl.when(flag_ref[0, 0] == 1)
                def _():
                    for s in range(shards):
                        send_ref[s] = h_ref[s]

                @pl.when(flag_ref[0, 0] == 0)
                def _():
                    for s in range(shards):
                        if s < live:
                            send_ref[s] = low_ref[s ^ mine, 0]
                        else:
                            send_ref[s] = jnp.zeros((tap_rows, chans), BF16)

    ins = [both, fwd, inv]
    in_specs = [
        resident(),
        per_step((1, 2 * rows, rows)),
        per_step((1, 2 * rows, rows)),
    ]
    if fold:
        ins += [where, packed]
        in_specs += [in_smem(), whole(packed.shape)]
    aliases = {}
    if part:
        aliases = {len(ins): 1}
        ins.append(low_before)
        in_specs.append(untouched())
    out_specs = [
        per_step((1, 2, rows, 2 * step)),
        pl.BlockSpec((live, 1, tap_rows, chans), lambda i: (0, part, 0, 0), pipeline_mode=pl.Buffered(1)),
        whole((8, chans)),
    ]
    out_shape = [
        jax.ShapeDtypeStruct((steps, 2, rows, 2 * step), F32),
        jax.ShapeDtypeStruct((live, parts, tap_rows, chans), BF16),
        jax.ShapeDtypeStruct((8, chans), F32),
    ]
    if fold:
        out_specs.append(whole(packed.shape))
        out_shape.append(jax.ShapeDtypeStruct(packed.shape, BF16))
    return pl.pallas_call(
        kernel,
        grid=(steps,),
        in_specs=in_specs,
        out_specs=out_specs,
        out_shape=out_shape,
        scratch_shapes=[
            pltpu.VMEM((steps, 2, rows, 2 * step), BF16),
            pltpu.VMEM((steps, 2, rows, chans), F32),
        ],
        input_output_aliases=aliases,
        cost_estimate=pl.CostEstimate(flops=20 * 10**9, transcendentals=0, bytes_accessed=25 * 10**6),
        name="raw_path",
    )(*ins)


def conv_path(both, taps, spec, skip, fwd, inv):
    shards, _, rows, chans = both.shape
    steps = shards + 1
    step = max(chans, LANES)
    blocks = min(taps.shape[0], shards)

    def kernel(x_ref, h_ref, spec_ref, skip_ref, fwd_ref, inv_ref, out_ref, a_ref, y_ref):
        k = pl.program_id(0)

        @pl.when(k == 0)
        def _():
            def store(at, rs, re, im):
                a_ref[at, rs, pl.ds(0, chans)] = re
                a_ref[at, rs, pl.ds(step, chans)] = im

            split_in(lambda s, rs: h_ref[s, rs, :], blocks, shards, rows, store)

        p = dot(fwd_ref[0], a_ref[k])
        h_re = p[:rows, :chans] + p[rows:, step : step + chans]
        h_im = p[:rows, step : step + chans] - p[rows:, :chans]
        g_re = spec_ref[0, 0, :, pl.ds(0, chans)]
        g_im = spec_ref[0, 1, :, pl.ds(0, chans)]
        m_re = spec_ref[0, 0, :, pl.ds(step, chans)]
        m_im = spec_ref[0, 1, :, pl.ds(step, chans)]
        y_re, y_im = backward(inv_ref[0], g_re * h_re - g_im * h_im, g_re * h_im + g_im * h_re, rows, step)
        y_ref[k, 0] = y_re
        y_ref[k, 1] = y_im
        y_re, y_im = backward(inv_ref[0], h_re * m_re + h_im * m_im, h_re * m_im - h_im * m_re, rows, step)
        y_ref[k, 2] = y_re
        y_ref[k, 3] = y_im

        @pl.when(k == steps - 1)
        def _():
            gain = skip_ref[...]
            for i in range(2):

                def work(r, i=i):
                    rs = pl.ds(r, 16)
                    spectrum = load_spec(lambda at: (y_ref[at, 2 * i, rs, :], y_ref[at, 2 * i + 1, rs, :]), shards)
                    out = real_idft(spectrum, shards)
                    out = [(out[s] + gain * x_ref[s, i, rs, :].astype(F32)).astype(BF16) for s in range(shards)]
                    for s in range(shards):
                        out_ref[s, i, rs, :] = out[s]

                    @pl.when(r == 0)
                    def _():
                        for s in range(shards - 1):
                            out_ref[s, i, pl.ds(rows, EDGE), :] = out[s + 1][:EDGE]
                        out_ref[shards - 1, i, pl.ds(rows, EDGE), :] = jnp.zeros((EDGE, chans), BF16)

                over_tiles(rows, work)

    out_block = (shards, 2, rows + EDGE, chans)
    return pl.pallas_call(
        kernel,
        grid=(steps,),
        in_specs=[
            resident(),
            resident(),
            per_step((1, 2, rows, 2 * step)),
            whole((1, chans)),
            per_step((1, 2 * rows, rows)),
            per_step((1, 2 * rows, rows)),
        ],
        out_specs=whole(out_block),
        out_shape=jax.ShapeDtypeStruct(out_block, BF16),
        scratch_shapes=[
            pltpu.VMEM((steps, rows, 2 * step), BF16),
            pltpu.VMEM((steps, 4, rows, chans), F32),
        ],
        cost_estimate=pl.CostEstimate(flops=20 * 10**9, transcendentals=0, bytes_accessed=25 * 10**6),
        name="conv_path",
    )(both, taps, spec, skip, fwd, inv)


def plan_lanes(width, chans):
    block = max(chans, LANES)
    while block < 512 and width % (2 * block) == 0:
        block *= 2
    return block


def put(ref, lead, rs, c, value):
    chans = ref.shape[-1]
    width = value.shape[1]
    if chans >= width:
        ref[(c // chans,) + lead + (rs, pl.ds(c % chans, width))] = value
        return
    for i in range(width // chans):
        ref[(c // chans + i,) + lead + (rs, slice(None))] = value[:, i * chans : (i + 1) * chans]


def take(ref, lead, rs, c, width, base=0):
    chans = ref.shape[-1]
    if chans >= width:
        return ref[(base + c // chans,) + lead + (rs, pl.ds(c % chans, width))].astype(F32)
    first = base + c // chans
    return jnp.concatenate(
        [ref[(first + i,) + lead + (rs, slice(None))].astype(F32) for i in range(width // chans)], axis=1
    )


def pack_taps(long_filter, shards, part, parts):
    rows, width = long_filter.shape
    width = width // parts
    chans = width // shards
    block = plan_lanes(width, chans)
    count = width // block
    groups = block // chans

    def kernel(x_ref, o_ref):
        for c in range(0, block, LANES):
            put(o_ref, (), pl.ds(0, rows), c, x_ref[:, pl.ds(c, LANES)].astype(BF16))

    return pl.pallas_call(
        kernel,
        grid=(count,),
        in_specs=[pl.BlockSpec((rows, block), lambda i: (0, part * count + i))],
        out_specs=pl.BlockSpec((groups, rows, chans), lambda i: (i, 0, 0)),
        out_shape=jax.ShapeDtypeStruct((shards, rows, chans), BF16),
        cost_estimate=pl.CostEstimate(flops=10**6, transcendentals=0, bytes_accessed=6 * 10**6),
        name="pack_taps",
    )(long_filter)


def scale_taps(small, where, lows, shared, shards, live, param_count):
    parts, rows, chans = lows[0].shape[-3:]
    width = shards * chans
    block = plan_lanes(width, chans)
    while (live * chans) % block:
        block //= 2
    count = width // block
    groups = block // chans
    split = live // groups
    listed = len(lows) > 1

    def kernel(*refs):
        small_ref, at_ref = refs[:2]
        low_refs = refs[2 : 2 + len(lows)]
        o_ref, short_ref, bias_ref = refs[-3:]
        q = pl.program_id(0)
        i = pl.program_id(1)
        total = jnp.zeros((SUMS, min(chans, LANES)), F32)
        for j in range(shards):
            total = total + small_ref[j, 0, :, pl.ds(0, min(chans, LANES))].astype(F32)
        total = total[SUMS - 2 : SUMS - 1, 0:1] + total[SUMS - 1 :, 0:1]
        clip = 1.0 / jnp.sqrt(jnp.broadcast_to(total, (1, LANES)) / param_count + 1e-06)
        gain = clip * at_ref[0, 0].astype(F32)
        for c in range(0, block, LANES):
            lines = take(small_ref, (q,), slice(None), c, LANES, i * groups) * clip
            for j in range(3):
                short_ref[j, :, pl.ds(c, LANES)] = lines[j * TAPS : (j + 1) * TAPS]
            bias_ref[:, pl.ds(c, LANES)] = lines[3 * TAPS : 3 * TAPS + 1]

        @pl.when(i < split)
        def _():
            if not listed:
                for c in range(0, block, LANES):
                    o_ref[:, pl.ds(c, LANES)] = take(low_refs[0], (0,), pl.ds(0, rows), c, LANES) * gain
                return
            for j in range(groups):
                source = (i * groups + j) ^ at_ref[0, 1]
                for d, x_ref in enumerate(low_refs):

                    @pl.when(source == d)
                    def _(j=j, x_ref=x_ref):
                        o_ref[:, pl.ds(j * chans, chans)] = x_ref[q].astype(F32) * jnp.concatenate([gain] * (chans // LANES), axis=1)

        for part, x_ref in enumerate(refs[2 + len(lows) : -3]):

            @pl.when(jnp.logical_and(i >= split, q == part))
            def _(x_ref=x_ref):
                for c in range(0, block, LANES):
                    o_ref[:, pl.ds(c, LANES)] = take(x_ref, (), pl.ds(0, rows), c, LANES) * gain

    def shared_map(part):
        def index(q, i):
            upper = jnp.maximum(i, split)
            held = split if part else count - 1
            return (jnp.where(q == part, upper, held), 0, 0)

        return index

    if listed:
        lows = [on_chip(x) for x in lows]
        low_specs = [resident() for _ in lows]
    else:
        low_specs = [pl.BlockSpec((groups, 1, rows, chans), lambda q, i: (jnp.minimum(i, split - 1), q, 0, 0))]
    return pl.pallas_call(
        kernel,
        grid=(parts, count),
        in_specs=[whole(small.shape), in_smem()]
        + low_specs
        + [pl.BlockSpec((groups, rows, chans), shared_map(p)) for p in range(len(shared))],
        out_specs=[
            pl.BlockSpec((rows, block), lambda q, i: (0, q * count + i)),
            pl.BlockSpec((3, TAPS, block), lambda q, i: (0, 0, q * count + i)),
            pl.BlockSpec((1, block), lambda q, i: (0, q * count + i)),
        ],
        out_shape=[
            jax.ShapeDtypeStruct((rows, parts * width), F32),
            jax.ShapeDtypeStruct((3, TAPS, parts * width), F32),
            jax.ShapeDtypeStruct((1, parts * width), F32),
        ],
        name="scale_taps",
    )(small, where, *lows, *shared)


def short_rows(ext_ref, w_ref, i, cs, r, rows):
    total = w_ref[i, 0:1, cs] * ext_ref[i, pl.ds(HALO + r, rows), :]
    for j in range(1, TAPS):
        total = total + w_ref[i, j : j + 1, cs] * ext_ref[i, pl.ds(HALO + r - j, rows), :]
    return total


def gates(streams, before, grad_out, short_filter, shards, part, parts, keep):
    _, rows, width = streams.shape
    width = width // parts
    chans = width // shards
    block = plan_lanes(width, chans)
    count = width // block
    groups = block // chans
    chunk = math.gcd(rows, 64)

    def kernel(x_ref, b_ref, go_ref, w_ref, o_ref, bias_ref, *refs):
        ext_ref = refs[-1]
        for c in range(0, block, LANES):
            cs = pl.ds(c, LANES)
            fill_ext(ext_ref, x_ref, b_ref, None, cs, rows)
            bias = jnp.zeros((8, LANES), F32)
            for r in range(0, rows, chunk):
                rs = pl.ds(r, chunk)
                x1s = short_rows(ext_ref, w_ref, 0, cs, r, chunk)
                vs = short_rows(ext_ref, w_ref, 2, cs, r, chunk)
                gated = (x1s * vs).astype(BF16)
                mix = go_ref[rs, cs].astype(F32) * short_rows(ext_ref, w_ref, 1, cs, r, chunk)
                mix = mix.astype(BF16)
                put(o_ref, (0,), rs, c, gated)
                put(o_ref, (1,), rs, c, mix)
                if keep:
                    refs[0][0, rs, cs] = x1s
                    refs[0][1, rs, cs] = vs
                term = gated.astype(F32) * mix.astype(F32)
                bias = bias + jnp.sum(term.reshape(chunk // 8, 8, LANES), axis=0)
            bias_ref[:, cs] = jnp.sum(bias, axis=0, keepdims=True)

    out_specs = [
        pl.BlockSpec((groups, 2, rows, chans), lambda i: (i, 0, 0, 0)),
        pl.BlockSpec((1, block), lambda i: (0, i)),
    ]
    out_shape = [
        jax.ShapeDtypeStruct((shards, 2, rows, chans), BF16),
        jax.ShapeDtypeStruct((1, width), F32),
    ]
    if keep:
        out_specs.append(pl.BlockSpec((2, rows, block), lambda i: (0, 0, i)))
        out_shape.append(jax.ShapeDtypeStruct((2, rows, width), F32))
    return pl.pallas_call(
        kernel,
        grid=(count,),
        in_specs=[
            pl.BlockSpec((3, rows, block), lambda i: (0, 0, part * count + i)),
            pl.BlockSpec((3, HALO, block), lambda i: (0, 0, part * count + i)),
            pl.BlockSpec((rows, block), lambda i: (0, part * count + i)),
            pl.BlockSpec((3, TAPS, block), lambda i: (0, 0, part * count + i)),
        ],
        out_specs=out_specs,
        out_shape=out_shape,
        scratch_shapes=[pltpu.VMEM((3, rows + HALO, LANES), F32)],
        cost_estimate=pl.CostEstimate(flops=60 * 10**6, transcendentals=0, bytes_accessed=7 * 10**6),
        name="gates",
    )(streams, before, grad_out, short_filter)


def fill_ext(ext_ref, x_ref, b_ref, n_ref, cs, rows):
    for i in range(3):
        ext_ref[i, pl.ds(0, HALO), :] = b_ref[i, :, cs].astype(F32)
        ext_ref[i, pl.ds(HALO, rows), :] = x_ref[i, :, cs].astype(F32)
        if n_ref is not None:
            ext_ref[i, pl.ds(HALO + rows, HALO), :] = n_ref[i, :, cs].astype(F32)


def short_sums(streams, before, grad_out, short_filter, back, bias, kept, earlier, shards, part, parts):
    _, rows, full = streams.shape
    width = full // parts
    chans = width // shards
    block = plan_lanes(width, chans)
    count = width // block
    groups = block // chans
    chunk = math.gcd(rows, 64)

    def kernel(x_ref, b_ref, go_ref, w_ref, y_ref, bias_ref, *refs):
        st_ref, ext_ref, pre_ref = refs[-3:]
        base = pl.program_id(0) * groups
        for c in range(0, block, LANES):
            cs = pl.ds(c, LANES)
            fill_ext(ext_ref, x_ref, b_ref, None, cs, rows)
            for r in range(0, rows, chunk):
                rs = pl.ds(r, chunk)
                upper = take(y_ref, (1,), rs, c, LANES, base)
                if kept is None:
                    x1s = short_rows(ext_ref, w_ref, 0, cs, r, chunk)
                    vs = short_rows(ext_ref, w_ref, 2, cs, r, chunk)
                else:
                    x1s = refs[0][0, rs, cs]
                    vs = refs[0][1, rs, cs]
                pre_ref[0, rs, :] = upper * vs
                pre_ref[2, rs, :] = upper * x1s
                pre_ref[1, rs, :] = go_ref[rs, cs].astype(F32) * take(y_ref, (0,), rs, c, LANES, base)
            lines = []
            for i in range(3):
                sums = [jnp.zeros((8, LANES), F32) for _ in range(TAPS)]
                for r in range(0, rows, chunk):
                    own = pre_ref[i, pl.ds(r, chunk), :]
                    for j in range(TAPS):
                        term = own * ext_ref[i, pl.ds(HALO + r - j, chunk), :]
                        sums[j] = sums[j] + jnp.sum(term.reshape(chunk // 8, 8, LANES), axis=0)
                lines += [jnp.sum(v, axis=0, keepdims=True) for v in sums]
            lines.append(bias_ref[:, cs])
            lines.append(jnp.zeros((SUMS - len(lines), LANES), F32))
            put(st_ref, (0,), pl.ds(0, SUMS), c, jnp.concatenate(lines, axis=0).astype(BF16))

    at = lambda i: part * count + i
    ins = [streams, before, grad_out, short_filter, back, bias]
    in_specs = [
        pl.BlockSpec((3, rows, block), lambda i: (0, 0, at(i))),
        pl.BlockSpec((3, HALO, block), lambda i: (0, 0, at(i))),
        pl.BlockSpec((rows, block), lambda i: (0, at(i))),
        pl.BlockSpec((3, TAPS, block), lambda i: (0, 0, at(i))),
        resident(),
        pl.BlockSpec((1, block), lambda i: (0, i)),
    ]
    if kept is not None:
        ins.append(kept)
        in_specs.append(pl.BlockSpec((2, rows, block), lambda i: (0, 0, i)))
    return pl.pallas_call(
        kernel,
        grid=(count,),
        in_specs=in_specs + [untouched() for _ in earlier],
        out_specs=pl.BlockSpec((groups, 1, SUMS, chans), lambda i: (i, part, 0, 0)),
        out_shape=jax.ShapeDtypeStruct((shards, parts, SUMS, chans), BF16),
        scratch_shapes=[
            pltpu.VMEM((3, rows + HALO, LANES), F32),
            pltpu.VMEM((3, rows, LANES), F32),
        ],
        input_output_aliases={len(ins): 0} if earlier else {},
        cost_estimate=pl.CostEstimate(flops=150 * 10**6, transcendentals=0, bytes_accessed=8 * 10**6),
        name="short_sums",
    )(*ins, *earlier)


def finish(streams, before, after, grad_out, short_filter, back, earlier, shards, part, parts):
    _, rows, full = streams.shape
    width = full // parts
    chans = width // shards
    block = plan_lanes(width, chans)
    count = width // block
    groups = block // chans
    chunk = math.gcd(rows, 64)

    def kernel(x_ref, b_ref, n_ref, go_ref, w_ref, y_ref, *refs):
        o_ref, gs_ref, ext_ref, pre_ref = refs[-4:]
        base = pl.program_id(0) * groups
        for c in range(0, block, LANES):
            cs = pl.ds(c, LANES)
            fill_ext(ext_ref, x_ref, b_ref, n_ref, cs, rows)
            for r in range(0, rows, chunk):
                rs = pl.ds(r, chunk)
                mixed = take(y_ref, (0,), rs, c, LANES, base)
                upper = take(y_ref, (1,), rs, c, LANES, base)
                pre_ref[0, rs, :] = upper * short_rows(ext_ref, w_ref, 2, cs, r, chunk)
                pre_ref[2, rs, :] = upper * short_rows(ext_ref, w_ref, 0, cs, r, chunk)
                pre_ref[1, rs, :] = go_ref[rs, cs].astype(F32) * mixed
                o_ref[rs, cs] = (short_rows(ext_ref, w_ref, 1, cs, r, chunk) * mixed).astype(BF16)
            mixed = take(y_ref, (0,), pl.ds(rows, EDGE), c, LANES, base)[:HALO]
            upper = take(y_ref, (1,), pl.ds(rows, EDGE), c, LANES, base)[:HALO]
            pre_ref[0, pl.ds(rows, HALO), :] = upper * short_rows(ext_ref, w_ref, 2, cs, rows, HALO)
            pre_ref[2, pl.ds(rows, HALO), :] = upper * short_rows(ext_ref, w_ref, 0, cs, rows, HALO)
            pre_ref[1, pl.ds(rows, HALO), :] = n_ref[3, :, cs].astype(F32) * mixed
            for i in range(3):
                for r in range(0, rows, chunk):
                    total = w_ref[i, 0:1, cs] * pre_ref[i, pl.ds(r, chunk), :]
                    for j in range(1, TAPS):
                        total = total + w_ref[i, j : j + 1, cs] * pre_ref[i, pl.ds(r + j, chunk), :]
                    gs_ref[i, pl.ds(r, chunk), cs] = total.astype(BF16)

    at = lambda i: part * count + i
    ins = [streams, before, after, grad_out, short_filter, back]
    return pl.pallas_call(
        kernel,
        grid=(count,),
        in_specs=[
            pl.BlockSpec((3, rows, block), lambda i: (0, 0, at(i))),
            pl.BlockSpec((3, HALO, block), lambda i: (0, 0, at(i))),
            pl.BlockSpec((4, HALO, block), lambda i: (0, 0, at(i))),
            pl.BlockSpec((rows, block), lambda i: (0, at(i))),
            pl.BlockSpec((3, TAPS, block), lambda i: (0, 0, at(i))),
            resident(),
        ]
        + [untouched() for _ in earlier],
        out_specs=[
            pl.BlockSpec((rows, block), lambda i: (0, at(i))),
            pl.BlockSpec((3, rows, block), lambda i: (0, 0, at(i))),
        ],
        out_shape=[
            jax.ShapeDtypeStruct((rows, full), BF16),
            jax.ShapeDtypeStruct((3, rows, full), BF16),
        ],
        scratch_shapes=[
            pltpu.VMEM((3, rows + 2 * HALO, LANES), F32),
            pltpu.VMEM((3, rows + HALO, LANES), F32),
        ],
        input_output_aliases={len(ins) + i: i for i in range(len(earlier))},
        cost_estimate=pl.CostEstimate(flops=150 * 10**6, transcendentals=0, bytes_accessed=12 * 10**6),
        name="finish",
    )(*ins, *earlier)


def shift(block, axis, distance):
    devices = range(lax.axis_size(axis))
    route = [(i - distance, i) for i in devices if i - distance in devices]
    return lax.ppermute(block, axis, route)


def exchange(blocks, groups=None):
    return lax.all_to_all(blocks, "seq", split_axis=0, concat_axis=0, axis_index_groups=groups, tiled=True)


def on_chip(value):
    lanes = -(-value.shape[-1] // LANES) * LANES
    if math.prod(value.shape[:-1]) * lanes * value.dtype.itemsize > ON_CHIP_BYTES:
        return value
    return pltpu.with_memory_space_constraint(value, pltpu.VMEM)


def following(value, earlier):
    return lax.optimization_barrier((value, earlier))[0]


def operator(streams, grad_out, long_filter, short_filter, skip_gain):
    shards = lax.axis_size("seq")
    rows = streams.shape[1]
    width = streams.shape[2]
    parts = 2 if width % (2 * shards * LANES) == 0 else 1
    span = width // parts
    chans = span // shards
    tap_rows = long_filter.shape[0]
    live = min(shards, shards * rows // tap_rows)
    fold = 2 * live <= shards
    mine = lax.axis_index("seq")
    is_low = mine < live
    where = jnp.stack([is_low.astype(jnp.int32), mine % live]).reshape(1, 2)
    fwd, inv = turn_tables(shards, rows)
    before = shift(streams[:, rows - HALO :], "seq", 1)
    after = shift(jnp.concatenate([streams[:, :HALO], grad_out[None, :HALO]], axis=0), "seq", -1)
    skips = [lax.dynamic_slice_in_dim(skip_gain, p * span + mine * chans, chans)[None] for p in range(parts)]

    both = []
    bias = []
    filtered = []
    packed = []
    for p in range(parts):
        keep = p == parts - 1 and parts > 1
        sent, terms, *rest = gates(streams, before, grad_out, short_filter, shards, p, parts, keep)
        bias.append(terms)
        filtered.append(rest[0] if rest else None)
        both.append(on_chip(exchange(sent)))
    for p in range(parts):
        packed.append(pack_taps(long_filter, shards, p, parts))
    spec = []
    shared = []
    squares = 0.0
    low = None
    for p in range(parts):
        out = raw_path(both[p], fwd, inv, where, packed[p], low, p, parts, tap_rows, live, fold)
        spec.append(out[0])
        low = out[1]
        squares = squares + jnp.sum(out[2])
        shared.append(exchange(out[3] if fold else packed[p]))
    back = []
    for p in range(parts):
        taps = shared[p].reshape(shards * tap_rows // rows, rows, chans)
        sent = conv_path(both[p], taps, spec[p], skips[p], fwd, inv)
        back.append(on_chip(exchange(sent)))
        sent_last = sent
    done = []
    sums = []
    lows = []

    def send_low(first, last, cue):
        ready = following(low, cue)
        if first == 0:
            lows.append(ready[0])
        for d in range(max(first, 1), last):
            lows.append(lax.ppermute(ready[d], "seq", [(i, i ^ d) for i in range(live)]))

    if fold:
        send_low(0, live // 2 + 1, sent_last)
    for p in range(parts):
        terms = (back[p], bias[p], filtered[p], sums)
        sums = [short_sums(streams, before, grad_out, short_filter, *terms, shards, p, parts)]
        if p == 0 and fold:
            send_low(live // 2 + 1, live, back[0])
        done = finish(streams, before, after, grad_out, short_filter, back[p], done, shards, p, parts)
    output, grad_streams = done
    sums = sums[0]
    if not fold:
        lows.append(exchange(following(low, back[-1])))
        sums = following(sums, lows[0])
    mine_sums = jnp.sum(exchange(sums).astype(F32), axis=0)
    local_sq = lax.psum(squares + jnp.sum(mine_sums * mine_sums), "chan")
    upper_sq = lax.reduce_precision(local_sq, 8, 7)
    line = lax.broadcasted_iota(jnp.int32, mine_sums.shape, 1)
    mine_sums = jnp.where(line == SUMS - 2, upper_sq, mine_sums)
    mine_sums = jnp.where(line == SUMS - 1, local_sq - upper_sq, mine_sums).astype(BF16)
    small = exchange(jnp.broadcast_to(mine_sums[None], (shards,) + mine_sums.shape))
    param_count = LF * D + (3 * TAPS + 1) * D
    filter_grad, short_grad, bias_grad = scale_taps(
        small, where, lows, shared if fold else [], shards, live, param_count
    )
    return output, grad_streams, filter_grad, short_grad, bias_grad[0]


def solution(mesh):
    placed = (
        P(None, "seq", "chan"),
        P("seq", "chan"),
        P("seq", "chan"),
        P(None, None, "chan"),
        P("chan"),
    )
    return jax.shard_map(
        operator,
        mesh=mesh,
        in_specs=placed,
        out_specs=(
            P("seq", "chan"),
            P(None, "seq", "chan"),
            P("seq", "chan"),
            P(None, None, "chan"),
            P("chan"),
        ),
        check_vma=False,
    )
```

```python
import math

import jax
import jax.numpy as jnp
from jax import lax
from jax.experimental import pallas as pl
from jax.experimental.pallas import tpu as pltpu
from jax.sharding import PartitionSpec as P


D = 8192
LF = 8192
TAPS = 7
HALO = 8
EDGE = 8
LANES = 128
SUMS = 24
ON_CHIP_BYTES = 9 * 2**18
F32 = jnp.float32
BF16 = jnp.bfloat16


def add(a, b):
    if a is None:
        return b
    if b is None:
        return a
    return a + b


def neg(a):
    return None if a is None else -a


def sub(a, b):
    if b is None:
        return a
    if a is None:
        return -b
    return a - b


def scaled(a, c):
    if a is None or abs(c) < 1e-12:
        return None
    if abs(c - 1.0) < 1e-12:
        return a
    if abs(c + 1.0) < 1e-12:
        return -a
    return a * c


def cadd(a, b):
    return (add(a[0], b[0]), add(a[1], b[1]))


def csub(a, b):
    return (sub(a[0], b[0]), sub(a[1], b[1]))


def times_i(a, sign):
    return (neg(a[1]), a[0]) if sign > 0 else (a[1], neg(a[0]))


def cmul(a, angle, gain=1.0):
    c = math.cos(angle)
    s = math.sin(angle)
    re, im = a
    if abs(abs(c) - abs(s)) < 1e-12 and re is not None and im is not None:
        root = abs(c) * gain
        sc = 1.0 if c > 0 else -1.0
        ss = 1.0 if s > 0 else -1.0
        if sc * ss > 0:
            return ((re - im) * (root * sc), (re + im) * (root * sc))
        return ((re + im) * (root * sc), (im - re) * (root * sc))
    c = c * gain
    s = s * gain
    return (sub(scaled(re, c), scaled(im, s)), add(scaled(im, c), scaled(re, s)))


def complex_dft(xs, sign):
    n = len(xs)
    if n == 1:
        return list(xs)
    half = n // 2
    sums = [cadd(xs[i], xs[i + half]) for i in range(half)]
    difs = [csub(xs[i], xs[i + half]) for i in range(half)]
    if n == 2:
        return [sums[0], difs[0]]
    quarter = n // 4
    out = [None] * n
    out[0::2] = complex_dft(sums, sign)
    turn = sign * 2.0 * math.pi / n
    first = []
    third = []
    for i in range(quarter):
        rot = times_i(difs[i + quarter], sign)
        first.append(cmul(cadd(difs[i], rot), turn * i))
        third.append(cmul(csub(difs[i], rot), turn * 3 * i))
    out[1::4] = complex_dft(first, sign)
    out[3::4] = complex_dft(third, sign)
    return out


def real_dft(xs):
    n = len(xs)
    if n == 1:
        return [(xs[0], None)]
    half = n // 2
    sums = [add(xs[i], xs[i + half]) for i in range(half)]
    difs = [sub(xs[i], xs[i + half]) for i in range(half)]
    if n == 2:
        return [(sums[0], None), (difs[0], None)]
    quarter = n // 4
    out = [None] * (half + 1)
    out[0::2] = real_dft(sums)
    turn = -2.0 * math.pi / n
    odd = [cmul((difs[i], neg(difs[i + quarter])), turn * i) for i in range(quarter)]
    for j, value in enumerate(complex_dft(odd, -1)):
        k = 4 * j + 1
        if k <= half:
            out[k] = value
        else:
            out[n - k] = (value[0], neg(value[1]))
    return out


def real_idft(spec, keep):
    n = 2 * (len(spec) - 1)
    if n == 2:
        both = [add(spec[0][0], spec[1][0]), sub(spec[0][0], spec[1][0])]
        return both[:keep]
    half = n // 2
    quarter = n // 4
    even = real_idft(spec[0::2], half)
    odd = []
    for j in range(quarter):
        k = 4 * j + 1
        odd.append(spec[k] if k <= half else (spec[n - k][0], neg(spec[n - k][1])))
    turn = 2.0 * math.pi / n
    rest = [cmul(v, turn * i, 2.0) for i, v in enumerate(complex_dft(odd, 1))]
    wave = [rest[i][0] for i in range(quarter)] + [neg(rest[i][1]) for i in range(quarter)]
    out = [add(even[i], wave[i]) for i in range(half)]
    if keep > half:
        out = out + [sub(even[i], wave[i]) for i in range(half)]
    return out[:keep]


def turn_tables(shards, rows):
    radix = 2 * shards
    count = radix * rows
    k1 = jnp.arange(shards + 1, dtype=jnp.int32)[:, None]
    r = jnp.arange(rows, dtype=jnp.int32)
    fine = 2.0 * math.pi / count * (k1 * r[None, :] % count).astype(F32)
    coarse = 2.0 * math.pi / rows * (r[:, None] * r[None, :] % rows).astype(F32)
    fine_c = jnp.cos(fine)
    fine_s = jnp.sin(fine)
    coarse_c = jnp.cos(coarse)[None]
    coarse_s = jnp.sin(coarse)[None]

    def pair(fc, fs, gain):
        cos = fc * coarse_c - fs * coarse_s
        sin = fs * coarse_c + fc * coarse_s
        return (jnp.concatenate([cos, sin], axis=1) * gain).astype(BF16)

    fwd = pair(fine_c[:, None, :], fine_s[:, None, :], 1.0)
    inv = pair(fine_c[:, :, None], fine_s[:, :, None], 1.0 / count)
    return fwd, inv


def over_tiles(rows, work):
    def step(i, carry):
        work(pl.multiple_of(i * 16, 16))
        return carry

    lax.fori_loop(0, rows // 16, step, 0)


def split_in(load, blocks, shards, rows, store):
    def work(r):
        rs = pl.ds(r, 16)
        xs = [load(s, rs).astype(F32) for s in range(blocks)]
        xs = xs + [None] * (2 * shards - blocks)
        for k, (re, im) in enumerate(real_dft(xs)):
            if im is None:
                im = jnp.zeros(re.shape, F32)
            store(k, rs, re.astype(BF16), im.astype(BF16))

    over_tiles(rows, work)


def load_spec(load, shards):
    spec = []
    for k in range(shards + 1):
        re, im = load(k)
        spec.append((re, None if k == 0 or k == shards else im))
    return spec


def dot(a, b):
    return jnp.dot(a, b, preferred_element_type=F32)


def backward(table, z_re, z_im, rows, step):
    chans = z_re.shape[1]
    z_re = z_re.astype(BF16)
    z_im = z_im.astype(BF16)
    if step == chans:
        p = dot(table, jnp.concatenate([z_re, z_im], axis=1))
        return p[:rows, :step] - p[rows:, step:], p[rows:, :step] + p[:rows, step:]
    p = dot(table, z_re)
    q = dot(table, z_im)
    return p[:rows] - q[rows:], p[rows:] + q[:rows]


def whole(shape):
    zeros = (0,) * len(shape)
    return pl.BlockSpec(shape, lambda *_: zeros, pipeline_mode=pl.Buffered(1))


def per_step(shape):
    zeros = (0,) * (len(shape) - 1)
    return pl.BlockSpec(shape, lambda i: (i,) + zeros)


def in_smem():
    return pl.BlockSpec(memory_space=pltpu.SMEM)


def resident():
    return pl.BlockSpec(memory_space=pltpu.VMEM)


def untouched():
    return pl.BlockSpec(memory_space=pl.ANY)


def raw_path(both, fwd, inv, where, packed, low_before, part, parts, tap_rows, live, fold):
    shards, _, rows, chans = both.shape
    steps = shards + 1
    step = max(chans, LANES)
    per_shard = tap_rows // rows
    blocks = live * per_shard

    def kernel(*refs):
        refs = list(refs)
        x_ref, fwd_ref, inv_ref = refs[:3]
        del refs[:3]
        if fold:
            flag_ref, h_ref = refs[:2]
            del refs[:2]
        if part:
            del refs[:1]
        spec_ref, low_ref, sq_ref = refs[:3]
        del refs[:3]
        if fold:
            send_ref = refs.pop(0)
        a_ref, y_ref = refs
        k = pl.program_id(0)
        mine = flag_ref[0, 1] if fold else 0

        @pl.when(k == 0)
        def _():
            for i in range(2):

                def store(at, rs, re, im, i=i):
                    a_ref[at, 0, rs, pl.ds(i * step, chans)] = re
                    a_ref[at, 1, rs, pl.ds(i * step, chans)] = im

                split_in(lambda s, rs, i=i: x_ref[s, i, rs, :], shards, shards, rows, store)

        p = dot(fwd_ref[0], a_ref[k, 0])
        q = dot(fwd_ref[0], a_ref[k, 1])
        re = p[:rows] + q[rows:]
        im = q[:rows] - p[rows:]
        spec_ref[0, 0] = re
        spec_ref[0, 1] = im
        g_re = re[:, :chans]
        g_im = im[:, :chans]
        m_re = re[:, step : step + chans]
        m_im = im[:, step : step + chans]
        y_re, y_im = backward(inv_ref[0], g_re * m_re + g_im * m_im, g_re * m_im - g_im * m_re, rows, step)
        y_ref[k, 0] = y_re
        y_ref[k, 1] = y_im

        @pl.when(k == steps - 1)
        def _():
            sq_ref[...] = jnp.zeros(sq_ref.shape, F32)

            def work(r):
                rs = pl.ds(r, 16)
                out = real_idft(load_spec(lambda at: (y_ref[at, 0, rs, :], y_ref[at, 1, rs, :]), shards), shards)
                square = None
                for s in range(blocks):
                    at = (s // per_shard) ^ mine
                    low_ref[at, 0, pl.ds((s % per_shard) * rows + r, 16), :] = out[s].astype(BF16)
                    square = add(square, out[s] * out[s])
                sq_ref[...] += square[:8] + square[8:]

            over_tiles(rows, work)
            if fold:

                @pl.when(flag_ref[0, 0] == 1)
                def _():
                    for s in range(shards):
                        send_ref[s] = h_ref[s]

                @pl.when(flag_ref[0, 0] == 0)
                def _():
                    for s in range(shards):
                        if s < live:
                            send_ref[s] = low_ref[s ^ mine, 0]
                        else:
                            send_ref[s] = jnp.zeros((tap_rows, chans), BF16)

    ins = [both, fwd, inv]
    in_specs = [
        resident(),
        per_step((1, 2 * rows, rows)),
        per_step((1, 2 * rows, rows)),
    ]
    if fold:
        ins += [where, packed]
        in_specs += [in_smem(), whole(packed.shape)]
    aliases = {}
    if part:
        aliases = {len(ins): 1}
        ins.append(low_before)
        in_specs.append(untouched())
    out_specs = [
        per_step((1, 2, rows, 2 * step)),
        pl.BlockSpec((live, 1, tap_rows, chans), lambda i: (0, part, 0, 0), pipeline_mode=pl.Buffered(1)),
        whole((8, chans)),
    ]
    out_shape = [
        jax.ShapeDtypeStruct((steps, 2, rows, 2 * step), F32),
        jax.ShapeDtypeStruct((live, parts, tap_rows, chans), BF16),
        jax.ShapeDtypeStruct((8, chans), F32),
    ]
    if fold:
        out_specs.append(whole(packed.shape))
        out_shape.append(jax.ShapeDtypeStruct(packed.shape, BF16))
    return pl.pallas_call(
        kernel,
        grid=(steps,),
        in_specs=in_specs,
        out_specs=out_specs,
        out_shape=out_shape,
        scratch_shapes=[
            pltpu.VMEM((steps, 2, rows, 2 * step), BF16),
            pltpu.VMEM((steps, 2, rows, chans), F32),
        ],
        input_output_aliases=aliases,
        cost_estimate=pl.CostEstimate(flops=20 * 10**9, transcendentals=0, bytes_accessed=25 * 10**6),
        name="raw_path",
    )(*ins)


def conv_path(both, taps, spec, skip, fwd, inv):
    shards, _, rows, chans = both.shape
    steps = shards + 1
    step = max(chans, LANES)
    blocks = min(taps.shape[0], shards)

    def kernel(x_ref, h_ref, spec_ref, skip_ref, fwd_ref, inv_ref, out_ref, a_ref, y_ref):
        k = pl.program_id(0)

        @pl.when(k == 0)
        def _():
            def store(at, rs, re, im):
                a_ref[at, rs, pl.ds(0, chans)] = re
                a_ref[at, rs, pl.ds(step, chans)] = im

            split_in(lambda s, rs: h_ref[s, rs, :], blocks, shards, rows, store)

        p = dot(fwd_ref[0], a_ref[k])
        h_re = p[:rows, :chans] + p[rows:, step : step + chans]
        h_im = p[:rows, step : step + chans] - p[rows:, :chans]
        g_re = spec_ref[0, 0, :, pl.ds(0, chans)]
        g_im = spec_ref[0, 1, :, pl.ds(0, chans)]
        m_re = spec_ref[0, 0, :, pl.ds(step, chans)]
        m_im = spec_ref[0, 1, :, pl.ds(step, chans)]
        y_re, y_im = backward(inv_ref[0], g_re * h_re - g_im * h_im, g_re * h_im + g_im * h_re, rows, step)
        y_ref[k, 0] = y_re
        y_ref[k, 1] = y_im
        y_re, y_im = backward(inv_ref[0], h_re * m_re + h_im * m_im, h_re * m_im - h_im * m_re, rows, step)
        y_ref[k, 2] = y_re
        y_ref[k, 3] = y_im

        @pl.when(k == steps - 1)
        def _():
            gain = skip_ref[...]
            for i in range(2):

                def work(r, i=i):
                    rs = pl.ds(r, 16)
                    spectrum = load_spec(lambda at: (y_ref[at, 2 * i, rs, :], y_ref[at, 2 * i + 1, rs, :]), shards)
                    out = real_idft(spectrum, shards)
                    out = [(out[s] + gain * x_ref[s, i, rs, :].astype(F32)).astype(BF16) for s in range(shards)]
                    for s in range(shards):
                        out_ref[s, i, rs, :] = out[s]

                    @pl.when(r == 0)
                    def _():
                        for s in range(shards - 1):
                            out_ref[s, i, pl.ds(rows, EDGE), :] = out[s + 1][:EDGE]
                        out_ref[shards - 1, i, pl.ds(rows, EDGE), :] = jnp.zeros((EDGE, chans), BF16)

                over_tiles(rows, work)

    out_block = (shards, 2, rows + EDGE, chans)
    return pl.pallas_call(
        kernel,
        grid=(steps,),
        in_specs=[
            resident(),
            resident(),
            per_step((1, 2, rows, 2 * step)),
            whole((1, chans)),
            per_step((1, 2 * rows, rows)),
            per_step((1, 2 * rows, rows)),
        ],
        out_specs=whole(out_block),
        out_shape=jax.ShapeDtypeStruct(out_block, BF16),
        scratch_shapes=[
            pltpu.VMEM((steps, rows, 2 * step), BF16),
            pltpu.VMEM((steps, 4, rows, chans), F32),
        ],
        cost_estimate=pl.CostEstimate(flops=20 * 10**9, transcendentals=0, bytes_accessed=25 * 10**6),
        name="conv_path",
    )(both, taps, spec, skip, fwd, inv)


def plan_lanes(width, chans, most=512):
    block = max(chans, LANES)
    while block < most and width % (2 * block) == 0:
        block *= 2
    return block


def put(ref, lead, rs, c, value):
    chans = ref.shape[-1]
    width = value.shape[1]
    if chans >= width:
        ref[(c // chans,) + lead + (rs, pl.ds(c % chans, width))] = value
        return
    for i in range(width // chans):
        ref[(c // chans + i,) + lead + (rs, slice(None))] = value[:, i * chans : (i + 1) * chans]


def take(ref, lead, rs, c, width, base=0):
    chans = ref.shape[-1]
    if chans >= width:
        return ref[(base + c // chans,) + lead + (rs, pl.ds(c % chans, width))].astype(F32)
    first = base + c // chans
    return jnp.concatenate(
        [ref[(first + i,) + lead + (rs, slice(None))].astype(F32) for i in range(width // chans)], axis=1
    )


def pack_taps(long_filter, shards, part, parts):
    rows, width = long_filter.shape
    width = width // parts
    chans = width // shards
    block = plan_lanes(width, chans)
    count = width // block
    groups = block // chans

    def kernel(x_ref, o_ref):
        for c in range(0, block, LANES):
            put(o_ref, (), pl.ds(0, rows), c, x_ref[:, pl.ds(c, LANES)].astype(BF16))

    return pl.pallas_call(
        kernel,
        grid=(count,),
        in_specs=[pl.BlockSpec((rows, block), lambda i: (0, part * count + i))],
        out_specs=pl.BlockSpec((groups, rows, chans), lambda i: (i, 0, 0)),
        out_shape=jax.ShapeDtypeStruct((shards, rows, chans), BF16),
        cost_estimate=pl.CostEstimate(flops=10**6, transcendentals=0, bytes_accessed=6 * 10**6),
        name="pack_taps",
    )(long_filter)


def scale_taps(small, where, lows, shared, shards, live, param_count):
    parts, rows, chans = lows[0].shape[-3:]
    width = shards * chans
    block = plan_lanes(width, chans, 1024)
    while (live * chans) % block:
        block //= 2
    count = width // block
    groups = block // chans
    split = live // groups
    listed = len(lows) > 1
    sides = small.shape[0] // shards

    def kernel(*refs):
        small_ref, at_ref = refs[:2]
        low_refs = refs[2 : 2 + len(lows)]
        o_ref, short_ref, bias_ref = refs[-3:]
        q = pl.program_id(0)
        i = pl.program_id(1)
        lanes = min(chans, LANES)
        total = jnp.sum(small_ref[:, 0, SUMS - 8 :, pl.ds(0, lanes)].astype(F32), axis=0)
        total = total[6:7, 0:1] + total[7:8, 0:1]
        clip = 1.0 / jnp.sqrt(jnp.broadcast_to(total, (1, LANES)) / param_count + 1e-06)
        gain = clip * at_ref[0, 0].astype(F32)
        for c in range(0, block, LANES):
            lines = [
                small_ref[(i * groups + (c + b) // chans) * sides + at_ref[0, 2], q, :, pl.ds((c + b) % chans, lanes)]
                for b in range(0, LANES, lanes)
            ]
            lines = jnp.concatenate([v.astype(F32) for v in lines], axis=1) * clip
            for j in range(3):
                short_ref[j, :, pl.ds(c, LANES)] = lines[j * TAPS : (j + 1) * TAPS]
            bias_ref[:, pl.ds(c, LANES)] = lines[3 * TAPS : 3 * TAPS + 1]

        @pl.when(i < split)
        def _():
            if not listed:
                for c in range(0, block, LANES):
                    o_ref[:, pl.ds(c, LANES)] = take(low_refs[0], (0,), pl.ds(0, rows), c, LANES) * gain
                return
            for j in range(groups):
                source = (i * groups + j) ^ at_ref[0, 1]
                for d, x_ref in enumerate(low_refs):

                    @pl.when(source == d)
                    def _(j=j, x_ref=x_ref):
                        o_ref[:, pl.ds(j * chans, chans)] = x_ref[q].astype(F32) * jnp.concatenate([gain] * (chans // LANES), axis=1)

        for part, x_ref in enumerate(refs[2 + len(lows) : -3]):

            @pl.when(jnp.logical_and(i >= split, q == part))
            def _(x_ref=x_ref):
                for c in range(0, block, LANES):
                    o_ref[:, pl.ds(c, LANES)] = take(x_ref, (), pl.ds(0, rows), c, LANES) * gain

    def shared_map(part):
        def index(q, i):
            upper = jnp.maximum(i, split)
            held = split if part else count - 1
            return (jnp.where(q == part, upper, held), 0, 0)

        return index

    if listed:
        lows = [on_chip(x) for x in lows]
        low_specs = [resident() for _ in lows]
    else:
        low_specs = [pl.BlockSpec((groups, 1, rows, chans), lambda q, i: (jnp.minimum(i, split - 1), q, 0, 0))]
    return pl.pallas_call(
        kernel,
        grid=(parts, count),
        in_specs=[whole(small.shape), in_smem()]
        + low_specs
        + [pl.BlockSpec((groups, rows, chans), shared_map(p)) for p in range(len(shared))],
        out_specs=[
            pl.BlockSpec((rows, block), lambda q, i: (0, q * count + i)),
            pl.BlockSpec((3, TAPS, block), lambda q, i: (0, 0, q * count + i)),
            pl.BlockSpec((1, block), lambda q, i: (0, q * count + i)),
        ],
        out_shape=[
            jax.ShapeDtypeStruct((rows, parts * width), F32),
            jax.ShapeDtypeStruct((3, TAPS, parts * width), F32),
            jax.ShapeDtypeStruct((1, parts * width), F32),
        ],
        name="scale_taps",
    )(small, where, *lows, *shared)


def short_rows(ext_ref, w_ref, i, cs, r, rows):
    total = w_ref[i, 0:1, cs] * ext_ref[i, pl.ds(HALO + r, rows), :]
    for j in range(1, TAPS):
        total = total + w_ref[i, j : j + 1, cs] * ext_ref[i, pl.ds(HALO + r - j, rows), :]
    return total


def gates(streams, before, grad_out, short_filter, shards, part, parts, keep):
    _, rows, width = streams.shape
    width = width // parts
    chans = width // shards
    block = plan_lanes(width, chans)
    count = width // block
    groups = block // chans
    chunk = math.gcd(rows, 64)

    def kernel(x_ref, b_ref, go_ref, w_ref, o_ref, bias_ref, *refs):
        ext_ref = refs[-1]
        for c in range(0, block, LANES):
            cs = pl.ds(c, LANES)
            fill_ext(ext_ref, x_ref, b_ref, None, cs, rows)
            bias = jnp.zeros((8, LANES), F32)
            for r in range(0, rows, chunk):
                rs = pl.ds(r, chunk)
                x1s = short_rows(ext_ref, w_ref, 0, cs, r, chunk)
                vs = short_rows(ext_ref, w_ref, 2, cs, r, chunk)
                gated = (x1s * vs).astype(BF16)
                mix = go_ref[rs, cs].astype(F32) * short_rows(ext_ref, w_ref, 1, cs, r, chunk)
                mix = mix.astype(BF16)
                put(o_ref, (0,), rs, c, gated)
                put(o_ref, (1,), rs, c, mix)
                if keep:
                    refs[0][0, rs, cs] = x1s
                    refs[0][1, rs, cs] = vs
                term = gated.astype(F32) * mix.astype(F32)
                bias = bias + jnp.sum(term.reshape(chunk // 8, 8, LANES), axis=0)
            bias_ref[:, cs] = jnp.sum(bias, axis=0, keepdims=True)

    out_specs = [
        pl.BlockSpec((groups, 2, rows, chans), lambda i: (i, 0, 0, 0)),
        pl.BlockSpec((1, block), lambda i: (0, i)),
    ]
    out_shape = [
        jax.ShapeDtypeStruct((shards, 2, rows, chans), BF16),
        jax.ShapeDtypeStruct((1, width), F32),
    ]
    if keep:
        out_specs.append(pl.BlockSpec((2, rows, block), lambda i: (0, 0, i)))
        out_shape.append(jax.ShapeDtypeStruct((2, rows, width), F32))
    return pl.pallas_call(
        kernel,
        grid=(count,),
        in_specs=[
            pl.BlockSpec((3, rows, block), lambda i: (0, 0, part * count + i)),
            pl.BlockSpec((3, HALO, block), lambda i: (0, 0, part * count + i)),
            pl.BlockSpec((rows, block), lambda i: (0, part * count + i)),
            pl.BlockSpec((3, TAPS, block), lambda i: (0, 0, part * count + i)),
        ],
        out_specs=out_specs,
        out_shape=out_shape,
        scratch_shapes=[pltpu.VMEM((3, rows + HALO, LANES), F32)],
        cost_estimate=pl.CostEstimate(flops=60 * 10**6, transcendentals=0, bytes_accessed=7 * 10**6),
        name="gates",
    )(streams, before, grad_out, short_filter)


def fill_ext(ext_ref, x_ref, b_ref, n_ref, cs, rows):
    for i in range(3):
        ext_ref[i, pl.ds(0, HALO), :] = b_ref[i, :, cs].astype(F32)
        ext_ref[i, pl.ds(HALO, rows), :] = x_ref[i, :, cs].astype(F32)
        if n_ref is not None:
            ext_ref[i, pl.ds(HALO + rows, HALO), :] = n_ref[i, :, cs].astype(F32)


def short_sums(streams, before, grad_out, short_filter, back, bias, kept, earlier, shards, part, parts):
    _, rows, full = streams.shape
    width = full // parts
    chans = width // shards
    block = plan_lanes(width, chans)
    count = width // block
    groups = block // chans
    chunk = math.gcd(rows, 64)

    def kernel(x_ref, b_ref, go_ref, w_ref, y_ref, bias_ref, *refs):
        st_ref, ext_ref, pre_ref = refs[-3:]
        base = pl.program_id(0) * groups
        for c in range(0, block, LANES):
            cs = pl.ds(c, LANES)
            fill_ext(ext_ref, x_ref, b_ref, None, cs, rows)
            for r in range(0, rows, chunk):
                rs = pl.ds(r, chunk)
                upper = take(y_ref, (1,), rs, c, LANES, base)
                if kept is None:
                    x1s = short_rows(ext_ref, w_ref, 0, cs, r, chunk)
                    vs = short_rows(ext_ref, w_ref, 2, cs, r, chunk)
                else:
                    x1s = refs[0][0, rs, cs]
                    vs = refs[0][1, rs, cs]
                pre_ref[0, rs, :] = upper * vs
                pre_ref[2, rs, :] = upper * x1s
                pre_ref[1, rs, :] = go_ref[rs, cs].astype(F32) * take(y_ref, (0,), rs, c, LANES, base)
            lines = []
            for i in range(3):
                sums = [jnp.zeros((8, LANES), F32) for _ in range(TAPS)]
                for r in range(0, rows, chunk):
                    own = pre_ref[i, pl.ds(r, chunk), :]
                    for j in range(TAPS):
                        term = own * ext_ref[i, pl.ds(HALO + r - j, chunk), :]
                        sums[j] = sums[j] + jnp.sum(term.reshape(chunk // 8, 8, LANES), axis=0)
                lines += [jnp.sum(v, axis=0, keepdims=True) for v in sums]
            lines.append(bias_ref[:, cs])
            lines.append(jnp.zeros((SUMS - len(lines), LANES), F32))
            put(st_ref, (0,), pl.ds(0, SUMS), c, jnp.concatenate(lines, axis=0).astype(BF16))

    at = lambda i: part * count + i
    ins = [streams, before, grad_out, short_filter, back, bias]
    in_specs = [
        pl.BlockSpec((3, rows, block), lambda i: (0, 0, at(i))),
        pl.BlockSpec((3, HALO, block), lambda i: (0, 0, at(i))),
        pl.BlockSpec((rows, block), lambda i: (0, at(i))),
        pl.BlockSpec((3, TAPS, block), lambda i: (0, 0, at(i))),
        resident(),
        pl.BlockSpec((1, block), lambda i: (0, i)),
    ]
    if kept is not None:
        ins.append(kept)
        in_specs.append(pl.BlockSpec((2, rows, block), lambda i: (0, 0, i)))
    return pl.pallas_call(
        kernel,
        grid=(count,),
        in_specs=in_specs + [untouched() for _ in earlier],
        out_specs=pl.BlockSpec((groups, 1, SUMS, chans), lambda i: (i, part, 0, 0)),
        out_shape=jax.ShapeDtypeStruct((shards, parts, SUMS, chans), BF16),
        scratch_shapes=[
            pltpu.VMEM((3, rows + HALO, LANES), F32),
            pltpu.VMEM((3, rows, LANES), F32),
        ],
        input_output_aliases={len(ins): 0} if earlier else {},
        cost_estimate=pl.CostEstimate(flops=150 * 10**6, transcendentals=0, bytes_accessed=8 * 10**6),
        name="short_sums",
    )(*ins, *earlier)


def finish(streams, before, after, grad_out, short_filter, back, earlier, shards, part, parts, piece, pieces):
    _, rows, full = streams.shape
    width = full // parts
    chans = width // shards
    block = plan_lanes(width, chans)
    count = width // block
    steps = count // pieces
    groups = block // chans
    chunk = math.gcd(rows, 64)

    def kernel(x_ref, b_ref, n_ref, go_ref, w_ref, y_ref, *refs):
        o_ref, gs_ref, ext_ref, pre_ref = refs[-4:]
        base = (piece * steps + pl.program_id(0)) * groups
        for c in range(0, block, LANES):
            cs = pl.ds(c, LANES)
            fill_ext(ext_ref, x_ref, b_ref, n_ref, cs, rows)
            for r in range(0, rows, chunk):
                rs = pl.ds(r, chunk)
                mixed = take(y_ref, (0,), rs, c, LANES, base)
                upper = take(y_ref, (1,), rs, c, LANES, base)
                pre_ref[0, rs, :] = upper * short_rows(ext_ref, w_ref, 2, cs, r, chunk)
                pre_ref[2, rs, :] = upper * short_rows(ext_ref, w_ref, 0, cs, r, chunk)
                pre_ref[1, rs, :] = go_ref[rs, cs].astype(F32) * mixed
                o_ref[rs, cs] = (short_rows(ext_ref, w_ref, 1, cs, r, chunk) * mixed).astype(BF16)
            mixed = take(y_ref, (0,), pl.ds(rows, EDGE), c, LANES, base)[:HALO]
            upper = take(y_ref, (1,), pl.ds(rows, EDGE), c, LANES, base)[:HALO]
            pre_ref[0, pl.ds(rows, HALO), :] = upper * short_rows(ext_ref, w_ref, 2, cs, rows, HALO)
            pre_ref[2, pl.ds(rows, HALO), :] = upper * short_rows(ext_ref, w_ref, 0, cs, rows, HALO)
            pre_ref[1, pl.ds(rows, HALO), :] = n_ref[3, :, cs].astype(F32) * mixed
            for i in range(3):
                for r in range(0, rows, chunk):
                    total = w_ref[i, 0:1, cs] * pre_ref[i, pl.ds(r, chunk), :]
                    for j in range(1, TAPS):
                        total = total + w_ref[i, j : j + 1, cs] * pre_ref[i, pl.ds(r + j, chunk), :]
                    gs_ref[i, pl.ds(r, chunk), cs] = total.astype(BF16)

    at = lambda i: part * count + piece * steps + i
    ins = [streams, before, after, grad_out, short_filter, back]
    return pl.pallas_call(
        kernel,
        grid=(steps,),
        in_specs=[
            pl.BlockSpec((3, rows, block), lambda i: (0, 0, at(i))),
            pl.BlockSpec((3, HALO, block), lambda i: (0, 0, at(i))),
            pl.BlockSpec((4, HALO, block), lambda i: (0, 0, at(i))),
            pl.BlockSpec((rows, block), lambda i: (0, at(i))),
            pl.BlockSpec((3, TAPS, block), lambda i: (0, 0, at(i))),
            resident(),
        ]
        + [untouched() for _ in earlier],
        out_specs=[
            pl.BlockSpec((rows, block), lambda i: (0, at(i))),
            pl.BlockSpec((3, rows, block), lambda i: (0, 0, at(i))),
        ],
        out_shape=[
            jax.ShapeDtypeStruct((rows, full), BF16),
            jax.ShapeDtypeStruct((3, rows, full), BF16),
        ],
        scratch_shapes=[
            pltpu.VMEM((3, rows + 2 * HALO, LANES), F32),
            pltpu.VMEM((3, rows + HALO, LANES), F32),
        ],
        input_output_aliases={len(ins) + i: i for i in range(len(earlier))},
        cost_estimate=pl.CostEstimate(flops=150 * 10**6, transcendentals=0, bytes_accessed=12 * 10**6),
        name="finish",
    )(*ins, *earlier)


def shift(block, axis, distance):
    devices = range(lax.axis_size(axis))
    route = [(i - distance, i) for i in devices if i - distance in devices]
    return lax.ppermute(block, axis, route)


def exchange(blocks, groups=None):
    return lax.all_to_all(blocks, "seq", split_axis=0, concat_axis=0, axis_index_groups=groups, tiled=True)


def on_chip(value):
    lanes = -(-value.shape[-1] // LANES) * LANES
    if math.prod(value.shape[:-1]) * lanes * value.dtype.itemsize > ON_CHIP_BYTES:
        return value
    return pltpu.with_memory_space_constraint(value, pltpu.VMEM)


def following(value, earlier):
    return lax.optimization_barrier((value, earlier))[0]


def operator(streams, grad_out, long_filter, short_filter, skip_gain):
    shards = lax.axis_size("seq")
    rows = streams.shape[1]
    width = streams.shape[2]
    parts = 2 if width % (2 * shards * LANES) == 0 else 1
    span = width // parts
    chans = span // shards
    tap_rows = long_filter.shape[0]
    live = min(shards, shards * rows // tap_rows)
    fold = 2 * live <= shards
    mine = lax.axis_index("seq")
    is_low = mine < live
    where = jnp.stack([is_low.astype(jnp.int32), mine % live, lax.axis_index("chan")]).reshape(1, 3)
    fwd, inv = turn_tables(shards, rows)
    before = shift(streams[:, rows - HALO :], "seq", 1)
    after = shift(jnp.concatenate([streams[:, :HALO], grad_out[None, :HALO]], axis=0), "seq", -1)
    skips = [lax.dynamic_slice_in_dim(skip_gain, p * span + mine * chans, chans)[None] for p in range(parts)]

    both = []
    bias = []
    filtered = []
    packed = []
    for p in range(parts):
        keep = p == parts - 1 and parts > 1
        sent, terms, *rest = gates(streams, before, grad_out, short_filter, shards, p, parts, keep)
        bias.append(terms)
        filtered.append(rest[0] if rest else None)
        both.append(on_chip(exchange(sent)))
    for p in range(parts):
        packed.append(pack_taps(long_filter, shards, p, parts))
    spec = []
    shared = []
    squares = 0.0
    low = None
    for p in range(parts):
        out = raw_path(both[p], fwd, inv, where, packed[p], low, p, parts, tap_rows, live, fold)
        spec.append(out[0])
        low = out[1]
        squares = squares + jnp.sum(out[2])
        shared.append(exchange(out[3] if fold else packed[p]))
    back = []
    if parts > 1:
        skips[-1], squares = lax.optimization_barrier((skips[-1], squares))
    for p in range(parts):
        taps = shared[p].reshape(shards * tap_rows // rows, rows, chans)
        sent = conv_path(both[p], taps, spec[p], skips[p], fwd, inv)
        back.append(on_chip(exchange(sent)))
        sent_last = sent
    done = []
    sums = []
    lows = []

    def send_low(first, last, cue):
        ready = following(low, cue)
        if first == 0:
            lows.append(ready[0])
        for d in range(max(first, 1), last):
            lows.append(lax.ppermute(ready[d], "seq", [(i, i ^ d) for i in range(live)]))

    if fold:
        send_low(0, live // 2 + 1, sent_last)
    for p in range(parts):
        terms = (back[p], bias[p], filtered[p], sums)
        sums = [short_sums(streams, before, grad_out, short_filter, *terms, shards, p, parts)]
        if p == 0 and fold:
            send_low(live // 2 + 1, live, back[0])
        pieces = 2 if p and span // plan_lanes(span, chans) % 2 == 0 else 1
        for piece in range(pieces):
            given = (streams, before, after, grad_out, short_filter, back[p], done)
            done = finish(*given, shards, p, parts, piece, pieces)
    output, grad_streams = done
    sums = sums[0]
    if not fold:
        lows.append(exchange(following(low, back[-1])))
        sums = following(sums, lows[0])
    mine_sums = jnp.sum(exchange(sums).astype(F32), axis=0)
    local_sq = squares + jnp.sum(mine_sums * mine_sums)
    upper_sq = lax.reduce_precision(local_sq, 8, 7)
    line = lax.broadcasted_iota(jnp.int32, mine_sums.shape, 1)
    mine_sums = jnp.where(line == SUMS - 2, upper_sq, mine_sums)
    mine_sums = jnp.where(line == SUMS - 1, local_sq - upper_sq, mine_sums).astype(BF16)
    copies = jnp.broadcast_to(mine_sums[None], (shards * lax.axis_size("chan"),) + mine_sums.shape)
    small = lax.all_to_all(copies, ("seq", "chan"), split_axis=0, concat_axis=0, tiled=True)
    param_count = LF * D + (3 * TAPS + 1) * D
    filter_grad, short_grad, bias_grad = scale_taps(
        small, where, lows, shared if fold else [], shards, live, param_count
    )
    return output, grad_streams, filter_grad, short_grad, bias_grad[0]


def solution(mesh):
    placed = (
        P(None, "seq", "chan"),
        P("seq", "chan"),
        P("seq", "chan"),
        P(None, None, "chan"),
        P("chan"),
    )
    return jax.shard_map(
        operator,
        mesh=mesh,
        in_specs=placed,
        out_specs=(
            P("seq", "chan"),
            P(None, "seq", "chan"),
            P("seq", "chan"),
            P(None, None, "chan"),
            P("chan"),
        ),
        check_vma=False,
    )
```

```python
import math

import jax
import jax.numpy as jnp
from jax import lax
from jax.experimental import pallas as pl
from jax.experimental.pallas import tpu as pltpu
from jax.sharding import PartitionSpec as P


D = 8192
LF = 8192
TAPS = 7
HALO = 8
EDGE = 8
LANES = 128
SUMS = 24
ON_CHIP_BYTES = 9 * 2**18
F32 = jnp.float32
BF16 = jnp.bfloat16


def add(a, b):
    if a is None:
        return b
    if b is None:
        return a
    return a + b


def neg(a):
    return None if a is None else -a


def sub(a, b):
    if b is None:
        return a
    if a is None:
        return -b
    return a - b


def scaled(a, c):
    if a is None or abs(c) < 1e-12:
        return None
    if abs(c - 1.0) < 1e-12:
        return a
    if abs(c + 1.0) < 1e-12:
        return -a
    return a * c


def cadd(a, b):
    return (add(a[0], b[0]), add(a[1], b[1]))


def csub(a, b):
    return (sub(a[0], b[0]), sub(a[1], b[1]))


def times_i(a, sign):
    return (neg(a[1]), a[0]) if sign > 0 else (a[1], neg(a[0]))


def cmul(a, angle, gain=1.0):
    c = math.cos(angle)
    s = math.sin(angle)
    re, im = a
    if abs(abs(c) - abs(s)) < 1e-12 and re is not None and im is not None:
        root = abs(c) * gain
        sc = 1.0 if c > 0 else -1.0
        ss = 1.0 if s > 0 else -1.0
        if sc * ss > 0:
            return ((re - im) * (root * sc), (re + im) * (root * sc))
        return ((re + im) * (root * sc), (im - re) * (root * sc))
    c = c * gain
    s = s * gain
    return (sub(scaled(re, c), scaled(im, s)), add(scaled(im, c), scaled(re, s)))


def complex_dft(xs, sign):
    n = len(xs)
    if n == 1:
        return list(xs)
    half = n // 2
    sums = [cadd(xs[i], xs[i + half]) for i in range(half)]
    difs = [csub(xs[i], xs[i + half]) for i in range(half)]
    if n == 2:
        return [sums[0], difs[0]]
    quarter = n // 4
    out = [None] * n
    out[0::2] = complex_dft(sums, sign)
    turn = sign * 2.0 * math.pi / n
    first = []
    third = []
    for i in range(quarter):
        rot = times_i(difs[i + quarter], sign)
        first.append(cmul(cadd(difs[i], rot), turn * i))
        third.append(cmul(csub(difs[i], rot), turn * 3 * i))
    out[1::4] = complex_dft(first, sign)
    out[3::4] = complex_dft(third, sign)
    return out


def real_dft(xs):
    n = len(xs)
    if n == 1:
        return [(xs[0], None)]
    half = n // 2
    sums = [add(xs[i], xs[i + half]) for i in range(half)]
    difs = [sub(xs[i], xs[i + half]) for i in range(half)]
    if n == 2:
        return [(sums[0], None), (difs[0], None)]
    quarter = n // 4
    out = [None] * (half + 1)
    out[0::2] = real_dft(sums)
    turn = -2.0 * math.pi / n
    odd = [cmul((difs[i], neg(difs[i + quarter])), turn * i) for i in range(quarter)]
    for j, value in enumerate(complex_dft(odd, -1)):
        k = 4 * j + 1
        if k <= half:
            out[k] = value
        else:
            out[n - k] = (value[0], neg(value[1]))
    return out


def real_idft(spec, keep):
    n = 2 * (len(spec) - 1)
    if n == 2:
        both = [add(spec[0][0], spec[1][0]), sub(spec[0][0], spec[1][0])]
        return both[:keep]
    half = n // 2
    quarter = n // 4
    even = real_idft(spec[0::2], half)
    odd = []
    for j in range(quarter):
        k = 4 * j + 1
        odd.append(spec[k] if k <= half else (spec[n - k][0], neg(spec[n - k][1])))
    turn = 2.0 * math.pi / n
    rest = [cmul(v, turn * i, 2.0) for i, v in enumerate(complex_dft(odd, 1))]
    wave = [rest[i][0] for i in range(quarter)] + [neg(rest[i][1]) for i in range(quarter)]
    out = [add(even[i], wave[i]) for i in range(half)]
    if keep > half:
        out = out + [sub(even[i], wave[i]) for i in range(half)]
    return out[:keep]


def turn_tables(shards, rows):
    radix = 2 * shards
    count = radix * rows
    k1 = jnp.arange(shards + 1, dtype=jnp.int32)[:, None]
    r = jnp.arange(rows, dtype=jnp.int32)
    fine = 2.0 * math.pi / count * (k1 * r[None, :] % count).astype(F32)
    coarse = 2.0 * math.pi / rows * (r[:, None] * r[None, :] % rows).astype(F32)
    fine_c = jnp.cos(fine)
    fine_s = jnp.sin(fine)
    coarse_c = jnp.cos(coarse)[None]
    coarse_s = jnp.sin(coarse)[None]

    def pair(fc, fs, gain):
        cos = fc * coarse_c - fs * coarse_s
        sin = fs * coarse_c + fc * coarse_s
        return (jnp.concatenate([cos, sin], axis=1) * gain).astype(BF16)

    fwd = pair(fine_c[:, None, :], fine_s[:, None, :], 1.0)
    inv = pair(fine_c[:, :, None], fine_s[:, :, None], 1.0 / count)
    return fwd, inv


def over_tiles(rows, work):
    def step(i, carry):
        work(pl.multiple_of(i * 16, 16))
        return carry

    lax.fori_loop(0, rows // 16, step, 0)


def split_in(load, blocks, shards, rows, store):
    def work(r):
        rs = pl.ds(r, 16)
        xs = [load(s, rs).astype(F32) for s in range(blocks)]
        xs = xs + [None] * (2 * shards - blocks)
        for k, (re, im) in enumerate(real_dft(xs)):
            if im is None:
                im = jnp.zeros(re.shape, F32)
            store(k, rs, re.astype(BF16), im.astype(BF16))

    over_tiles(rows, work)


def load_spec(load, shards):
    spec = []
    for k in range(shards + 1):
        re, im = load(k)
        spec.append((re, None if k == 0 or k == shards else im))
    return spec


def dot(a, b):
    return jnp.dot(a, b, preferred_element_type=F32)


def backward(table, z_re, z_im, rows, step):
    chans = z_re.shape[1]
    z_re = z_re.astype(BF16)
    z_im = z_im.astype(BF16)
    if step == chans:
        p = dot(table, jnp.concatenate([z_re, z_im], axis=1))
        return p[:rows, :step] - p[rows:, step:], p[rows:, :step] + p[:rows, step:]
    p = dot(table, z_re)
    q = dot(table, z_im)
    return p[:rows] - q[rows:], p[rows:] + q[:rows]


def whole(shape):
    zeros = (0,) * len(shape)
    return pl.BlockSpec(shape, lambda *_: zeros, pipeline_mode=pl.Buffered(1))


def per_step(shape):
    zeros = (0,) * (len(shape) - 1)
    return pl.BlockSpec(shape, lambda i: (i,) + zeros)


def in_smem():
    return pl.BlockSpec(memory_space=pltpu.SMEM)


def resident():
    return pl.BlockSpec(memory_space=pltpu.VMEM)


def untouched():
    return pl.BlockSpec(memory_space=pl.ANY)


def raw_path(both, fwd, inv, where, packed, low_before, part, parts, tap_rows, live, fold):
    shards, _, rows, chans = both.shape
    steps = shards + 1
    step = max(chans, LANES)
    per_shard = tap_rows // rows
    blocks = live * per_shard

    def kernel(*refs):
        refs = list(refs)
        x_ref, fwd_ref, inv_ref = refs[:3]
        del refs[:3]
        if fold:
            flag_ref, h_ref = refs[:2]
            del refs[:2]
        if part:
            del refs[:1]
        spec_ref, low_ref, sq_ref = refs[:3]
        del refs[:3]
        if fold:
            send_ref = refs.pop(0)
        a_ref, y_ref = refs
        k = pl.program_id(0)
        mine = flag_ref[0, 1] if fold else 0

        @pl.when(k == 0)
        def _():
            for i in range(2):

                def store(at, rs, re, im, i=i):
                    a_ref[at, 0, rs, pl.ds(i * step, chans)] = re
                    a_ref[at, 1, rs, pl.ds(i * step, chans)] = im

                split_in(lambda s, rs, i=i: x_ref[s, i, rs, :], shards, shards, rows, store)

        p = dot(fwd_ref[0], a_ref[k, 0])
        q = dot(fwd_ref[0], a_ref[k, 1])
        re = p[:rows] + q[rows:]
        im = q[:rows] - p[rows:]
        spec_ref[0, 0] = re
        spec_ref[0, 1] = im
        g_re = re[:, :chans]
        g_im = im[:, :chans]
        m_re = re[:, step : step + chans]
        m_im = im[:, step : step + chans]
        y_re, y_im = backward(inv_ref[0], g_re * m_re + g_im * m_im, g_re * m_im - g_im * m_re, rows, step)
        y_ref[k, 0] = y_re
        y_ref[k, 1] = y_im

        @pl.when(k == steps - 1)
        def _():
            sq_ref[...] = jnp.zeros(sq_ref.shape, F32)

            def work(r):
                rs = pl.ds(r, 16)
                out = real_idft(load_spec(lambda at: (y_ref[at, 0, rs, :], y_ref[at, 1, rs, :]), shards), shards)
                square = None
                for s in range(blocks):
                    at = (s // per_shard) ^ mine
                    low_ref[at, 0, pl.ds((s % per_shard) * rows + r, 16), :] = out[s].astype(BF16)
                    square = add(square, out[s] * out[s])
                sq_ref[...] += square[:8] + square[8:]

            over_tiles(rows, work)
            if fold:

                @pl.when(flag_ref[0, 0] == 1)
                def _():
                    for s in range(shards):
                        send_ref[s] = h_ref[s]

                @pl.when(flag_ref[0, 0] == 0)
                def _():
                    for s in range(shards):
                        if s < live:
                            send_ref[s] = low_ref[s ^ mine, 0]
                        else:
                            send_ref[s] = jnp.zeros((tap_rows, chans), BF16)

    ins = [both, fwd, inv]
    in_specs = [
        resident(),
        per_step((1, 2 * rows, rows)),
        per_step((1, 2 * rows, rows)),
    ]
    if fold:
        ins += [where, packed]
        in_specs += [in_smem(), whole(packed.shape)]
    aliases = {}
    if part:
        aliases = {len(ins): 1}
        ins.append(low_before)
        in_specs.append(untouched())
    out_specs = [
        per_step((1, 2, rows, 2 * step)),
        pl.BlockSpec((live, 1, tap_rows, chans), lambda i: (0, part, 0, 0), pipeline_mode=pl.Buffered(1)),
        whole((8, chans)),
    ]
    out_shape = [
        jax.ShapeDtypeStruct((steps, 2, rows, 2 * step), F32),
        jax.ShapeDtypeStruct((live, parts, tap_rows, chans), BF16),
        jax.ShapeDtypeStruct((8, chans), F32),
    ]
    if fold:
        out_specs.append(whole(packed.shape))
        out_shape.append(jax.ShapeDtypeStruct(packed.shape, BF16))
    return pl.pallas_call(
        kernel,
        grid=(steps,),
        in_specs=in_specs,
        out_specs=out_specs,
        out_shape=out_shape,
        scratch_shapes=[
            pltpu.VMEM((steps, 2, rows, 2 * step), BF16),
            pltpu.VMEM((steps, 2, rows, chans), F32),
        ],
        input_output_aliases=aliases,
        cost_estimate=pl.CostEstimate(flops=20 * 10**9, transcendentals=0, bytes_accessed=25 * 10**6),
        name="raw_path",
    )(*ins)


def conv_path(both, taps, spec, skip, fwd, inv):
    shards, _, rows, chans = both.shape
    steps = shards + 1
    step = max(chans, LANES)
    blocks = min(taps.shape[0], shards)

    def kernel(x_ref, h_ref, spec_ref, skip_ref, fwd_ref, inv_ref, out_ref, a_ref, y_ref):
        k = pl.program_id(0)

        @pl.when(k == 0)
        def _():
            def store(at, rs, re, im):
                a_ref[at, rs, pl.ds(0, chans)] = re
                a_ref[at, rs, pl.ds(step, chans)] = im

            split_in(lambda s, rs: h_ref[s, rs, :], blocks, shards, rows, store)

        p = dot(fwd_ref[0], a_ref[k])
        h_re = p[:rows, :chans] + p[rows:, step : step + chans]
        h_im = p[:rows, step : step + chans] - p[rows:, :chans]
        g_re = spec_ref[0, 0, :, pl.ds(0, chans)]
        g_im = spec_ref[0, 1, :, pl.ds(0, chans)]
        m_re = spec_ref[0, 0, :, pl.ds(step, chans)]
        m_im = spec_ref[0, 1, :, pl.ds(step, chans)]
        y_re, y_im = backward(inv_ref[0], g_re * h_re - g_im * h_im, g_re * h_im + g_im * h_re, rows, step)
        y_ref[k, 0] = y_re
        y_ref[k, 1] = y_im
        y_re, y_im = backward(inv_ref[0], h_re * m_re + h_im * m_im, h_re * m_im - h_im * m_re, rows, step)
        y_ref[k, 2] = y_re
        y_ref[k, 3] = y_im

        @pl.when(k == steps - 1)
        def _():
            gain = skip_ref[...]
            for i in range(2):

                def work(r, i=i):
                    rs = pl.ds(r, 16)
                    spectrum = load_spec(lambda at: (y_ref[at, 2 * i, rs, :], y_ref[at, 2 * i + 1, rs, :]), shards)
                    out = real_idft(spectrum, shards)
                    out = [(out[s] + gain * x_ref[s, i, rs, :].astype(F32)).astype(BF16) for s in range(shards)]
                    for s in range(shards):
                        out_ref[s, i, rs, :] = out[s]

                    @pl.when(r == 0)
                    def _():
                        for s in range(shards - 1):
                            out_ref[s, i, pl.ds(rows, EDGE), :] = out[s + 1][:EDGE]
                        out_ref[shards - 1, i, pl.ds(rows, EDGE), :] = jnp.zeros((EDGE, chans), BF16)

                over_tiles(rows, work)

    out_block = (shards, 2, rows + EDGE, chans)
    return pl.pallas_call(
        kernel,
        grid=(steps,),
        in_specs=[
            resident(),
            resident(),
            per_step((1, 2, rows, 2 * step)),
            whole((1, chans)),
            per_step((1, 2 * rows, rows)),
            per_step((1, 2 * rows, rows)),
        ],
        out_specs=whole(out_block),
        out_shape=jax.ShapeDtypeStruct(out_block, BF16),
        scratch_shapes=[
            pltpu.VMEM((steps, rows, 2 * step), BF16),
            pltpu.VMEM((steps, 4, rows, chans), F32),
        ],
        cost_estimate=pl.CostEstimate(flops=20 * 10**9, transcendentals=0, bytes_accessed=25 * 10**6),
        name="conv_path",
    )(both, taps, spec, skip, fwd, inv)


def plan_lanes(width, chans, most=512):
    block = max(chans, LANES)
    while block < most and width % (2 * block) == 0:
        block *= 2
    return block


def put(ref, lead, rs, c, value):
    chans = ref.shape[-1]
    width = value.shape[1]
    if chans >= width:
        ref[(c // chans,) + lead + (rs, pl.ds(c % chans, width))] = value
        return
    for i in range(width // chans):
        ref[(c // chans + i,) + lead + (rs, slice(None))] = value[:, i * chans : (i + 1) * chans]


def take(ref, lead, rs, c, width, base=0):
    chans = ref.shape[-1]
    if chans >= width:
        return ref[(base + c // chans,) + lead + (rs, pl.ds(c % chans, width))].astype(F32)
    first = base + c // chans
    return jnp.concatenate(
        [ref[(first + i,) + lead + (rs, slice(None))].astype(F32) for i in range(width // chans)], axis=1
    )


def pack_taps(long_filter, shards, part, parts):
    rows, width = long_filter.shape
    width = width // parts
    chans = width // shards
    block = plan_lanes(width, chans)
    count = width // block
    groups = block // chans

    def kernel(x_ref, o_ref):
        for c in range(0, block, LANES):
            put(o_ref, (), pl.ds(0, rows), c, x_ref[:, pl.ds(c, LANES)].astype(BF16))

    return pl.pallas_call(
        kernel,
        grid=(count,),
        in_specs=[pl.BlockSpec((rows, block), lambda i: (0, part * count + i))],
        out_specs=pl.BlockSpec((groups, rows, chans), lambda i: (i, 0, 0)),
        out_shape=jax.ShapeDtypeStruct((shards, rows, chans), BF16),
        cost_estimate=pl.CostEstimate(flops=10**6, transcendentals=0, bytes_accessed=6 * 10**6),
        name="pack_taps",
    )(long_filter)


def scale_taps(small, where, lows, shared, shards, live, param_count):
    parts, rows, chans = lows[0].shape[-3:]
    width = shards * chans
    block = plan_lanes(width, chans, 1024)
    while (live * chans) % block:
        block //= 2
    count = width // block
    groups = block // chans
    split = live // groups
    listed = len(lows) > 1
    sides = small.shape[0] // shards

    def kernel(*refs):
        small_ref, at_ref = refs[:2]
        low_refs = refs[2 : 2 + len(lows)]
        o_ref, short_ref, bias_ref = refs[-3:]
        q = pl.program_id(0)
        i = pl.program_id(1)
        lanes = min(chans, LANES)
        total = jnp.sum(small_ref[:, 0, SUMS - 8 :, pl.ds(0, lanes)].astype(F32), axis=0)
        total = total[6:7, 0:1] + total[7:8, 0:1]
        clip = 1.0 / jnp.sqrt(jnp.broadcast_to(total, (1, LANES)) / param_count + 1e-06)
        gain = clip * at_ref[0, 0].astype(F32)
        for c in range(0, block, LANES):
            lines = [
                small_ref[(i * groups + (c + b) // chans) * sides + at_ref[0, 2], q, :, pl.ds((c + b) % chans, lanes)]
                for b in range(0, LANES, lanes)
            ]
            lines = jnp.concatenate([v.astype(F32) for v in lines], axis=1) * clip
            for j in range(3):
                short_ref[j, :, pl.ds(c, LANES)] = lines[j * TAPS : (j + 1) * TAPS]
            bias_ref[:, pl.ds(c, LANES)] = lines[3 * TAPS : 3 * TAPS + 1]

        @pl.when(i < split)
        def _():
            if not listed:
                for c in range(0, block, LANES):
                    o_ref[:, pl.ds(c, LANES)] = take(low_refs[0], (0,), pl.ds(0, rows), c, LANES) * gain
                return
            for j in range(groups):
                source = (i * groups + j) ^ at_ref[0, 1]
                for d, x_ref in enumerate(low_refs):

                    @pl.when(source == d)
                    def _(j=j, x_ref=x_ref):
                        o_ref[:, pl.ds(j * chans, chans)] = x_ref[q].astype(F32) * jnp.concatenate([gain] * (chans // LANES), axis=1)

        for part, x_ref in enumerate(refs[2 + len(lows) : -3]):

            @pl.when(jnp.logical_and(i >= split, q == part))
            def _(x_ref=x_ref):
                for c in range(0, block, LANES):
                    o_ref[:, pl.ds(c, LANES)] = take(x_ref, (), pl.ds(0, rows), c, LANES) * gain

    def shared_map(part):
        def index(q, i):
            upper = jnp.maximum(i, split)
            held = split if part else count - 1
            return (jnp.where(q == part, upper, held), 0, 0)

        return index

    if listed:
        lows = [on_chip(x) for x in lows]
        low_specs = [resident() for _ in lows]
    else:
        low_specs = [pl.BlockSpec((groups, 1, rows, chans), lambda q, i: (jnp.minimum(i, split - 1), q, 0, 0))]
    return pl.pallas_call(
        kernel,
        grid=(parts, count),
        in_specs=[whole(small.shape), in_smem()]
        + low_specs
        + [pl.BlockSpec((groups, rows, chans), shared_map(p)) for p in range(len(shared))],
        out_specs=[
            pl.BlockSpec((rows, block), lambda q, i: (0, q * count + i)),
            pl.BlockSpec((3, TAPS, block), lambda q, i: (0, 0, q * count + i)),
            pl.BlockSpec((1, block), lambda q, i: (0, q * count + i)),
        ],
        out_shape=[
            jax.ShapeDtypeStruct((rows, parts * width), F32),
            jax.ShapeDtypeStruct((3, TAPS, parts * width), F32),
            jax.ShapeDtypeStruct((1, parts * width), F32),
        ],
        name="scale_taps",
    )(small, where, *lows, *shared)


def add_sums(pieces, squares, copies):
    shards, parts, lines, chans = pieces.shape

    def kernel(x_ref, sq_ref, o_ref):
        total = jnp.sum(sq_ref[...], axis=0, keepdims=True)
        total = jnp.sum(total, axis=1, keepdims=True)
        sums = []
        for p in range(parts):
            value = x_ref[0, p].astype(F32)
            for s in range(1, shards):
                value = value + x_ref[s, p].astype(F32)
            sums.append(value)
            square = jnp.sum(value * value, axis=0, keepdims=True)
            total = total + jnp.sum(square, axis=1, keepdims=True)
        upper = total.astype(BF16).astype(F32)
        line = lax.broadcasted_iota(jnp.int32, (lines, chans), 0)
        for p in range(parts):
            value = jnp.where(line == lines - 2, upper, sums[p])
            value = jnp.where(line == lines - 1, total - upper, value).astype(BF16)
            for j in range(copies):
                o_ref[j, p] = value

    shape = (copies, parts, lines, chans)
    return pl.pallas_call(
        kernel,
        in_specs=[resident(), resident()],
        out_specs=resident(),
        out_shape=jax.ShapeDtypeStruct(shape, BF16),
        name="add_sums",
    )(pieces, squares)


def short_rows(ext_ref, w_ref, i, cs, r, rows):
    total = w_ref[i, 0:1, cs] * ext_ref[i, pl.ds(HALO + r, rows), :]
    for j in range(1, TAPS):
        total = total + w_ref[i, j : j + 1, cs] * ext_ref[i, pl.ds(HALO + r - j, rows), :]
    return total


def gates(streams, before, grad_out, short_filter, shards, part, parts, keep):
    _, rows, width = streams.shape
    width = width // parts
    chans = width // shards
    block = plan_lanes(width, chans)
    count = width // block
    groups = block // chans
    chunk = math.gcd(rows, 64)

    def kernel(x_ref, b_ref, go_ref, w_ref, o_ref, bias_ref, *refs):
        ext_ref = refs[-1]
        for c in range(0, block, LANES):
            cs = pl.ds(c, LANES)
            fill_ext(ext_ref, x_ref, b_ref, None, cs, rows)
            bias = jnp.zeros((8, LANES), F32)
            for r in range(0, rows, chunk):
                rs = pl.ds(r, chunk)
                x1s = short_rows(ext_ref, w_ref, 0, cs, r, chunk)
                vs = short_rows(ext_ref, w_ref, 2, cs, r, chunk)
                gated = (x1s * vs).astype(BF16)
                mix = go_ref[rs, cs].astype(F32) * short_rows(ext_ref, w_ref, 1, cs, r, chunk)
                mix = mix.astype(BF16)
                put(o_ref, (0,), rs, c, gated)
                put(o_ref, (1,), rs, c, mix)
                if keep:
                    refs[0][0, rs, cs] = x1s
                    refs[0][1, rs, cs] = vs
                term = gated.astype(F32) * mix.astype(F32)
                bias = bias + jnp.sum(term.reshape(chunk // 8, 8, LANES), axis=0)
            bias_ref[:, cs] = jnp.sum(bias, axis=0, keepdims=True)

    out_specs = [
        pl.BlockSpec((groups, 2, rows, chans), lambda i: (i, 0, 0, 0)),
        pl.BlockSpec((1, block), lambda i: (0, i)),
    ]
    out_shape = [
        jax.ShapeDtypeStruct((shards, 2, rows, chans), BF16),
        jax.ShapeDtypeStruct((1, width), F32),
    ]
    if keep:
        out_specs.append(pl.BlockSpec((2, rows, block), lambda i: (0, 0, i)))
        out_shape.append(jax.ShapeDtypeStruct((2, rows, width), F32))
    return pl.pallas_call(
        kernel,
        grid=(count,),
        in_specs=[
            pl.BlockSpec((3, rows, block), lambda i: (0, 0, part * count + i)),
            pl.BlockSpec((3, HALO, block), lambda i: (0, 0, part * count + i)),
            pl.BlockSpec((rows, block), lambda i: (0, part * count + i)),
            pl.BlockSpec((3, TAPS, block), lambda i: (0, 0, part * count + i)),
        ],
        out_specs=out_specs,
        out_shape=out_shape,
        scratch_shapes=[pltpu.VMEM((3, rows + HALO, LANES), F32)],
        cost_estimate=pl.CostEstimate(flops=60 * 10**6, transcendentals=0, bytes_accessed=7 * 10**6),
        name="gates",
    )(streams, before, grad_out, short_filter)


def fill_ext(ext_ref, x_ref, b_ref, n_ref, cs, rows):
    for i in range(3):
        ext_ref[i, pl.ds(0, HALO), :] = b_ref[i, :, cs].astype(F32)
        ext_ref[i, pl.ds(HALO, rows), :] = x_ref[i, :, cs].astype(F32)
        if n_ref is not None:
            ext_ref[i, pl.ds(HALO + rows, HALO), :] = n_ref[i, :, cs].astype(F32)


def short_sums(streams, before, grad_out, short_filter, back, bias, kept, earlier, shards, part, parts):
    _, rows, full = streams.shape
    width = full // parts
    chans = width // shards
    block = plan_lanes(width, chans)
    count = width // block
    groups = block // chans
    chunk = math.gcd(rows, 64)

    def kernel(x_ref, b_ref, go_ref, w_ref, y_ref, bias_ref, *refs):
        st_ref, ext_ref, pre_ref = refs[-3:]
        base = pl.program_id(0) * groups
        for c in range(0, block, LANES):
            cs = pl.ds(c, LANES)
            fill_ext(ext_ref, x_ref, b_ref, None, cs, rows)
            for r in range(0, rows, chunk):
                rs = pl.ds(r, chunk)
                upper = take(y_ref, (1,), rs, c, LANES, base)
                if kept is None:
                    x1s = short_rows(ext_ref, w_ref, 0, cs, r, chunk)
                    vs = short_rows(ext_ref, w_ref, 2, cs, r, chunk)
                else:
                    x1s = refs[0][0, rs, cs]
                    vs = refs[0][1, rs, cs]
                pre_ref[0, rs, :] = upper * vs
                pre_ref[2, rs, :] = upper * x1s
                pre_ref[1, rs, :] = go_ref[rs, cs].astype(F32) * take(y_ref, (0,), rs, c, LANES, base)
            lines = []
            for i in range(3):
                sums = [jnp.zeros((8, LANES), F32) for _ in range(TAPS)]
                for r in range(0, rows, chunk):
                    own = pre_ref[i, pl.ds(r, chunk), :]
                    for j in range(TAPS):
                        term = own * ext_ref[i, pl.ds(HALO + r - j, chunk), :]
                        sums[j] = sums[j] + jnp.sum(term.reshape(chunk // 8, 8, LANES), axis=0)
                lines += [jnp.sum(v, axis=0, keepdims=True) for v in sums]
            lines.append(bias_ref[:, cs])
            lines.append(jnp.zeros((SUMS - len(lines), LANES), F32))
            put(st_ref, (0,), pl.ds(0, SUMS), c, jnp.concatenate(lines, axis=0).astype(BF16))

    at = lambda i: part * count + i
    ins = [streams, before, grad_out, short_filter, back, bias]
    in_specs = [
        pl.BlockSpec((3, rows, block), lambda i: (0, 0, at(i))),
        pl.BlockSpec((3, HALO, block), lambda i: (0, 0, at(i))),
        pl.BlockSpec((rows, block), lambda i: (0, at(i))),
        pl.BlockSpec((3, TAPS, block), lambda i: (0, 0, at(i))),
        resident(),
        pl.BlockSpec((1, block), lambda i: (0, i)),
    ]
    if kept is not None:
        ins.append(kept)
        in_specs.append(pl.BlockSpec((2, rows, block), lambda i: (0, 0, i)))
    return pl.pallas_call(
        kernel,
        grid=(count,),
        in_specs=in_specs + [untouched() for _ in earlier],
        out_specs=pl.BlockSpec((groups, 1, SUMS, chans), lambda i: (i, part, 0, 0)),
        out_shape=jax.ShapeDtypeStruct((shards, parts, SUMS, chans), BF16),
        scratch_shapes=[
            pltpu.VMEM((3, rows + HALO, LANES), F32),
            pltpu.VMEM((3, rows, LANES), F32),
        ],
        input_output_aliases={len(ins): 0} if earlier else {},
        cost_estimate=pl.CostEstimate(flops=150 * 10**6, transcendentals=0, bytes_accessed=8 * 10**6),
        name="short_sums",
    )(*ins, *earlier)


def finish(streams, before, after, grad_out, short_filter, back, earlier, shards, part, parts):
    _, rows, full = streams.shape
    width = full // parts
    chans = width // shards
    block = plan_lanes(width, chans)
    count = width // block
    groups = block // chans
    chunk = math.gcd(rows, 64)

    def kernel(x_ref, b_ref, n_ref, go_ref, w_ref, y_ref, *refs):
        o_ref, gs_ref, ext_ref, pre_ref = refs[-4:]
        base = pl.program_id(0) * groups
        for c in range(0, block, LANES):
            cs = pl.ds(c, LANES)
            fill_ext(ext_ref, x_ref, b_ref, n_ref, cs, rows)
            for r in range(0, rows, chunk):
                rs = pl.ds(r, chunk)
                mixed = take(y_ref, (0,), rs, c, LANES, base)
                upper = take(y_ref, (1,), rs, c, LANES, base)
                pre_ref[0, rs, :] = upper * short_rows(ext_ref, w_ref, 2, cs, r, chunk)
                pre_ref[2, rs, :] = upper * short_rows(ext_ref, w_ref, 0, cs, r, chunk)
                pre_ref[1, rs, :] = go_ref[rs, cs].astype(F32) * mixed
                o_ref[rs, cs] = (short_rows(ext_ref, w_ref, 1, cs, r, chunk) * mixed).astype(BF16)
            mixed = take(y_ref, (0,), pl.ds(rows, EDGE), c, LANES, base)[:HALO]
            upper = take(y_ref, (1,), pl.ds(rows, EDGE), c, LANES, base)[:HALO]
            pre_ref[0, pl.ds(rows, HALO), :] = upper * short_rows(ext_ref, w_ref, 2, cs, rows, HALO)
            pre_ref[2, pl.ds(rows, HALO), :] = upper * short_rows(ext_ref, w_ref, 0, cs, rows, HALO)
            pre_ref[1, pl.ds(rows, HALO), :] = n_ref[3, :, cs].astype(F32) * mixed
            for i in range(3):
                for r in range(0, rows, chunk):
                    total = w_ref[i, 0:1, cs] * pre_ref[i, pl.ds(r, chunk), :]
                    for j in range(1, TAPS):
                        total = total + w_ref[i, j : j + 1, cs] * pre_ref[i, pl.ds(r + j, chunk), :]
                    gs_ref[i, pl.ds(r, chunk), cs] = total.astype(BF16)

    at = lambda i: part * count + i
    ins = [streams, before, after, grad_out, short_filter, back]
    return pl.pallas_call(
        kernel,
        grid=(count,),
        in_specs=[
            pl.BlockSpec((3, rows, block), lambda i: (0, 0, at(i))),
            pl.BlockSpec((3, HALO, block), lambda i: (0, 0, at(i))),
            pl.BlockSpec((4, HALO, block), lambda i: (0, 0, at(i))),
            pl.BlockSpec((rows, block), lambda i: (0, at(i))),
            pl.BlockSpec((3, TAPS, block), lambda i: (0, 0, at(i))),
            resident(),
        ]
        + [untouched() for _ in earlier],
        out_specs=[
            pl.BlockSpec((rows, block), lambda i: (0, at(i))),
            pl.BlockSpec((3, rows, block), lambda i: (0, 0, at(i))),
        ],
        out_shape=[
            jax.ShapeDtypeStruct((rows, full), BF16),
            jax.ShapeDtypeStruct((3, rows, full), BF16),
        ],
        scratch_shapes=[
            pltpu.VMEM((3, rows + 2 * HALO, LANES), F32),
            pltpu.VMEM((3, rows + HALO, LANES), F32),
        ],
        input_output_aliases={len(ins) + i: i for i in range(len(earlier))},
        cost_estimate=pl.CostEstimate(flops=150 * 10**6, transcendentals=0, bytes_accessed=12 * 10**6),
        name="finish",
    )(*ins, *earlier)


def shift(block, axis, distance):
    devices = range(lax.axis_size(axis))
    route = [(i - distance, i) for i in devices if i - distance in devices]
    return lax.ppermute(block, axis, route)


def exchange(blocks, groups=None):
    return lax.all_to_all(blocks, "seq", split_axis=0, concat_axis=0, axis_index_groups=groups, tiled=True)


def on_chip(value):
    lanes = -(-value.shape[-1] // LANES) * LANES
    if math.prod(value.shape[:-1]) * lanes * value.dtype.itemsize > ON_CHIP_BYTES:
        return value
    return pltpu.with_memory_space_constraint(value, pltpu.VMEM)


def following(value, earlier):
    return lax.optimization_barrier((value, earlier))[0]


def operator(streams, grad_out, long_filter, short_filter, skip_gain):
    shards = lax.axis_size("seq")
    rows = streams.shape[1]
    width = streams.shape[2]
    parts = 2 if width % (2 * shards * LANES) == 0 else 1
    span = width // parts
    chans = span // shards
    tap_rows = long_filter.shape[0]
    live = min(shards, shards * rows // tap_rows)
    fold = 2 * live <= shards
    mine = lax.axis_index("seq")
    is_low = mine < live
    where = jnp.stack([is_low.astype(jnp.int32), mine % live, lax.axis_index("chan")]).reshape(1, 3)
    fwd, inv = turn_tables(shards, rows)
    before = shift(streams[:, rows - HALO :], "seq", 1)
    after = shift(jnp.concatenate([streams[:, :HALO], grad_out[None, :HALO]], axis=0), "seq", -1)
    skips = [lax.dynamic_slice_in_dim(skip_gain, p * span + mine * chans, chans)[None] for p in range(parts)]

    both = []
    bias = []
    filtered = []
    packed = []
    for p in range(parts):
        keep = p == parts - 1 and parts > 1
        sent, terms, *rest = gates(streams, before, grad_out, short_filter, shards, p, parts, keep)
        bias.append(terms)
        filtered.append(rest[0] if rest else None)
        both.append(on_chip(exchange(sent)))
    for p in range(parts):
        packed.append(pack_taps(long_filter, shards, p, parts))
    spec = []
    shared = []
    squares = []
    low = None
    for p in range(parts):
        out = raw_path(both[p], fwd, inv, where, packed[p], low, p, parts, tap_rows, live, fold)
        spec.append(out[0])
        low = out[1]
        squares.append(out[2])
        shared.append(exchange(out[3] if fold else packed[p]))
    back = []
    sent_all = []
    for p in range(parts):
        taps = shared[p].reshape(shards * tap_rows // rows, rows, chans)
        sent = conv_path(both[p], taps, spec[p], skips[p], fwd, inv)
        back.append(on_chip(exchange(sent)))
        sent_all.append(sent)
    done = []
    sums = []
    lows = []

    def send_low(steps, cue):
        ready = following(low, cue)
        for d in steps:
            lows[d] = lax.ppermute(ready[d], "seq", [(i, i ^ d) for i in range(live)])

    if fold:
        half = live // 2
        lows = [low[0]] + [None] * (live - 1)
        send_low(range(half, half + half // 2), sent_all[0])
        send_low(range(half + half // 2, live), sent_all[-1])
    for p in range(parts):
        terms = (back[p], bias[p], filtered[p], sums)
        sums = [short_sums(streams, before, grad_out, short_filter, *terms, shards, p, parts)]
        if p == 0 and fold:
            send_low(range(1, half), back[0])
        done = finish(streams, before, after, grad_out, short_filter, back[p], done, shards, p, parts)
    output, grad_streams = done
    sums = sums[0]
    if not fold:
        lows.append(exchange(following(low, back[-1])))
        sums = following(sums, lows[0])
    pieces = on_chip(exchange(sums))
    copies = add_sums(pieces, jnp.concatenate(squares, axis=0), shards * lax.axis_size("chan"))
    small = lax.all_to_all(copies, ("seq", "chan"), split_axis=0, concat_axis=0, tiled=True)
    param_count = LF * D + (3 * TAPS + 1) * D
    filter_grad, short_grad, bias_grad = scale_taps(
        small, where, lows, shared if fold else [], shards, live, param_count
    )
    return output, grad_streams, filter_grad, short_grad, bias_grad[0]


def solution(mesh):
    placed = (
        P(None, "seq", "chan"),
        P("seq", "chan"),
        P("seq", "chan"),
        P(None, None, "chan"),
        P("chan"),
    )
    return jax.shard_map(
        operator,
        mesh=mesh,
        in_specs=placed,
        out_specs=(
            P("seq", "chan"),
            P(None, "seq", "chan"),
            P("seq", "chan"),
            P(None, None, "chan"),
            P("chan"),
        ),
        check_vma=False,
    )
```

```python
import math

import jax
import jax.numpy as jnp
from jax import lax
from jax.experimental import pallas as pl
from jax.experimental.pallas import tpu as pltpu
from jax.sharding import PartitionSpec as P


D = 8192
LF = 8192
TAPS = 7
HALO = 8
EDGE = 8
LANES = 128
SUMS = 24
ON_CHIP_BYTES = 9 * 2**18
F32 = jnp.float32
BF16 = jnp.bfloat16


def add(a, b):
    if a is None:
        return b
    if b is None:
        return a
    return a + b


def neg(a):
    return None if a is None else -a


def sub(a, b):
    if b is None:
        return a
    if a is None:
        return -b
    return a - b


def scaled(a, c):
    if a is None or abs(c) < 1e-12:
        return None
    if abs(c - 1.0) < 1e-12:
        return a
    if abs(c + 1.0) < 1e-12:
        return -a
    return a * c


def cadd(a, b):
    return (add(a[0], b[0]), add(a[1], b[1]))


def csub(a, b):
    return (sub(a[0], b[0]), sub(a[1], b[1]))


def times_i(a, sign):
    return (neg(a[1]), a[0]) if sign > 0 else (a[1], neg(a[0]))


def cmul(a, angle, gain=1.0):
    c = math.cos(angle)
    s = math.sin(angle)
    re, im = a
    if abs(abs(c) - abs(s)) < 1e-12 and re is not None and im is not None:
        root = abs(c) * gain
        sc = 1.0 if c > 0 else -1.0
        ss = 1.0 if s > 0 else -1.0
        if sc * ss > 0:
            return ((re - im) * (root * sc), (re + im) * (root * sc))
        return ((re + im) * (root * sc), (im - re) * (root * sc))
    c = c * gain
    s = s * gain
    return (sub(scaled(re, c), scaled(im, s)), add(scaled(im, c), scaled(re, s)))


def complex_dft(xs, sign):
    n = len(xs)
    if n == 1:
        return list(xs)
    half = n // 2
    sums = [cadd(xs[i], xs[i + half]) for i in range(half)]
    difs = [csub(xs[i], xs[i + half]) for i in range(half)]
    if n == 2:
        return [sums[0], difs[0]]
    quarter = n // 4
    out = [None] * n
    out[0::2] = complex_dft(sums, sign)
    turn = sign * 2.0 * math.pi / n
    first = []
    third = []
    for i in range(quarter):
        rot = times_i(difs[i + quarter], sign)
        first.append(cmul(cadd(difs[i], rot), turn * i))
        third.append(cmul(csub(difs[i], rot), turn * 3 * i))
    out[1::4] = complex_dft(first, sign)
    out[3::4] = complex_dft(third, sign)
    return out


def real_dft(xs):
    n = len(xs)
    if n == 1:
        return [(xs[0], None)]
    half = n // 2
    sums = [add(xs[i], xs[i + half]) for i in range(half)]
    difs = [sub(xs[i], xs[i + half]) for i in range(half)]
    if n == 2:
        return [(sums[0], None), (difs[0], None)]
    quarter = n // 4
    out = [None] * (half + 1)
    out[0::2] = real_dft(sums)
    turn = -2.0 * math.pi / n
    odd = [cmul((difs[i], neg(difs[i + quarter])), turn * i) for i in range(quarter)]
    for j, value in enumerate(complex_dft(odd, -1)):
        k = 4 * j + 1
        if k <= half:
            out[k] = value
        else:
            out[n - k] = (value[0], neg(value[1]))
    return out


def real_idft(spec, keep):
    n = 2 * (len(spec) - 1)
    if n == 2:
        both = [add(spec[0][0], spec[1][0]), sub(spec[0][0], spec[1][0])]
        return both[:keep]
    half = n // 2
    quarter = n // 4
    even = real_idft(spec[0::2], half)
    odd = []
    for j in range(quarter):
        k = 4 * j + 1
        odd.append(spec[k] if k <= half else (spec[n - k][0], neg(spec[n - k][1])))
    turn = 2.0 * math.pi / n
    rest = [cmul(v, turn * i, 2.0) for i, v in enumerate(complex_dft(odd, 1))]
    wave = [rest[i][0] for i in range(quarter)] + [neg(rest[i][1]) for i in range(quarter)]
    out = [add(even[i], wave[i]) for i in range(half)]
    if keep > half:
        out = out + [sub(even[i], wave[i]) for i in range(half)]
    return out[:keep]


def turn_tables(shards, rows):
    radix = 2 * shards
    count = radix * rows
    k1 = jnp.arange(shards + 1, dtype=jnp.int32)[:, None]
    r = jnp.arange(rows, dtype=jnp.int32)
    fine = 2.0 * math.pi / count * (k1 * r[None, :] % count).astype(F32)
    coarse = 2.0 * math.pi / rows * (r[:, None] * r[None, :] % rows).astype(F32)
    fine_c = jnp.cos(fine)
    fine_s = jnp.sin(fine)
    coarse_c = jnp.cos(coarse)[None]
    coarse_s = jnp.sin(coarse)[None]

    def pair(fc, fs, gain):
        cos = fc * coarse_c - fs * coarse_s
        sin = fs * coarse_c + fc * coarse_s
        return (jnp.concatenate([cos, sin], axis=1) * gain).astype(BF16)

    fwd = pair(fine_c[:, None, :], fine_s[:, None, :], 1.0)
    inv = pair(fine_c[:, :, None], fine_s[:, :, None], 1.0 / count)
    return fwd, inv


def over_tiles(rows, work):
    def step(i, carry):
        work(pl.multiple_of(i * 16, 16))
        return carry

    lax.fori_loop(0, rows // 16, step, 0)


def split_in(load, blocks, shards, rows, store):
    def work(r):
        rs = pl.ds(r, 16)
        xs = [load(s, rs).astype(F32) for s in range(blocks)]
        xs = xs + [None] * (2 * shards - blocks)
        for k, (re, im) in enumerate(real_dft(xs)):
            if im is None:
                im = jnp.zeros(re.shape, F32)
            store(k, rs, re.astype(BF16), im.astype(BF16))

    over_tiles(rows, work)


def load_spec(load, shards):
    spec = []
    for k in range(shards + 1):
        re, im = load(k)
        spec.append((re, None if k == 0 or k == shards else im))
    return spec


def dot(a, b):
    return jnp.dot(a, b, preferred_element_type=F32)


def backward(table, z_re, z_im, rows, step):
    chans = z_re.shape[1]
    z_re = z_re.astype(BF16)
    z_im = z_im.astype(BF16)
    if step == chans:
        p = dot(table, jnp.concatenate([z_re, z_im], axis=1))
        return p[:rows, :step] - p[rows:, step:], p[rows:, :step] + p[:rows, step:]
    p = dot(table, z_re)
    q = dot(table, z_im)
    return p[:rows] - q[rows:], p[rows:] + q[:rows]


def whole(shape):
    zeros = (0,) * len(shape)
    return pl.BlockSpec(shape, lambda *_: zeros, pipeline_mode=pl.Buffered(1))


def per_step(shape):
    zeros = (0,) * (len(shape) - 1)
    return pl.BlockSpec(shape, lambda i: (i,) + zeros)


def in_smem():
    return pl.BlockSpec(memory_space=pltpu.SMEM)


def resident():
    return pl.BlockSpec(memory_space=pltpu.VMEM)


def untouched():
    return pl.BlockSpec(memory_space=pl.ANY)


def raw_path(both, fwd, inv, where, packed, low_before, part, parts, tap_rows, live, fold):
    shards, _, rows, chans = both.shape
    steps = shards + 1
    step = max(chans, LANES)
    per_shard = tap_rows // rows
    blocks = live * per_shard

    def kernel(*refs):
        refs = list(refs)
        x_ref, fwd_ref, inv_ref = refs[:3]
        del refs[:3]
        if fold:
            flag_ref, h_ref = refs[:2]
            del refs[:2]
        if part:
            del refs[:1]
        spec_ref, low_ref, sq_ref = refs[:3]
        del refs[:3]
        if fold:
            send_ref = refs.pop(0)
        a_ref, y_ref = refs
        k = pl.program_id(0)
        mine = flag_ref[0, 1] if fold else 0

        @pl.when(k == 0)
        def _():
            for i in range(2):

                def store(at, rs, re, im, i=i):
                    a_ref[at, 0, rs, pl.ds(i * step, chans)] = re
                    a_ref[at, 1, rs, pl.ds(i * step, chans)] = im

                split_in(lambda s, rs, i=i: x_ref[s, i, rs, :], shards, shards, rows, store)

        p = dot(fwd_ref[0], a_ref[k, 0])
        q = dot(fwd_ref[0], a_ref[k, 1])
        re = p[:rows] + q[rows:]
        im = q[:rows] - p[rows:]
        spec_ref[0, 0] = re
        spec_ref[0, 1] = im
        g_re = re[:, :chans]
        g_im = im[:, :chans]
        m_re = re[:, step : step + chans]
        m_im = im[:, step : step + chans]
        y_re, y_im = backward(inv_ref[0], g_re * m_re + g_im * m_im, g_re * m_im - g_im * m_re, rows, step)
        y_ref[k, 0] = y_re
        y_ref[k, 1] = y_im

        @pl.when(k == steps - 1)
        def _():
            sq_ref[...] = jnp.zeros(sq_ref.shape, F32)

            def work(r):
                rs = pl.ds(r, 16)
                out = real_idft(load_spec(lambda at: (y_ref[at, 0, rs, :], y_ref[at, 1, rs, :]), shards), shards)
                square = None
                for s in range(blocks):
                    at = (s // per_shard) ^ mine
                    low_ref[at, 0, pl.ds((s % per_shard) * rows + r, 16), :] = out[s].astype(BF16)
                    square = add(square, out[s] * out[s])
                sq_ref[...] += square[:8] + square[8:]

            over_tiles(rows, work)
            if fold:

                @pl.when(flag_ref[0, 0] == 1)
                def _():
                    for s in range(shards):
                        send_ref[s] = h_ref[s]

                @pl.when(flag_ref[0, 0] == 0)
                def _():
                    for s in range(shards):
                        if s < live:
                            send_ref[s] = low_ref[s ^ mine, 0]
                        else:
                            send_ref[s] = jnp.zeros((tap_rows, chans), BF16)

    ins = [both, fwd, inv]
    in_specs = [
        resident(),
        per_step((1, 2 * rows, rows)),
        per_step((1, 2 * rows, rows)),
    ]
    if fold:
        ins += [where, packed]
        in_specs += [in_smem(), whole(packed.shape)]
    aliases = {}
    if part:
        aliases = {len(ins): 1}
        ins.append(low_before)
        in_specs.append(untouched())
    out_specs = [
        per_step((1, 2, rows, 2 * step)),
        pl.BlockSpec((live, 1, tap_rows, chans), lambda i: (0, part, 0, 0), pipeline_mode=pl.Buffered(1)),
        whole((8, chans)),
    ]
    out_shape = [
        jax.ShapeDtypeStruct((steps, 2, rows, 2 * step), F32),
        jax.ShapeDtypeStruct((live, parts, tap_rows, chans), BF16),
        jax.ShapeDtypeStruct((8, chans), F32),
    ]
    if fold:
        out_specs.append(whole(packed.shape))
        out_shape.append(jax.ShapeDtypeStruct(packed.shape, BF16))
    return pl.pallas_call(
        kernel,
        grid=(steps,),
        in_specs=in_specs,
        out_specs=out_specs,
        out_shape=out_shape,
        scratch_shapes=[
            pltpu.VMEM((steps, 2, rows, 2 * step), BF16),
            pltpu.VMEM((steps, 2, rows, chans), F32),
        ],
        input_output_aliases=aliases,
        cost_estimate=pl.CostEstimate(flops=20 * 10**9, transcendentals=0, bytes_accessed=25 * 10**6),
        name="raw_path",
    )(*ins)


def conv_path(both, taps, spec, skip, fwd, inv):
    shards, _, rows, chans = both.shape
    steps = shards + 1
    step = max(chans, LANES)
    blocks = min(taps.shape[0], shards)

    def kernel(x_ref, h_ref, spec_ref, skip_ref, fwd_ref, inv_ref, out_ref, a_ref, y_ref):
        k = pl.program_id(0)

        @pl.when(k == 0)
        def _():
            def store(at, rs, re, im):
                a_ref[at, rs, pl.ds(0, chans)] = re
                a_ref[at, rs, pl.ds(step, chans)] = im

            split_in(lambda s, rs: h_ref[s, rs, :], blocks, shards, rows, store)

        p = dot(fwd_ref[0], a_ref[k])
        h_re = p[:rows, :chans] + p[rows:, step : step + chans]
        h_im = p[:rows, step : step + chans] - p[rows:, :chans]
        g_re = spec_ref[0, 0, :, pl.ds(0, chans)]
        g_im = spec_ref[0, 1, :, pl.ds(0, chans)]
        m_re = spec_ref[0, 0, :, pl.ds(step, chans)]
        m_im = spec_ref[0, 1, :, pl.ds(step, chans)]
        y_re, y_im = backward(inv_ref[0], g_re * h_re - g_im * h_im, g_re * h_im + g_im * h_re, rows, step)
        y_ref[k, 0] = y_re
        y_ref[k, 1] = y_im
        y_re, y_im = backward(inv_ref[0], h_re * m_re + h_im * m_im, h_re * m_im - h_im * m_re, rows, step)
        y_ref[k, 2] = y_re
        y_ref[k, 3] = y_im

        @pl.when(k == steps - 1)
        def _():
            gain = skip_ref[...]
            for i in range(2):

                def work(r, i=i):
                    rs = pl.ds(r, 16)
                    spectrum = load_spec(lambda at: (y_ref[at, 2 * i, rs, :], y_ref[at, 2 * i + 1, rs, :]), shards)
                    out = real_idft(spectrum, shards)
                    out = [(out[s] + gain * x_ref[s, i, rs, :].astype(F32)).astype(BF16) for s in range(shards)]
                    for s in range(shards):
                        out_ref[s, i, rs, :] = out[s]

                    @pl.when(r == 0)
                    def _():
                        for s in range(shards - 1):
                            out_ref[s, i, pl.ds(rows, EDGE), :] = out[s + 1][:EDGE]
                        out_ref[shards - 1, i, pl.ds(rows, EDGE), :] = jnp.zeros((EDGE, chans), BF16)

                over_tiles(rows, work)

    out_block = (shards, 2, rows + EDGE, chans)
    return pl.pallas_call(
        kernel,
        grid=(steps,),
        in_specs=[
            resident(),
            resident(),
            per_step((1, 2, rows, 2 * step)),
            whole((1, chans)),
            per_step((1, 2 * rows, rows)),
            per_step((1, 2 * rows, rows)),
        ],
        out_specs=whole(out_block),
        out_shape=jax.ShapeDtypeStruct(out_block, BF16),
        scratch_shapes=[
            pltpu.VMEM((steps, rows, 2 * step), BF16),
            pltpu.VMEM((steps, 4, rows, chans), F32),
        ],
        cost_estimate=pl.CostEstimate(flops=20 * 10**9, transcendentals=0, bytes_accessed=25 * 10**6),
        name="conv_path",
    )(both, taps, spec, skip, fwd, inv)


def plan_lanes(width, chans, most=512):
    block = max(chans, LANES)
    while block < most and width % (2 * block) == 0:
        block *= 2
    return block


def put(ref, lead, rs, c, value):
    chans = ref.shape[-1]
    width = value.shape[1]
    if chans >= width:
        ref[(c // chans,) + lead + (rs, pl.ds(c % chans, width))] = value
        return
    for i in range(width // chans):
        ref[(c // chans + i,) + lead + (rs, slice(None))] = value[:, i * chans : (i + 1) * chans]


def take(ref, lead, rs, c, width, base=0):
    chans = ref.shape[-1]
    if chans >= width:
        return ref[(base + c // chans,) + lead + (rs, pl.ds(c % chans, width))].astype(F32)
    first = base + c // chans
    return jnp.concatenate(
        [ref[(first + i,) + lead + (rs, slice(None))].astype(F32) for i in range(width // chans)], axis=1
    )


def pack_taps(long_filter, shards, part, parts):
    rows, width = long_filter.shape
    width = width // parts
    chans = width // shards
    block = plan_lanes(width, chans)
    count = width // block
    groups = block // chans

    def kernel(x_ref, o_ref):
        for c in range(0, block, LANES):
            put(o_ref, (), pl.ds(0, rows), c, x_ref[:, pl.ds(c, LANES)].astype(BF16))

    return pl.pallas_call(
        kernel,
        grid=(count,),
        in_specs=[pl.BlockSpec((rows, block), lambda i: (0, part * count + i))],
        out_specs=pl.BlockSpec((groups, rows, chans), lambda i: (i, 0, 0)),
        out_shape=jax.ShapeDtypeStruct((shards, rows, chans), BF16),
        cost_estimate=pl.CostEstimate(flops=10**6, transcendentals=0, bytes_accessed=6 * 10**6),
        name="pack_taps",
    )(long_filter)


def scale_taps(small, where, lows, shared, shards, live, param_count):
    parts, rows, chans = lows[0].shape[-3:]
    width = shards * chans
    block = plan_lanes(width, chans, 1024)
    while (live * chans) % block:
        block //= 2
    count = width // block
    groups = block // chans
    split = live // groups
    listed = len(lows) > 1
    sides = small.shape[0] // shards

    def kernel(*refs):
        small_ref, at_ref = refs[:2]
        low_refs = refs[2 : 2 + len(lows)]
        o_ref, short_ref, bias_ref = refs[-3:]
        q = pl.program_id(0)
        i = pl.program_id(1)
        lanes = min(chans, LANES)
        total = jnp.sum(small_ref[:, 0, SUMS - 8 :, pl.ds(0, lanes)].astype(F32), axis=0)
        total = total[6:7, 0:1] + total[7:8, 0:1]
        clip = 1.0 / jnp.sqrt(jnp.broadcast_to(total, (1, LANES)) / param_count + 1e-06)
        gain = clip * at_ref[0, 0].astype(F32)
        for c in range(0, block, LANES):
            lines = [
                small_ref[(i * groups + (c + b) // chans) * sides + at_ref[0, 2], q, :, pl.ds((c + b) % chans, lanes)]
                for b in range(0, LANES, lanes)
            ]
            lines = jnp.concatenate([v.astype(F32) for v in lines], axis=1) * clip
            for j in range(3):
                short_ref[j, :, pl.ds(c, LANES)] = lines[j * TAPS : (j + 1) * TAPS]
            bias_ref[:, pl.ds(c, LANES)] = lines[3 * TAPS : 3 * TAPS + 1]

        @pl.when(i < split)
        def _():
            if not listed:
                for c in range(0, block, LANES):
                    o_ref[:, pl.ds(c, LANES)] = take(low_refs[0], (0,), pl.ds(0, rows), c, LANES) * gain
                return
            for j in range(groups):
                source = (i * groups + j) ^ at_ref[0, 1]
                for d, x_ref in enumerate(low_refs):

                    @pl.when(source == d)
                    def _(j=j, x_ref=x_ref):
                        o_ref[:, pl.ds(j * chans, chans)] = x_ref[q].astype(F32) * jnp.concatenate([gain] * (chans // LANES), axis=1)

        for part, x_ref in enumerate(refs[2 + len(lows) : -3]):

            @pl.when(jnp.logical_and(i >= split, q == part))
            def _(x_ref=x_ref):
                for c in range(0, block, LANES):
                    o_ref[:, pl.ds(c, LANES)] = take(x_ref, (), pl.ds(0, rows), c, LANES) * gain

    def shared_map(part):
        def index(q, i):
            upper = jnp.maximum(i, split)
            held = split if part else count - 1
            return (jnp.where(q == part, upper, held), 0, 0)

        return index

    if listed:
        lows = [on_chip(x) for x in lows]
        low_specs = [resident() for _ in lows]
    else:
        low_specs = [pl.BlockSpec((groups, 1, rows, chans), lambda q, i: (jnp.minimum(i, split - 1), q, 0, 0))]
    return pl.pallas_call(
        kernel,
        grid=(parts, count),
        in_specs=[whole(small.shape), in_smem()]
        + low_specs
        + [pl.BlockSpec((groups, rows, chans), shared_map(p)) for p in range(len(shared))],
        out_specs=[
            pl.BlockSpec((rows, block), lambda q, i: (0, q * count + i)),
            pl.BlockSpec((3, TAPS, block), lambda q, i: (0, 0, q * count + i)),
            pl.BlockSpec((1, block), lambda q, i: (0, q * count + i)),
        ],
        out_shape=[
            jax.ShapeDtypeStruct((rows, parts * width), F32),
            jax.ShapeDtypeStruct((3, TAPS, parts * width), F32),
            jax.ShapeDtypeStruct((1, parts * width), F32),
        ],
        name="scale_taps",
    )(small, where, *lows, *shared)


def add_sums(pieces, squares, copies):
    shards, parts, lines, chans = pieces.shape

    def kernel(x_ref, sq_ref, o_ref):
        total = jnp.sum(sq_ref[...], axis=0, keepdims=True)
        total = jnp.sum(total, axis=1, keepdims=True)
        sums = []
        for p in range(parts):
            value = x_ref[0, p].astype(F32)
            for s in range(1, shards):
                value = value + x_ref[s, p].astype(F32)
            sums.append(value)
            square = jnp.sum(value * value, axis=0, keepdims=True)
            total = total + jnp.sum(square, axis=1, keepdims=True)
        upper = total.astype(BF16).astype(F32)
        line = lax.broadcasted_iota(jnp.int32, (lines, chans), 0)
        for p in range(parts):
            value = jnp.where(line == lines - 2, upper, sums[p])
            value = jnp.where(line == lines - 1, total - upper, value).astype(BF16)
            for j in range(copies):
                o_ref[j, p] = value

    shape = (copies, parts, lines, chans)
    return pl.pallas_call(
        kernel,
        in_specs=[resident(), resident()],
        out_specs=resident(),
        out_shape=jax.ShapeDtypeStruct(shape, BF16),
        name="add_sums",
    )(pieces, squares)


def short_rows(ext_ref, w_ref, i, cs, r, rows):
    total = w_ref[i, 0:1, cs] * ext_ref[i, pl.ds(HALO + r, rows), :]
    for j in range(1, TAPS):
        total = total + w_ref[i, j : j + 1, cs] * ext_ref[i, pl.ds(HALO + r - j, rows), :]
    return total


def gates(streams, before, grad_out, short_filter, shards, part, parts, keep):
    _, rows, width = streams.shape
    width = width // parts
    chans = width // shards
    block = plan_lanes(width, chans)
    count = width // block
    groups = block // chans
    chunk = math.gcd(rows, 64)

    def kernel(x_ref, b_ref, go_ref, w_ref, o_ref, bias_ref, *refs):
        ext_ref = refs[-1]
        for c in range(0, block, LANES):
            cs = pl.ds(c, LANES)
            fill_ext(ext_ref, x_ref, b_ref, None, cs, rows)
            bias = jnp.zeros((8, LANES), F32)
            for r in range(0, rows, chunk):
                rs = pl.ds(r, chunk)
                x1s = short_rows(ext_ref, w_ref, 0, cs, r, chunk)
                vs = short_rows(ext_ref, w_ref, 2, cs, r, chunk)
                gated = (x1s * vs).astype(BF16)
                mix = go_ref[rs, cs].astype(F32) * short_rows(ext_ref, w_ref, 1, cs, r, chunk)
                mix = mix.astype(BF16)
                put(o_ref, (0,), rs, c, gated)
                put(o_ref, (1,), rs, c, mix)
                if keep:
                    refs[0][0, rs, cs] = x1s
                    refs[0][1, rs, cs] = vs
                term = gated.astype(F32) * mix.astype(F32)
                bias = bias + jnp.sum(term.reshape(chunk // 8, 8, LANES), axis=0)
            bias_ref[:, cs] = jnp.sum(bias, axis=0, keepdims=True)

    out_specs = [
        pl.BlockSpec((groups, 2, rows, chans), lambda i: (i, 0, 0, 0)),
        pl.BlockSpec((1, block), lambda i: (0, i)),
    ]
    out_shape = [
        jax.ShapeDtypeStruct((shards, 2, rows, chans), BF16),
        jax.ShapeDtypeStruct((1, width), F32),
    ]
    if keep:
        out_specs.append(pl.BlockSpec((2, rows, block), lambda i: (0, 0, i)))
        out_shape.append(jax.ShapeDtypeStruct((2, rows, width), F32))
    return pl.pallas_call(
        kernel,
        grid=(count,),
        in_specs=[
            pl.BlockSpec((3, rows, block), lambda i: (0, 0, part * count + i)),
            pl.BlockSpec((3, HALO, block), lambda i: (0, 0, part * count + i)),
            pl.BlockSpec((rows, block), lambda i: (0, part * count + i)),
            pl.BlockSpec((3, TAPS, block), lambda i: (0, 0, part * count + i)),
        ],
        out_specs=out_specs,
        out_shape=out_shape,
        scratch_shapes=[pltpu.VMEM((3, rows + HALO, LANES), F32)],
        cost_estimate=pl.CostEstimate(flops=60 * 10**6, transcendentals=0, bytes_accessed=7 * 10**6),
        name="gates",
    )(streams, before, grad_out, short_filter)


def fill_ext(ext_ref, x_ref, b_ref, n_ref, cs, rows):
    for i in range(3):
        ext_ref[i, pl.ds(0, HALO), :] = b_ref[i, :, cs].astype(F32)
        ext_ref[i, pl.ds(HALO, rows), :] = x_ref[i, :, cs].astype(F32)
        if n_ref is not None:
            ext_ref[i, pl.ds(HALO + rows, HALO), :] = n_ref[i, :, cs].astype(F32)


def short_sums(streams, before, grad_out, short_filter, back, bias, kept, earlier, shards, part, parts):
    _, rows, full = streams.shape
    width = full // parts
    chans = width // shards
    block = plan_lanes(width, chans)
    count = width // block
    groups = block // chans
    chunk = math.gcd(rows, 64)

    def kernel(x_ref, b_ref, go_ref, w_ref, y_ref, bias_ref, *refs):
        st_ref, ext_ref, pre_ref = refs[-3:]
        base = pl.program_id(0) * groups
        for c in range(0, block, LANES):
            cs = pl.ds(c, LANES)
            fill_ext(ext_ref, x_ref, b_ref, None, cs, rows)
            for r in range(0, rows, chunk):
                rs = pl.ds(r, chunk)
                upper = take(y_ref, (1,), rs, c, LANES, base)
                if kept is None:
                    x1s = short_rows(ext_ref, w_ref, 0, cs, r, chunk)
                    vs = short_rows(ext_ref, w_ref, 2, cs, r, chunk)
                else:
                    x1s = refs[0][0, rs, cs]
                    vs = refs[0][1, rs, cs]
                pre_ref[0, rs, :] = upper * vs
                pre_ref[2, rs, :] = upper * x1s
                pre_ref[1, rs, :] = go_ref[rs, cs].astype(F32) * take(y_ref, (0,), rs, c, LANES, base)
            lines = []
            for i in range(3):
                sums = [jnp.zeros((8, LANES), F32) for _ in range(TAPS)]
                for r in range(0, rows, chunk):
                    own = pre_ref[i, pl.ds(r, chunk), :]
                    for j in range(TAPS):
                        term = own * ext_ref[i, pl.ds(HALO + r - j, chunk), :]
                        sums[j] = sums[j] + jnp.sum(term.reshape(chunk // 8, 8, LANES), axis=0)
                lines += [jnp.sum(v, axis=0, keepdims=True) for v in sums]
            lines.append(bias_ref[:, cs])
            lines.append(jnp.zeros((SUMS - len(lines), LANES), F32))
            put(st_ref, (0,), pl.ds(0, SUMS), c, jnp.concatenate(lines, axis=0).astype(BF16))

    at = lambda i: part * count + i
    ins = [streams, before, grad_out, short_filter, back, bias]
    in_specs = [
        pl.BlockSpec((3, rows, block), lambda i: (0, 0, at(i))),
        pl.BlockSpec((3, HALO, block), lambda i: (0, 0, at(i))),
        pl.BlockSpec((rows, block), lambda i: (0, at(i))),
        pl.BlockSpec((3, TAPS, block), lambda i: (0, 0, at(i))),
        resident(),
        pl.BlockSpec((1, block), lambda i: (0, i)),
    ]
    if kept is not None:
        ins.append(kept)
        in_specs.append(pl.BlockSpec((2, rows, block), lambda i: (0, 0, i)))
    return pl.pallas_call(
        kernel,
        grid=(count,),
        in_specs=in_specs + [untouched() for _ in earlier],
        out_specs=pl.BlockSpec((groups, 1, SUMS, chans), lambda i: (i, part, 0, 0)),
        out_shape=jax.ShapeDtypeStruct((shards, parts, SUMS, chans), BF16),
        scratch_shapes=[
            pltpu.VMEM((3, rows + HALO, LANES), F32),
            pltpu.VMEM((3, rows, LANES), F32),
        ],
        input_output_aliases={len(ins): 0} if earlier else {},
        cost_estimate=pl.CostEstimate(flops=150 * 10**6, transcendentals=0, bytes_accessed=8 * 10**6),
        name="short_sums",
    )(*ins, *earlier)


def finish(streams, before, after, grad_out, short_filter, back, earlier, shards, part, parts):
    _, rows, full = streams.shape
    width = full // parts
    chans = width // shards
    block = plan_lanes(width, chans)
    count = width // block
    groups = block // chans
    chunk = math.gcd(rows, 64)

    def kernel(x_ref, b_ref, n_ref, go_ref, w_ref, y_ref, *refs):
        o_ref, gs_ref, ext_ref, pre_ref = refs[-4:]
        base = pl.program_id(0) * groups
        for c in range(0, block, LANES):
            cs = pl.ds(c, LANES)
            fill_ext(ext_ref, x_ref, b_ref, n_ref, cs, rows)
            for r in range(0, rows, chunk):
                rs = pl.ds(r, chunk)
                mixed = take(y_ref, (0,), rs, c, LANES, base)
                upper = take(y_ref, (1,), rs, c, LANES, base)
                pre_ref[0, rs, :] = upper * short_rows(ext_ref, w_ref, 2, cs, r, chunk)
                pre_ref[2, rs, :] = upper * short_rows(ext_ref, w_ref, 0, cs, r, chunk)
                pre_ref[1, rs, :] = go_ref[rs, cs].astype(F32) * mixed
                o_ref[rs, cs] = (short_rows(ext_ref, w_ref, 1, cs, r, chunk) * mixed).astype(BF16)
            mixed = take(y_ref, (0,), pl.ds(rows, EDGE), c, LANES, base)[:HALO]
            upper = take(y_ref, (1,), pl.ds(rows, EDGE), c, LANES, base)[:HALO]
            pre_ref[0, pl.ds(rows, HALO), :] = upper * short_rows(ext_ref, w_ref, 2, cs, rows, HALO)
            pre_ref[2, pl.ds(rows, HALO), :] = upper * short_rows(ext_ref, w_ref, 0, cs, rows, HALO)
            pre_ref[1, pl.ds(rows, HALO), :] = n_ref[3, :, cs].astype(F32) * mixed
            for i in range(3):
                for r in range(0, rows, chunk):
                    total = w_ref[i, 0:1, cs] * pre_ref[i, pl.ds(r, chunk), :]
                    for j in range(1, TAPS):
                        total = total + w_ref[i, j : j + 1, cs] * pre_ref[i, pl.ds(r + j, chunk), :]
                    gs_ref[i, pl.ds(r, chunk), cs] = total.astype(BF16)

    at = lambda i: part * count + i
    ins = [streams, before, after, grad_out, short_filter, back]
    return pl.pallas_call(
        kernel,
        grid=(count,),
        in_specs=[
            pl.BlockSpec((3, rows, block), lambda i: (0, 0, at(i))),
            pl.BlockSpec((3, HALO, block), lambda i: (0, 0, at(i))),
            pl.BlockSpec((4, HALO, block), lambda i: (0, 0, at(i))),
            pl.BlockSpec((rows, block), lambda i: (0, at(i))),
            pl.BlockSpec((3, TAPS, block), lambda i: (0, 0, at(i))),
            resident(),
        ]
        + [untouched() for _ in earlier],
        out_specs=[
            pl.BlockSpec((rows, block), lambda i: (0, at(i))),
            pl.BlockSpec((3, rows, block), lambda i: (0, 0, at(i))),
        ],
        out_shape=[
            jax.ShapeDtypeStruct((rows, full), BF16),
            jax.ShapeDtypeStruct((3, rows, full), BF16),
        ],
        scratch_shapes=[
            pltpu.VMEM((3, rows + 2 * HALO, LANES), F32),
            pltpu.VMEM((3, rows + HALO, LANES), F32),
        ],
        input_output_aliases={len(ins) + i: i for i in range(len(earlier))},
        cost_estimate=pl.CostEstimate(flops=150 * 10**6, transcendentals=0, bytes_accessed=12 * 10**6),
        name="finish",
    )(*ins, *earlier)


def shift(block, axis, distance):
    devices = range(lax.axis_size(axis))
    route = [(i - distance, i) for i in devices if i - distance in devices]
    return lax.ppermute(block, axis, route)


def exchange(blocks, groups=None):
    return lax.all_to_all(blocks, "seq", split_axis=0, concat_axis=0, axis_index_groups=groups, tiled=True)


def on_chip(value):
    lanes = -(-value.shape[-1] // LANES) * LANES
    if math.prod(value.shape[:-1]) * lanes * value.dtype.itemsize > ON_CHIP_BYTES:
        return value
    return pltpu.with_memory_space_constraint(value, pltpu.VMEM)


def following(value, earlier):
    return lax.optimization_barrier((value, earlier))[0]


def operator(streams, grad_out, long_filter, short_filter, skip_gain):
    shards = lax.axis_size("seq")
    rows = streams.shape[1]
    width = streams.shape[2]
    parts = 2 if width % (2 * shards * LANES) == 0 else 1
    span = width // parts
    chans = span // shards
    tap_rows = long_filter.shape[0]
    live = min(shards, shards * rows // tap_rows)
    fold = 2 * live <= shards
    mine = lax.axis_index("seq")
    is_low = mine < live
    where = jnp.stack([is_low.astype(jnp.int32), mine % live, lax.axis_index("chan")]).reshape(1, 3)
    fwd, inv = turn_tables(shards, rows)
    before = shift(streams[:, rows - HALO :], "seq", 1)
    after = shift(jnp.concatenate([streams[:, :HALO], grad_out[None, :HALO]], axis=0), "seq", -1)
    skips = [lax.dynamic_slice_in_dim(skip_gain, p * span + mine * chans, chans)[None] for p in range(parts)]

    both = []
    bias = []
    filtered = []
    packed = []
    for p in range(parts):
        keep = p == parts - 1 and parts > 1
        sent, terms, *rest = gates(streams, before, grad_out, short_filter, shards, p, parts, keep)
        bias.append(terms)
        filtered.append(rest[0] if rest else None)
        both.append(on_chip(exchange(sent)))
    for p in range(parts):
        packed.append(pack_taps(long_filter, shards, p, parts))
    spec = []
    shared = []
    squares = []
    low = None
    for p in range(parts):
        out = raw_path(both[p], fwd, inv, where, packed[p], low, p, parts, tap_rows, live, fold)
        spec.append(out[0])
        low = out[1]
        squares.append(out[2])
        shared.append(exchange(out[3] if fold else packed[p]))
    back = []
    sent_all = []
    for p in range(parts):
        taps = shared[p].reshape(shards * tap_rows // rows, rows, chans)
        sent = conv_path(both[p], taps, spec[p], skips[p], fwd, inv)
        back.append(on_chip(exchange(sent)))
        sent_all.append(sent)
    done = []
    sums = []
    lows = []

    def send_low(steps, cue):
        ready = following(low, cue)
        for d in steps:
            lows[d] = lax.ppermute(ready[d], "seq", [(i, i ^ d) for i in range(live)])

    if fold:
        half = live // 2
        lows = [low[0]] + [None] * (live - 1)
        send_low(range(1, half), sent_all[-1])
    for p in range(parts):
        terms = (back[p], bias[p], filtered[p], sums)
        sums = [short_sums(streams, before, grad_out, short_filter, *terms, shards, p, parts)]
        if p == 0 and fold:
            send_low(range(half, live), back[0])
        done = finish(streams, before, after, grad_out, short_filter, back[p], done, shards, p, parts)
    output, grad_streams = done
    sums = sums[0]
    if not fold:
        lows.append(exchange(following(low, back[-1])))
        sums = following(sums, lows[0])
    pieces = on_chip(exchange(sums))
    copies = add_sums(pieces, jnp.concatenate(squares, axis=0), shards * lax.axis_size("chan"))
    small = lax.all_to_all(copies, ("seq", "chan"), split_axis=0, concat_axis=0, tiled=True)
    param_count = LF * D + (3 * TAPS + 1) * D
    filter_grad, short_grad, bias_grad = scale_taps(
        small, where, lows, shared if fold else [], shards, live, param_count
    )
    return output, grad_streams, filter_grad, short_grad, bias_grad[0]


def solution(mesh):
    placed = (
        P(None, "seq", "chan"),
        P("seq", "chan"),
        P("seq", "chan"),
        P(None, None, "chan"),
        P("chan"),
    )
    return jax.shard_map(
        operator,
        mesh=mesh,
        in_specs=placed,
        out_specs=(
            P("seq", "chan"),
            P(None, "seq", "chan"),
            P("seq", "chan"),
            P(None, None, "chan"),
            P("chan"),
        ),
        check_vma=False,
    )
```
